32 devices in a mesh: stn: 4 (over y, x), chan: 4 (over z), beam: 2 (over core).
Axes of the slice: x: 2, y: 2, z: 4, core: 2. Of those that a mesh axis runs over, the one named last changes fastest.
Arguments:
- volts: bfloat16 [2, 128, 12, 9216], P(None, 'stn', 'chan', 'beam'), may hold values from -6 to 6
- taps: float32 [16, 256], replicated, may hold values from -1.5 to 1.5
- delays: int32 [32, 128], P(None, 'stn'), may hold values from 0 to 1023
- station_sub: int32 [128], P('stn'), may hold values from 0 to 3
- beam_sub: int32 [32], replicated, may hold values from 0 to 3
Outputs:
- beams: float32 [32, 2, 12, 48, 256], P(('stn', 'chan', 'beam'))
The draws below stay inside these ranges and needn't reach their ends.
All inputs are finite; a program needn't handle non-finite values.
Results may differ from the reference program's by a relative error of at most 0.014.
Values may be sent and summed in bfloat16 or wider, within the bound.
A program may use at most 192 MiB of HBM per device.

```python
import math
import jax
import jax.numpy as jnp
from jax import lax

FINE = 256
TAPS = 16
STN_DEV = 32
SUBARRAYS = 4
STATIONS = 128
CHANNELS = 12
FRAMES = 48
SAMPLES = 9216
BEAMS = 32
N_STN = 4


def set_ends(drawn, key, low, top_value):
    dims = drawn.shape
    spot = [jax.random.randint(jax.random.fold_in(key, axis), (), 0, dims[axis]) for axis in range(len(dims))]
    drawn = drawn.at[tuple(spot)].set(low)
    longest = dims.index(max(dims))
    spot[longest] = (spot[longest] + 1) % dims[longest]
    return drawn.at[tuple(spot)].set(top_value)


def steps_of(own_key, extent, shards, low, high):
    loudness, own = 1.0, jax.random.fold_in(own_key, 6)
    for position, blocks in shards:
        steps = jnp.exp(jax.random.uniform(jax.random.fold_in(own, position), (blocks,), jnp.float32, low / len(shards), high / len(shards)))
        loudness = loudness * jnp.repeat(steps, extent[position] // blocks).reshape([-1 if axis == position else 1 for axis in range(len(extent))])
    return loudness


def noise(rng, shape, scale, limit, cuts=(), kind=jnp.bfloat16):
    factor_of = steps_of(rng, shape, cuts, -0.22, 0.18) if cuts else 1.0
    values = jax.random.normal(rng, shape, jnp.float32) * scale * factor_of
    return jnp.minimum(jnp.maximum(values, -limit), limit).astype(kind)


def setup_inputs(seed: int = 0) -> dict:
    arg_keys = jax.random.split(jax.random.key(seed), 6)
    return {
        "volts": noise(arg_keys[0], (2, STATIONS, CHANNELS, SAMPLES), 1.0, 6.0, ((1, 4), (2, 4), (3, 2))),
        "taps": noise(arg_keys[1], (TAPS, FINE), 0.25, 1.5, (), jnp.float32),
        "delays": set_ends(jax.random.randint(arg_keys[2], (BEAMS, STATIONS), 0, 1024), jax.random.fold_in(arg_keys[2], 1), 0, 1023).astype(jnp.int32),
        "station_sub": set_ends(jax.random.randint(arg_keys[3], (STATIONS,), 0, SUBARRAYS), jax.random.fold_in(arg_keys[3], 1), 0, SUBARRAYS - 1).astype(jnp.int32),
        "beam_sub": set_ends(jax.random.randint(arg_keys[4], (BEAMS,), 0, SUBARRAYS), jax.random.fold_in(arg_keys[4], 1), 0, SUBARRAYS - 1).astype(jnp.int32),
    }


def filter_frames(extended, taps, frame_count):
    tap_count, fine = taps.shape
    hop = 3 * fine // 4
    groups = frame_count // 4
    rows = groups + (tap_count + 2) // 3
    shape = extended.shape
    needed = 3 * hop + 3 * rows * fine
    padding = max(0, needed - shape[-1])
    padded = jnp.concatenate([extended, jnp.zeros(shape[:-1] + (padding,), extended.dtype)], axis=-1)
    streams = []
    for phase in range(4):
        start = phase * hop
        piece = lax.slice_in_dim(padded, start, start + 3 * rows * fine, 1, len(shape) - 1)
        streams.append(piece.reshape(shape[:-1] + (rows, 3, fine)))
    stacked = jnp.stack(streams, axis=-2)
    axis = len(shape) - 1
    total = None
    for tap in range(tap_count):
        lead = tap // 3
        inner = tap % 3
        window = lax.slice_in_dim(stacked, lead, lead + groups, 1, axis)[..., inner, :, :].astype(jnp.float32)
        term = taps[tap] * window
        total = term if total is None else total + term
    return total.reshape(shape[:-1] + (frame_count, fine)).astype(jnp.bfloat16)

def dft_tables(fine):
    index = jnp.arange(fine, dtype=jnp.int32)
    product = index[:, None] * index[None, :] % fine
    angle = 2.0 * jnp.pi * product.astype(jnp.float32) / fine
    scale = 1.0 / math.sqrt(fine)
    return ((jnp.cos(angle) * scale).astype(jnp.bfloat16), (jnp.sin(angle) * scale).astype(jnp.bfloat16))

def channelize(filtered, frame_start, hop):
    fine = filtered.shape[-1]
    cosine, sine = dft_tables(fine)
    spec_re = jnp.einsum('...j,jk->...k', filtered[0], cosine, preferred_element_type=jnp.float32) + jnp.einsum('...j,jk->...k', filtered[1], sine, preferred_element_type=jnp.float32)
    spec_im = jnp.einsum('...j,jk->...k', filtered[1], cosine, preferred_element_type=jnp.float32) - jnp.einsum('...j,jk->...k', filtered[0], sine, preferred_element_type=jnp.float32)
    frame_count = filtered.shape[-2]
    frame_index = frame_start + jnp.arange(frame_count, dtype=jnp.int32)
    fine_index = jnp.arange(fine, dtype=jnp.int32)
    turn = fine_index[None, :] * hop % fine * frame_index[:, None] % fine
    rot = 2.0 * jnp.pi * turn.astype(jnp.float32) / fine
    cos_rot = jnp.cos(rot)
    sin_rot = jnp.sin(rot)
    out_re = spec_re * cos_rot + spec_im * sin_rot
    out_im = spec_im * cos_rot - spec_re * sin_rot
    return jnp.stack([out_re, out_im]).astype(jnp.bfloat16)

def steering(delay_rows, beam_subs, station_subs, chan_start, chan_count, fine, amplitude):
    fine_index = jnp.arange(fine, dtype=jnp.int32)
    chan_index = chan_start + jnp.arange(chan_count, dtype=jnp.int32)
    freq_index = chan_index[:, None] * fine + fine_index[None, :]
    turn = delay_rows[:, :, None, None] * freq_index[None, None, :, :] % 65536
    phase = 2.0 * jnp.pi * turn.astype(jnp.float32) / 65536.0
    member = (beam_subs[:, None] == station_subs[None, :]).astype(jnp.float32)[:, :, None, None]
    weight_re = (amplitude * member * jnp.cos(phase)).astype(jnp.bfloat16)
    weight_im = (-amplitude * member * jnp.sin(phase)).astype(jnp.bfloat16)
    return (weight_re, weight_im)

def reference(volts, taps, delays, station_sub, beam_sub):
    hop = 3 * FINE // 4
    extra = TAPS * FINE - hop
    amplitude = 1.0 / math.sqrt(STATIONS // SUBARRAYS)

    def one_channel(chan):
        raw = lax.dynamic_slice_in_dim(volts, chan, 1, 2)
        extended = jnp.concatenate([raw, jnp.zeros((2, STATIONS, 1, extra), jnp.bfloat16)], axis=3)
        filtered = filter_frames(extended, taps, FRAMES)
        spectra = channelize(filtered, 0, hop)
        weight_re, weight_im = steering(delays, beam_sub, station_sub, chan, 1, FINE, amplitude)
        grouped = spectra.reshape(2, N_STN, STN_DEV, 1, FRAMES, FINE).astype(jnp.float32)
        w_re = weight_re.reshape(BEAMS, N_STN, STN_DEV, 1, FINE).astype(jnp.float32)
        w_im = weight_im.reshape(BEAMS, N_STN, STN_DEV, 1, FINE).astype(jnp.float32)
        form = 'bgsck,gscfk->gbcfk'
        part_re = jnp.einsum(form, w_re, grouped[0]) - jnp.einsum(form, w_im, grouped[1])
        part_im = jnp.einsum(form, w_re, grouped[1]) + jnp.einsum(form, w_im, grouped[0])
        part_re = part_re.astype(jnp.bfloat16).astype(jnp.float32)
        part_im = part_im.astype(jnp.bfloat16).astype(jnp.float32)
        total_re = lax.optimization_barrier(jnp.sum(part_re, axis=0))[:, 0]
        total_im = lax.optimization_barrier(jnp.sum(part_im, axis=0))[:, 0]
        return jnp.stack([total_re, total_im], axis=1)
    per_channel = lax.map(one_channel, jnp.arange(CHANNELS, dtype=jnp.int32))
    return jnp.transpose(per_channel, (1, 2, 0, 3, 4))
```

```python
import functools
import math

import jax
import jax.numpy as jnp
import numpy as np
from jax import lax
from jax.experimental import pallas as pl
from jax.experimental.pallas import tpu as pltpu
from jax.sharding import PartitionSpec as P

SUBARRAYS = 4
LANES = 128
QUAD = 4
PHASES = 4
VMEM_LIMIT = 56 * 2**20
MESH = pl.DeviceIdType.MESH


def dft_table(fine, lane_groups):
    index = np.arange(fine)
    angle = 2.0 * np.pi * (index[:, None] * index[None, :] % fine) / fine
    scale = 1.0 / math.sqrt(fine)
    cosine = np.cos(angle) * scale
    sine = np.sin(angle) * scale
    whole = np.stack([np.concatenate([cosine, sine]), np.concatenate([-sine, cosine])])
    halves = []
    for half in range(fine // LANES):
        k = half * LANES + (np.arange(LANES).reshape(-1, lane_groups).T).reshape(-1)
        halves.append(np.concatenate([whole[0][:, k].T, whole[1][:, k].T]))
    return jnp.asarray(np.stack(halves), jnp.bfloat16)


def unit_turn(turn):
    quarter = (turn + 8192) >> 14
    t = (turn - (quarter << 14)).astype(jnp.float32) * (2.0 * math.pi / 65536.0)
    u = t * t
    sine = t * (1.0 + u * (-1.0 / 6 + u * (1.0 / 120 + u * (-1.0 / 5040))))
    cosine = 1.0 + u * (-0.5 + u * (1.0 / 24 + u * (-1.0 / 720 + u * (1.0 / 40320))))
    odd = (quarter & 1) == 1
    c = jnp.where(odd, sine, cosine)
    s = jnp.where(odd, cosine, sine)
    c = jnp.where(((quarter + 1) & 2) == 2, -c, c)
    s = jnp.where((quarter & 2) == 2, -s, s)
    return c, s


def swap_index_with_lanes(tiles, block):
    lane = lax.broadcasted_iota(jnp.int32, tiles[0].shape, 1)
    bit = 1
    while bit < len(tiles):
        upper = (lane & (bit * block)) != 0
        swapped = list(tiles)
        for i in range(len(tiles)):
            if not i & bit:
                low, high = tiles[i], tiles[i | bit]
                swapped[i] = jnp.where(upper, pltpu.roll(high, bit * block, 1), low)
                swapped[i | bit] = jnp.where(upper, high, pltpu.roll(low, LANES - bit * block, 1))
        tiles = swapped
        bit *= 2
    return tiles


def kernel(
    sizes,
    amplitude,
    own_ref,
    taps_hbm,
    table_hbm,
    delays_hbm,
    station_hbm,
    beam_hbm,
    out_ref,
    volts,
    taps_ref,
    table,
    delay_in,
    station_in,
    beam_in,
    wide_taps,
    wide_int,
    member,
    steps,
    state,
    filtered,
    spectra,
    total_ref,
    turned,
    part,
    final,
    own_sem,
    small_sem,
    halo_send,
    halo_recv,
    send,
    recv,
    far_send,
    far_recv,
    keep_sem,
    *exchanged,
):
    n_chan, n_core, bits = sizes
    received, sent = exchanged[:bits], exchanged[bits:]
    chans, stations, samples = own_ref.shape[1:]
    tap_count, fine = taps_ref.shape
    beams = delay_in.shape[0]
    frames = final.shape[-2]
    halves = fine // LANES
    chunks = chans * halves
    lane_groups = LANES // stations
    hop = 3 * fine // 4
    groups = frames // PHASES
    quads = LANES // lane_groups // QUAD
    n_stn = 2**bits
    rows = 2 * beams // n_stn
    per = beams // n_stn
    width = frames * lane_groups
    tiles = QUAD * width // LANES
    halo = volts.shape[3] - samples
    stn, chan, core = (lax.axis_index(name) for name in ("stn", "chan", "beam"))

    def fetch(c):
        return pltpu.make_async_copy(
            own_ref.at[:, c], volts.at[:, c, :, pl.ds(0, samples)], own_sem.at[c]
        )

    small = [
        pltpu.make_async_copy(source, target, small_sem.at[i])
        for i, (source, target) in enumerate(
            (
                (taps_hbm, taps_ref),
                (delays_hbm, delay_in),
                (station_hbm, station_in),
                (beam_hbm, beam_in),
                (table_hbm, table),
            )
        )
    ]
    for copy in small:
        copy.start()
    for c in range(chans):
        fetch(c).start()

    own_bit = [(stn // 2 ** (bits - 1 - dim)) % 2 for dim in range(bits)]
    orders = (tuple(range(bits - 1, -1, -1)), tuple(range(bits)))

    def partner(dim):
        return (stn + (1 - 2 * own_bit[dim]) * 2 ** (bits - 1 - dim), chan, core)

    def far(dz, dc):
        return ((chan + dz) % n_chan, (core + dc) % n_core)

    offsets = [(dz, dc) for dz in range(n_chan) for dc in range(n_core)]
    barrier = pltpu.get_barrier_semaphore()
    peers = [partner(dim) for dim in range(bits)] + [(stn, *far(dz, dc)) for dz, dc in offsets[1:]]
    for peer in peers:
        pl.semaphore_signal(barrier, inc=1, device_id=peer, device_id_type=MESH)
    pl.semaphore_wait(barrier, len(peers))

    def halo_copy(c):
        return pltpu.make_async_remote_copy(
            src_ref=own_ref.at[:, c, :, pl.ds(0, halo)],
            dst_ref=volts.at[:, c, :, pl.ds(samples, halo)],
            send_sem=halo_send.at[c],
            recv_sem=halo_recv.at[c],
            device_id=(stn, chan, core - 1),
            device_id_type=MESH,
        )

    @pl.when(core > 0)
    def _():
        for c in range(chans):
            halo_copy(c).start()

    @pl.when(core == n_core - 1)
    def _():
        volts[:, :, :, samples:] = jnp.zeros((2, chans, stations, halo), volts.dtype)

    for copy in small:
        copy.wait()

    for phase in range(PHASES):
        shift = hop * phase % fine
        rolled = taps_ref[...]
        if shift:
            rolled = pltpu.roll(rolled, shift, 1)
        column = lax.broadcasted_iota(jnp.int32, (1, fine), 1)
        for u in range(tap_count + 1):
            late = rolled[u : u + 1] if u < tap_count else jnp.zeros((1, fine), jnp.float32)
            early = rolled[u - 1 : u] if u > 0 else jnp.zeros((1, fine), jnp.float32)
            row = jnp.where(column >= shift, late, early)
            wide_taps[phase, u] = jnp.broadcast_to(row, (16, fine)).astype(jnp.bfloat16)

    def widened(value, count):
        wide_int[...] = jnp.zeros(wide_int.shape, jnp.int32)
        wide_int[0:count, 0:stations] = value
        full = wide_int[...]
        step = stations
        while step < LANES:
            full = full + pltpu.roll(full, step, 1)
            step *= 2
        return full[0:count]

    group_of_lane = lax.broadcasted_iota(jnp.int32, (1, LANES), 1) // stations
    station_row = widened(station_in[...], 1).astype(jnp.float32)
    square = (beams, beams)
    diagonal = lax.broadcasted_iota(jnp.int32, square, 0) == lax.broadcasted_iota(jnp.int32, square, 1)
    beam_row = jnp.broadcast_to(beam_in[...].astype(jnp.float32), square)
    beam_column = jnp.sum(jnp.where(diagonal, beam_row, 0.0), axis=1, keepdims=True)
    member[...] = jnp.where(beam_column == station_row, amplitude, 0.0)
    delay = widened(delay_in[...], beams)
    wide_int[...] = delay
    for i, stride in enumerate((lane_groups, QUAD * lane_groups)):
        c, s = unit_turn((delay * stride) & 65535)
        steps[i, 0] = c
        steps[i, 1] = -s

    def filter_channel(c):
        @pl.loop(0, 2)
        def _(ri):
            for half in range(halves):
                for phase in range(PHASES):
                    shift = hop * phase % fine
                    block0 = hop * phase // fine
                    first = 0 if shift < (half + 1) * LANES else 1
                    last = tap_count - 1 if shift <= half * LANES else tap_count
                    lanes = slice(half * LANES, (half + 1) * LANES)
                    taps = {
                        u: wide_taps[phase, u, :, lanes][None] for u in range(first, last + 1)
                    }
                    sums = [[None, None] for _ in range(groups)]
                    for block in range(block0 + first, block0 + last + 1 + 3 * (groups - 1)):
                        at = block * fine + half * LANES
                        value = volts[ri, c, :, at : at + LANES].reshape(stations // 16, 16, LANES)
                        for g in range(groups):
                            u = block - block0 - 3 * g
                            if first <= u <= last:
                                term = taps[u] * value
                                so_far = sums[g][u % 2]
                                sums[g][u % 2] = term if so_far is None else so_far + term
                    for g in range(groups):
                        f = PHASES * g + phase
                        filtered[
                            f * stations : (f + 1) * stations,
                            pl.ds(pl.multiple_of(ri * fine + half * LANES, LANES), LANES),
                        ] = (sums[g][0] + sums[g][1]).reshape(stations, LANES)

    def transform(half):
        @pl.loop(0, frames // lane_groups)
        def _(fb):
            rhs = filtered[pl.ds(pl.multiple_of(fb * LANES, LANES), LANES), :]
            result = lax.dot_general(
                table[half], rhs, (((1,), (1,)), ((), ())), preferred_element_type=jnp.float32
            )
            count = LANES // lane_groups
            for ri in range(2):
                pieces = [
                    result[(ri * lane_groups + j) * count : (ri * lane_groups + j + 1) * count]
                    for j in range(lane_groups)
                ]
                for j, piece in enumerate(swap_index_with_lanes(pieces, stations)):
                    at = pl.multiple_of((fb * lane_groups + j) * count, count)
                    spectra[ri, pl.ds(at, count), :] = piece

    def form_beams(chunk, c, half):
        count = LANES // lane_groups
        frequency = (chan * chans + c) * fine + half * LANES + group_of_lane
        cosine, sine = unit_turn((wide_int[...] * frequency) & 65535)
        state[0] = cosine * member[...]
        state[1] = -sine * member[...]
        lane = lax.broadcasted_iota(jnp.int32, (frames, LANES), 1) // stations
        out_lane = lax.broadcasted_iota(jnp.int32, (2 * beams, LANES), 1)

        def times(a, i):
            e_re, e_im = steps[i, 0], steps[i, 1]
            return (a[0] * e_re - a[1] * e_im, a[0] * e_im + a[1] * e_re)

        def stacked(top, bottom):
            both = [v.reshape(n_stn, per, LANES) for v in (top, bottom)]
            return jnp.stack(both, axis=1).reshape(2 * beams, LANES)

        @pl.loop(0, quads)
        def _(quad):
            first = weight = (state[0], state[1])
            outs = []
            for q in range(QUAD):
                if q:
                    weight = times(weight, 0)
                w_re, w_im = weight
                lhs = jnp.concatenate([stacked(w_re, w_im), stacked(-w_im, w_re)], axis=1)
                at = quad * QUAD + q
                x = [spectra.at[ri][pl.ds(at, frames, stride=count), :] for ri in range(2)]
                blocks = [
                    jnp.concatenate([jnp.where(lane == j, v, 0.0) for v in x], axis=1)
                    for j in range(lane_groups)
                ]
                if width < LANES:
                    blocks.append(jnp.zeros((LANES - width, 2 * LANES), jnp.float32))
                rhs = jnp.concatenate(blocks, axis=0)
                result = lax.dot_general(
                    lhs.astype(jnp.bfloat16),
                    rhs.astype(jnp.bfloat16),
                    (((1,), (1,)), ((), ())),
                    preferred_element_type=jnp.float32,
                )
                turn = q * width % LANES
                outs.append(pltpu.roll(result, turn, 1) if turn else result)
            following = times(first, 1)
            state[0] = following[0]
            state[1] = following[1]
            for t in range(tiles):
                value = None
                for q in range(QUAD):
                    start = q * width - t * LANES
                    if -width < start < LANES:
                        value = outs[q] if value is None else jnp.where(out_lane >= start, outs[q], value)
                value = value.astype(jnp.bfloat16)
                for d in range(n_stn):
                    place = [(d >> (bits - 1 - dim)) & 1 for dim in range(bits)]
                    part[(chunk, quad // (quads // 2), *place, quad % (quads // 2), t)] = value[
                        d * rows : (d + 1) * rows
                    ]

    def region(order, stage, last):
        index = [slice(None)] * bits
        for dim in orders[order][:stage]:
            index[dim] = own_bit[dim]
        if stage < bits:
            index[orders[order][stage]] = last(orders[order][stage])
        return index

    def other(dim):
        return 1 - own_bit[dim]

    def with_received(chunk, order, stage, index):
        value = part[(chunk, order, *index)].astype(jnp.float32)
        for earlier in range(stage):
            kept = [dim for dim in range(bits) if dim not in orders[order][: earlier + 1]]
            piece = received[earlier][(chunk, order, *(index[dim] for dim in kept))]
            value = value + piece.astype(jnp.float32)
        return value

    def hop_copy(chunk, order, stage):
        if stage == 0:
            source = part.at[(chunk, order, *region(order, 0, other))]
        else:
            source = sent[stage - 1].at[chunk, order]
        return pltpu.make_async_remote_copy(
            src_ref=source,
            dst_ref=received[stage].at[chunk, order],
            send_sem=send.at[stage, chunk, order],
            recv_sem=recv.at[stage, chunk, order],
            device_id=partner(orders[order][stage]),
            device_id_type=MESH,
        )

    def place_of(chunk):
        c = chunk // halves
        lanes = pl.ds(pl.multiple_of((chunk % halves) * LANES, LANES), LANES)
        return out_ref.at[:, :, chan * chans + c, core, :, lanes]

    def deliver(chunk, number):
        z, k = far(*offsets[number])
        return pltpu.make_async_remote_copy(
            src_ref=final.at[chunk, z, k],
            dst_ref=place_of(chunk),
            send_sem=far_send.at[chunk, number],
            recv_sem=far_recv.at[chunk, number],
            device_id=(stn, z, k),
            device_id_type=MESH,
        )

    def keep(chunk):
        return pltpu.make_async_copy(final.at[chunk, chan, core], place_of(chunk), keep_sem.at[chunk])

    def finish(chunk):
        for order in range(2):
            value = with_received(chunk, order, bits, own_bit)
            for quad in range(quads // 2):
                at = (order * (quads // 2) + quad) * rows
                for t in range(tiles):
                    total_ref[t, at : at + rows, :] = value[quad, t]
        for t in range(tiles):
            turned[t * LANES : (t + 1) * LANES, :] = total_ref[t].T
        pieces = [turned[i * frames : (i + 1) * frames, :] for i in range(rows)]
        for row, piece in enumerate(swap_index_with_lanes(pieces, 1)):
            ri, b = divmod(row, per)
            device, at = divmod(b, per // (n_chan * n_core))
            z, k = divmod(device, n_core)
            final[chunk, z, k, at, ri] = piece.astype(jnp.bfloat16)

    def step(chunk, stage):
        for order in range(2):
            hop_copy(chunk, order, stage - 1).wait_recv()
            if stage < bits:
                sent[stage - 1][chunk, order] = with_received(
                    chunk, order, stage, region(order, stage, other)
                ).astype(jnp.bfloat16)
                hop_copy(chunk, order, stage).start()
        if stage == bits:
            finish(chunk)
            for number in range(len(offsets) - 1, 0, -1):
                deliver(chunk, number).start()
            keep(chunk).start()

    @pl.loop(0, chunks + bits)
    def _(tick):
        @pl.when(tick < chunks)
        def _():
            c = tick // halves
            half = tick % halves

            @pl.when(half == 0)
            def _():
                fetch(c).wait()

                @pl.when(core < n_core - 1)
                def _():
                    halo_copy(c).wait_recv()

                filter_channel(c)

            transform(half)
            form_beams(tick, c, half)
            for order in range(2):
                hop_copy(tick, order, 0).start()

        for stage in range(1, bits + 1):
            chunk = tick - stage

            @pl.when((chunk >= 0) & (chunk < chunks))
            def _(chunk=chunk, stage=stage):
                step(chunk, stage)

    @pl.when(core > 0)
    def _():
        for c in range(chans):
            halo_copy(c).wait_send()

    @pl.loop(0, chunks)
    def _(chunk):
        for order in range(2):
            for stage in range(bits):
                hop_copy(chunk, order, stage).wait_send()
        for number in range(1, len(offsets)):
            deliver(chunk, number).wait()
        keep(chunk).wait()


def body(volts, taps, delays, station_sub, beam_sub):
    own = jnp.transpose(volts, (0, 2, 1, 3))
    chans, stations, samples = own.shape[1:]
    tap_count, fine = taps.shape
    beams = delays.shape[0]
    n_stn, n_chan, n_core = (lax.axis_size(name) for name in ("stn", "chan", "beam"))
    bits = n_stn.bit_length() - 1
    hop = 3 * fine // 4
    frames = samples // hop
    per = beams // n_stn
    per_device = per // (n_chan * n_core)
    halves = fine // LANES
    chunks = chans * halves
    lane_groups = LANES // stations
    quads = LANES // lane_groups // QUAD
    tiles = QUAD * frames * lane_groups // LANES
    rows = 2 * per
    peers = n_chan * n_core
    assert n_stn == 2**bits and rows == QUAD * lane_groups and quads * rows == LANES
    assert QUAD * frames * lane_groups == tiles * LANES and frames * lane_groups <= LANES
    blocks = hop * (PHASES - 1) // fine + tap_count + 1 + 3 * (frames // PHASES - 1)
    amplitude = 1.0 / math.sqrt(stations * n_stn // SUBARRAYS)
    block = (quads // 2, tiles, rows, LANES)
    pieces = [
        pltpu.VMEM((chunks, 2) + (2,) * (bits - 1 - t) + block, jnp.bfloat16) for t in range(bits)
    ]
    hbm = pl.BlockSpec(memory_space=pltpu.HBM)
    dma = pltpu.SemaphoreType.DMA
    out = pl.pallas_call(
        functools.partial(kernel, (n_chan, n_core, bits), amplitude),
        out_shape=jax.ShapeDtypeStruct(
            (per_device, 2, n_chan * chans, n_core, frames, fine), jnp.bfloat16
        ),
        in_specs=[hbm] * 6,
        out_specs=pl.BlockSpec(memory_space=pl.ANY),
        scratch_shapes=[
            pltpu.VMEM((2, chans, stations, blocks * fine), jnp.bfloat16),
            pltpu.VMEM((tap_count, fine), jnp.float32),
            pltpu.VMEM((halves, 2 * LANES, 2 * fine), jnp.bfloat16),
            pltpu.VMEM((beams, stations), jnp.int32),
            pltpu.VMEM((1, stations), jnp.int32),
            pltpu.VMEM((1, beams), jnp.int32),
            pltpu.VMEM((PHASES, tap_count + 1, 16, fine), jnp.bfloat16),
            pltpu.VMEM((beams, LANES), jnp.int32),
            pltpu.VMEM((beams, LANES), jnp.float32),
            pltpu.VMEM((2, 2, beams, LANES), jnp.float32),
            pltpu.VMEM((2, beams, LANES), jnp.float32),
            pltpu.VMEM((frames * stations, 2 * fine), jnp.bfloat16),
            pltpu.VMEM((2, frames * LANES // lane_groups, LANES), jnp.float32),
            pltpu.VMEM((tiles, LANES, LANES), jnp.float32),
            pltpu.VMEM((tiles * LANES, LANES), jnp.float32),
            pltpu.VMEM((chunks, 2) + (2,) * bits + block, jnp.bfloat16),
            pltpu.VMEM((chunks, n_chan, n_core, per_device, 2, frames, LANES), jnp.bfloat16),
            dma((chans,)),
            dma((5,)),
            dma((chans,)),
            dma((chans,)),
            dma((bits, chunks, 2)),
            dma((bits, chunks, 2)),
            dma((chunks, peers)),
            dma((chunks, peers)),
            dma((chunks,)),
            *pieces,
            *pieces[1:],
        ],
        compiler_params=pltpu.CompilerParams(
            collective_id=0, has_side_effects=True, vmem_limit_bytes=VMEM_LIMIT
        ),
        name="channelize_and_beamform",
    )(
        own,
        taps,
        dft_table(fine, lane_groups),
        delays,
        station_sub[None],
        beam_sub[None],
    )
    return out.reshape(per_device, 2, n_chan * chans, n_core * frames, fine).astype(jnp.float32)


def solution(mesh):
    placed = (P(None, "stn", "chan", "beam"), P(), P(None, "stn"), P("stn"), P())
    return jax.shard_map(
        body,
        mesh=mesh,
        in_specs=placed,
        out_specs=P(("stn", "chan", "beam"), None, None, None, None),
        check_vma=False,
    )
```

```python
import functools
import math

import jax
import jax.numpy as jnp
import numpy as np
from jax import lax
from jax.experimental import pallas as pl
from jax.experimental.pallas import tpu as pltpu
from jax.sharding import PartitionSpec as P

SUBARRAYS = 4
LANES = 128
QUAD = 4
WIDE = 2
UNROLL_FB = True
BEAM_UNROLL = 8
PHASES = 4
VMEM_LIMIT = 56 * 2**20
MESH = pl.DeviceIdType.MESH


def dft_table(fine, lane_groups):
    index = np.arange(fine)
    angle = 2.0 * np.pi * (index[:, None] * index[None, :] % fine) / fine
    scale = 1.0 / math.sqrt(fine)
    cosine = np.cos(angle) * scale
    sine = np.sin(angle) * scale
    whole = np.stack([np.concatenate([cosine, sine]), np.concatenate([-sine, cosine])])
    halves = []
    for half in range(fine // LANES):
        k = half * LANES + (np.arange(LANES).reshape(-1, lane_groups).T).reshape(-1)
        halves.append(np.concatenate([whole[0][:, k].T, whole[1][:, k].T]))
    return jnp.asarray(np.concatenate(halves), jnp.bfloat16)


def unit_turn(turn):
    quarter = (turn + 8192) >> 14
    t = (turn - (quarter << 14)).astype(jnp.float32) * (2.0 * math.pi / 65536.0)
    u = t * t
    sine = t * (1.0 + u * (-1.0 / 6 + u * (1.0 / 120 + u * (-1.0 / 5040))))
    cosine = 1.0 + u * (-0.5 + u * (1.0 / 24 + u * (-1.0 / 720 + u * (1.0 / 40320))))
    odd = (quarter & 1) == 1
    c = jnp.where(odd, sine, cosine)
    s = jnp.where(odd, cosine, sine)
    c = jnp.where(((quarter + 1) & 2) == 2, -c, c)
    s = jnp.where((quarter & 2) == 2, -s, s)
    return c, s


def swap_index_with_lanes(tiles, block):
    lane = lax.broadcasted_iota(jnp.int32, tiles[0].shape, 1)
    bit = 1
    while bit < len(tiles):
        upper = (lane & (bit * block)) != 0
        swapped = list(tiles)
        for i in range(len(tiles)):
            if not i & bit:
                low, high = tiles[i], tiles[i | bit]
                swapped[i] = jnp.where(upper, pltpu.roll(high, bit * block, 1), low)
                swapped[i | bit] = jnp.where(upper, high, pltpu.roll(low, LANES - bit * block, 1))
        tiles = swapped
        bit *= 2
    return tiles


def kernel(
    sizes,
    amplitude,
    own_ref,
    taps_hbm,
    table_hbm,
    delays_hbm,
    station_hbm,
    beam_hbm,
    out_ref,
    volts,
    taps_ref,
    table,
    delay_in,
    station_in,
    beam_in,
    wide_taps,
    wide_int,
    member,
    steps,
    state,
    filtered,
    spectra,
    total_ref,
    turned,
    part,
    final,
    own_sem,
    small_sem,
    halo_send,
    halo_recv,
    send,
    recv,
    far_send,
    far_recv,
    keep_sem,
    *exchanged,
):
    n_chan, n_core, bits = sizes
    received, sent = exchanged[:bits], exchanged[bits:]
    chans, stations, samples = own_ref.shape[1:]
    tap_count, fine = taps_ref.shape
    beams = delay_in.shape[0]
    frames = final.shape[-2]
    halves = fine // LANES
    chunks = chans * halves
    lane_groups = LANES // stations
    hop = 3 * fine // 4
    groups = frames // PHASES
    quads = LANES // lane_groups // QUAD
    n_stn = 2**bits
    rows = 2 * beams // n_stn
    per = beams // n_stn
    width = frames * lane_groups
    tiles = QUAD * width // LANES
    halo = volts.shape[3] - samples
    stn, chan, core = (lax.axis_index(name) for name in ("stn", "chan", "beam"))

    def fetch(c):
        return pltpu.make_async_copy(
            own_ref.at[:, c], volts.at[:, c, :, pl.ds(0, samples)], own_sem.at[c]
        )

    small = [
        pltpu.make_async_copy(source, target, small_sem.at[i])
        for i, (source, target) in enumerate(
            (
                (taps_hbm, taps_ref),
                (delays_hbm, delay_in),
                (station_hbm, station_in),
                (beam_hbm, beam_in),
                (table_hbm, table),
            )
        )
    ]
    for copy in small:
        copy.start()
    for c in range(chans):
        fetch(c).start()

    own_bit = [(stn // 2 ** (bits - 1 - dim)) % 2 for dim in range(bits)]
    orders = (tuple(range(bits - 1, -1, -1)), tuple(range(bits)))

    def partner(dim):
        return (stn + (1 - 2 * own_bit[dim]) * 2 ** (bits - 1 - dim), chan, core)

    def far(dz, dc):
        return ((chan + dz) % n_chan, (core + dc) % n_core)

    offsets = [(dz, dc) for dz in range(n_chan) for dc in range(n_core)]
    barrier = pltpu.get_barrier_semaphore()
    peers = [partner(dim) for dim in range(bits)] + [(stn, *far(dz, dc)) for dz, dc in offsets[1:]]
    for peer in peers:
        pl.semaphore_signal(barrier, inc=1, device_id=peer, device_id_type=MESH)
    pl.semaphore_wait(barrier, len(peers))

    def halo_copy(c):
        return pltpu.make_async_remote_copy(
            src_ref=own_ref.at[:, c, :, pl.ds(0, halo)],
            dst_ref=volts.at[:, c, :, pl.ds(samples, halo)],
            send_sem=halo_send.at[c],
            recv_sem=halo_recv.at[c],
            device_id=(stn, chan, core - 1),
            device_id_type=MESH,
        )

    @pl.when(core > 0)
    def _():
        for c in range(chans):
            halo_copy(c).start()

    @pl.when(core == n_core - 1)
    def _():
        volts[:, :, :, samples:] = jnp.zeros((2, chans, stations, halo), volts.dtype)

    for copy in small:
        copy.wait()

    for phase in range(PHASES):
        shift = hop * phase % fine
        rolled = taps_ref[...]
        if shift:
            rolled = pltpu.roll(rolled, shift, 1)
        column = lax.broadcasted_iota(jnp.int32, (1, fine), 1)
        for u in range(tap_count + 1):
            late = rolled[u : u + 1] if u < tap_count else jnp.zeros((1, fine), jnp.float32)
            early = rolled[u - 1 : u] if u > 0 else jnp.zeros((1, fine), jnp.float32)
            row = jnp.where(column >= shift, late, early)
            wide_taps[phase, u] = jnp.broadcast_to(row, (16, fine)).astype(jnp.bfloat16)

    def widened(value, count):
        wide_int[...] = jnp.zeros(wide_int.shape, jnp.int32)
        wide_int[0:count, 0:stations] = value
        full = wide_int[...]
        step = stations
        while step < LANES:
            full = full + pltpu.roll(full, step, 1)
            step *= 2
        return full[0:count]

    group_of_lane = lax.broadcasted_iota(jnp.int32, (1, LANES), 1) // stations
    station_row = widened(station_in[...], 1).astype(jnp.float32)
    square = (beams, beams)
    diagonal = lax.broadcasted_iota(jnp.int32, square, 0) == lax.broadcasted_iota(jnp.int32, square, 1)
    beam_row = jnp.broadcast_to(beam_in[...].astype(jnp.float32), square)
    beam_column = jnp.sum(jnp.where(diagonal, beam_row, 0.0), axis=1, keepdims=True)
    member[...] = jnp.where(beam_column == station_row, amplitude, 0.0)
    delay = widened(delay_in[...], beams)
    wide_int[...] = delay
    for i, stride in enumerate((lane_groups, QUAD * lane_groups)):
        c, s = unit_turn((delay * stride) & 65535)
        steps[i, 0] = c
        steps[i, 1] = -s

    def filter_channel(c):
        @pl.loop(0, 2)
        def _(ri):
            for half in range(halves):
                for phase in range(PHASES):
                    shift = hop * phase % fine
                    block0 = hop * phase // fine
                    first = 0 if shift < (half + 1) * LANES else 1
                    last = tap_count - 1 if shift <= half * LANES else tap_count
                    lanes = slice(half * LANES, (half + 1) * LANES)
                    taps = {
                        u: wide_taps[phase, u, :, lanes][None] for u in range(first, last + 1)
                    }
                    sums = [[None, None] for _ in range(groups)]
                    for block in range(block0 + first, block0 + last + 1 + 3 * (groups - 1)):
                        at = block * fine + half * LANES
                        value = volts[ri, c, :, at : at + LANES].reshape(stations // 16, 16, LANES)
                        for g in range(groups):
                            u = block - block0 - 3 * g
                            if first <= u <= last:
                                term = taps[u] * value
                                so_far = sums[g][u % 2]
                                sums[g][u % 2] = term if so_far is None else so_far + term
                    for g in range(groups):
                        f = PHASES * g + phase
                        filtered[
                            f * stations : (f + 1) * stations,
                            pl.ds(pl.multiple_of(ri * fine + half * LANES, LANES), LANES),
                        ] = (sums[g][0] + sums[g][1]).reshape(stations, LANES)

    def transform():
        count = LANES // lane_groups

        def one(fb):
            rhs = filtered[pl.ds(pl.multiple_of(fb * LANES, LANES), WIDE * LANES), :]
            result = lax.dot_general(
                table[...], rhs, (((1,), (1,)), ((), ())), preferred_element_type=jnp.float32
            )
            for half in range(halves):
                for ri in range(2):
                    for sub in range(WIDE):
                        pieces = [
                            result[
                                ((half * 2 + ri) * lane_groups + j) * count : ((half * 2 + ri) * lane_groups + j + 1) * count,
                                sub * LANES : (sub + 1) * LANES,
                            ]
                            for j in range(lane_groups)
                        ]
                        for j, piece in enumerate(swap_index_with_lanes(pieces, stations)):
                            at = pl.multiple_of(((fb + sub) * lane_groups + j) * count, count)
                            spectra[half, ri, pl.ds(at, count), :] = piece

        if UNROLL_FB:
            for fb in range(0, frames // lane_groups, WIDE):
                one(fb)
        else:
            @pl.loop(0, frames // lane_groups // WIDE)
            def _(fb):
                one(fb * WIDE)

    def form_beams(chunk, c, half):
        count = LANES // lane_groups
        frequency = (chan * chans + c) * fine + half * LANES + group_of_lane
        cosine, sine = unit_turn((wide_int[...] * frequency) & 65535)
        state[0] = cosine * member[...]
        state[1] = -sine * member[...]
        lane = lax.broadcasted_iota(jnp.int32, (frames, LANES), 1) // stations
        out_lane = lax.broadcasted_iota(jnp.int32, (2 * beams, LANES), 1)

        def times(a, i):
            e_re, e_im = steps[i, 0], steps[i, 1]
            return (a[0] * e_re - a[1] * e_im, a[0] * e_im + a[1] * e_re)

        def stacked(top, bottom):
            both = [v.reshape(n_stn, per, LANES) for v in (top, bottom)]
            return jnp.stack(both, axis=1).reshape(2 * beams, LANES)

        @pl.loop(0, quads, unroll=BEAM_UNROLL)
        def _(quad):
            first = weight = (state[0], state[1])
            outs = []
            for q in range(QUAD):
                if q:
                    weight = times(weight, 0)
                w_re, w_im = weight
                lhs = jnp.concatenate([stacked(w_re, w_im), stacked(-w_im, w_re)], axis=1)
                at = quad * QUAD + q
                x = [spectra.at[half, ri][pl.ds(at, frames, stride=count), :] for ri in range(2)]
                blocks = [
                    jnp.concatenate([jnp.where(lane == j, v, 0.0) for v in x], axis=1)
                    for j in range(lane_groups)
                ]
                if width < LANES:
                    blocks.append(jnp.zeros((LANES - width, 2 * LANES), jnp.float32))
                turn = q * width % LANES
                if turn:
                    blocks = [jnp.concatenate(blocks, axis=0)]
                    blocks = [blocks[0][LANES - turn :], blocks[0][: LANES - turn]]
                rhs = jnp.concatenate(blocks, axis=0)
                result = lax.dot_general(
                    lhs.astype(jnp.bfloat16),
                    rhs.astype(jnp.bfloat16),
                    (((1,), (1,)), ((), ())),
                    preferred_element_type=jnp.float32,
                )
                outs.append(result)
            following = times(first, 1)
            state[0] = following[0]
            state[1] = following[1]
            for t in range(tiles):
                value = None
                for q in range(QUAD):
                    start = q * width - t * LANES
                    if -width < start < LANES:
                        value = outs[q] if value is None else jnp.where(out_lane >= start, outs[q], value)
                value = value.astype(jnp.bfloat16)
                for d in range(n_stn):
                    place = [(d >> (bits - 1 - dim)) & 1 for dim in range(bits)]
                    part[(chunk, quad // (quads // 2), *place, quad % (quads // 2), t)] = value[
                        d * rows : (d + 1) * rows
                    ]

    def region(order, stage, last):
        index = [slice(None)] * bits
        for dim in orders[order][:stage]:
            index[dim] = own_bit[dim]
        if stage < bits:
            index[orders[order][stage]] = last(orders[order][stage])
        return index

    def other(dim):
        return 1 - own_bit[dim]

    def with_received(chunk, order, stage, index):
        value = part[(chunk, order, *index)].astype(jnp.float32)
        for earlier in range(stage):
            kept = [dim for dim in range(bits) if dim not in orders[order][: earlier + 1]]
            piece = received[earlier][(chunk, order, *(index[dim] for dim in kept))]
            value = value + piece.astype(jnp.float32)
        return value

    def hop_copy(chunk, order, stage):
        if stage == 0:
            source = part.at[(chunk, order, *region(order, 0, other))]
        else:
            source = sent[stage - 1].at[chunk, order]
        return pltpu.make_async_remote_copy(
            src_ref=source,
            dst_ref=received[stage].at[chunk, order],
            send_sem=send.at[stage, chunk, order],
            recv_sem=recv.at[stage, chunk, order],
            device_id=partner(orders[order][stage]),
            device_id_type=MESH,
        )

    def place_of(chunk):
        c = chunk // halves
        lanes = pl.ds(pl.multiple_of((chunk % halves) * LANES, LANES), LANES)
        return out_ref.at[:, :, chan * chans + c, core, :, lanes]

    def deliver(chunk, number):
        z, k = far(*offsets[number])
        return pltpu.make_async_remote_copy(
            src_ref=final.at[chunk, z, k],
            dst_ref=place_of(chunk),
            send_sem=far_send.at[chunk, number],
            recv_sem=far_recv.at[chunk, number],
            device_id=(stn, z, k),
            device_id_type=MESH,
        )

    def keep(chunk):
        return pltpu.make_async_copy(final.at[chunk, chan, core], place_of(chunk), keep_sem.at[chunk])

    def finish(chunk):
        for order in range(2):
            value = with_received(chunk, order, bits, own_bit)
            for quad in range(quads // 2):
                at = (order * (quads // 2) + quad) * rows
                for t in range(tiles):
                    total_ref[t, at : at + rows, :] = value[quad, t]
        for t in range(tiles):
            turned[t * LANES : (t + 1) * LANES, :] = total_ref[t].T
        pieces = [turned[i * frames : (i + 1) * frames, :] for i in range(rows)]
        for row, piece in enumerate(swap_index_with_lanes(pieces, 1)):
            ri, b = divmod(row, per)
            device, at = divmod(b, per // (n_chan * n_core))
            z, k = divmod(device, n_core)
            final[chunk, z, k, at, ri] = piece.astype(jnp.bfloat16)

    def step(chunk, stage):
        for order in range(2):
            hop_copy(chunk, order, stage - 1).wait_recv()
            if stage < bits:
                sent[stage - 1][chunk, order] = with_received(
                    chunk, order, stage, region(order, stage, other)
                ).astype(jnp.bfloat16)
                hop_copy(chunk, order, stage).start()
        if stage == bits:
            finish(chunk)
            for number in range(len(offsets) - 1, 0, -1):
                deliver(chunk, number).start()
            keep(chunk).start()

    @pl.loop(0, chunks + bits)
    def _(tick):
        @pl.when(tick < chunks)
        def _():
            c = tick // halves
            half = tick % halves

            @pl.when(half == 0)
            def _():
                fetch(c).wait()

                @pl.when(core < n_core - 1)
                def _():
                    halo_copy(c).wait_recv()

                filter_channel(c)
                transform()

            form_beams(tick, c, half)
            for order in range(2):
                hop_copy(tick, order, 0).start()

        for stage in range(1, bits + 1):
            chunk = tick - stage

            @pl.when((chunk >= 0) & (chunk < chunks))
            def _(chunk=chunk, stage=stage):
                step(chunk, stage)

    @pl.when(core > 0)
    def _():
        for c in range(chans):
            halo_copy(c).wait_send()

    @pl.loop(0, chunks)
    def _(chunk):
        for order in range(2):
            for stage in range(bits):
                hop_copy(chunk, order, stage).wait_send()
        for number in range(1, len(offsets)):
            deliver(chunk, number).wait()
        keep(chunk).wait()


def body(volts, taps, delays, station_sub, beam_sub):
    own = jnp.transpose(volts, (0, 2, 1, 3))
    chans, stations, samples = own.shape[1:]
    tap_count, fine = taps.shape
    beams = delays.shape[0]
    n_stn, n_chan, n_core = (lax.axis_size(name) for name in ("stn", "chan", "beam"))
    bits = n_stn.bit_length() - 1
    hop = 3 * fine // 4
    frames = samples // hop
    per = beams // n_stn
    per_device = per // (n_chan * n_core)
    halves = fine // LANES
    chunks = chans * halves
    lane_groups = LANES // stations
    quads = LANES // lane_groups // QUAD
    tiles = QUAD * frames * lane_groups // LANES
    rows = 2 * per
    peers = n_chan * n_core
    assert n_stn == 2**bits and rows == QUAD * lane_groups and quads * rows == LANES
    assert QUAD * frames * lane_groups == tiles * LANES and frames * lane_groups <= LANES
    blocks = hop * (PHASES - 1) // fine + tap_count + 1 + 3 * (frames // PHASES - 1)
    amplitude = 1.0 / math.sqrt(stations * n_stn // SUBARRAYS)
    block = (quads // 2, tiles, rows, LANES)
    pieces = [
        pltpu.VMEM((chunks, 2) + (2,) * (bits - 1 - t) + block, jnp.bfloat16) for t in range(bits)
    ]
    hbm = pl.BlockSpec(memory_space=pltpu.HBM)
    dma = pltpu.SemaphoreType.DMA
    out = pl.pallas_call(
        functools.partial(kernel, (n_chan, n_core, bits), amplitude),
        out_shape=jax.ShapeDtypeStruct(
            (per_device, 2, n_chan * chans, n_core, frames, fine), jnp.bfloat16
        ),
        in_specs=[hbm] * 6,
        out_specs=pl.BlockSpec(memory_space=pl.ANY),
        scratch_shapes=[
            pltpu.VMEM((2, chans, stations, blocks * fine), jnp.bfloat16),
            pltpu.VMEM((tap_count, fine), jnp.float32),
            pltpu.VMEM((halves * 2 * LANES, 2 * fine), jnp.bfloat16),
            pltpu.VMEM((beams, stations), jnp.int32),
            pltpu.VMEM((1, stations), jnp.int32),
            pltpu.VMEM((1, beams), jnp.int32),
            pltpu.VMEM((PHASES, tap_count + 1, 16, fine), jnp.bfloat16),
            pltpu.VMEM((beams, LANES), jnp.int32),
            pltpu.VMEM((beams, LANES), jnp.float32),
            pltpu.VMEM((2, 2, beams, LANES), jnp.float32),
            pltpu.VMEM((2, beams, LANES), jnp.float32),
            pltpu.VMEM((frames * stations, 2 * fine), jnp.bfloat16),
            pltpu.VMEM((halves, 2, frames * LANES // lane_groups, LANES), jnp.float32),
            pltpu.VMEM((tiles, LANES, LANES), jnp.float32),
            pltpu.VMEM((tiles * LANES, LANES), jnp.float32),
            pltpu.VMEM((chunks, 2) + (2,) * bits + block, jnp.bfloat16),
            pltpu.VMEM((chunks, n_chan, n_core, per_device, 2, frames, LANES), jnp.bfloat16),
            dma((chans,)),
            dma((5,)),
            dma((chans,)),
            dma((chans,)),
            dma((bits, chunks, 2)),
            dma((bits, chunks, 2)),
            dma((chunks, peers)),
            dma((chunks, peers)),
            dma((chunks,)),
            *pieces,
            *pieces[1:],
        ],
        compiler_params=pltpu.CompilerParams(
            collective_id=0, has_side_effects=True, vmem_limit_bytes=VMEM_LIMIT
        ),
        name="channelize_and_beamform",
    )(
        own,
        taps,
        dft_table(fine, lane_groups),
        delays,
        station_sub[None],
        beam_sub[None],
    )
    return out.reshape(per_device, 2, n_chan * chans, n_core * frames, fine).astype(jnp.float32)


def solution(mesh):
    placed = (P(None, "stn", "chan", "beam"), P(), P(None, "stn"), P("stn"), P())
    return jax.shard_map(
        body,
        mesh=mesh,
        in_specs=placed,
        out_specs=P(("stn", "chan", "beam"), None, None, None, None),
        check_vma=False,
    )
```

```python
import functools
import math

import jax
import jax.numpy as jnp
import numpy as np
from jax import lax
from jax.experimental import pallas as pl
from jax.experimental.pallas import tpu as pltpu
from jax.sharding import PartitionSpec as P

SUBARRAYS = 4
LANES = 128
QUAD = 4
WIDE = 2
UNROLL_FB = True
LEAD = 2
DELAY = 0
DRAIN = 3
PHASES = 4
VMEM_LIMIT = 32 * 2**20
MESH = pl.DeviceIdType.MESH


def dft_table(fine, lane_groups):
    index = np.arange(fine)
    angle = 2.0 * np.pi * (index[:, None] * index[None, :] % fine) / fine
    scale = 1.0 / math.sqrt(fine)
    cosine = np.cos(angle) * scale
    sine = np.sin(angle) * scale
    whole = np.stack([np.concatenate([cosine, sine]), np.concatenate([-sine, cosine])])
    halves = []
    for half in range(fine // LANES):
        k = half * LANES + (np.arange(LANES).reshape(-1, lane_groups).T).reshape(-1)
        halves.append(np.concatenate([whole[0][:, k].T, whole[1][:, k].T]))
    return jnp.asarray(np.concatenate(halves), jnp.bfloat16)


def unit_turn(turn):
    quarter = (turn + 8192) >> 14
    t = (turn - (quarter << 14)).astype(jnp.float32) * (2.0 * math.pi / 65536.0)
    u = t * t
    sine = t * (1.0 + u * (-1.0 / 6 + u * (1.0 / 120 + u * (-1.0 / 5040))))
    cosine = 1.0 + u * (-0.5 + u * (1.0 / 24 + u * (-1.0 / 720 + u * (1.0 / 40320))))
    odd = (quarter & 1) == 1
    c = jnp.where(odd, sine, cosine)
    s = jnp.where(odd, cosine, sine)
    c = jnp.where(((quarter + 1) & 2) == 2, -c, c)
    s = jnp.where((quarter & 2) == 2, -s, s)
    return c, s


def swap_index_with_lanes(tiles, block):
    lane = lax.broadcasted_iota(jnp.int32, tiles[0].shape, 1)
    bit = 1
    while bit < len(tiles):
        upper = (lane & (bit * block)) != 0
        swapped = list(tiles)
        for i in range(len(tiles)):
            if not i & bit:
                low, high = tiles[i], tiles[i | bit]
                swapped[i] = jnp.where(upper, pltpu.roll(high, bit * block, 1), low)
                swapped[i | bit] = jnp.where(upper, high, pltpu.roll(low, LANES - bit * block, 1))
        tiles = swapped
        bit *= 2
    return tiles


def kernel(
    sizes,
    amplitude,
    own_ref,
    taps_hbm,
    table_hbm,
    delays_hbm,
    station_hbm,
    beam_hbm,
    out_ref,
    volts,
    taps_ref,
    table,
    delay_in,
    station_in,
    beam_in,
    wide_taps,
    wide_int,
    member,
    steps,
    state,
    filtered,
    spectra,
    total_ref,
    turned,
    part,
    final,
    own_sem,
    small_sem,
    halo_send,
    halo_recv,
    send,
    recv,
    far_send,
    far_recv,
    keep_sem,
    *exchanged,
):
    n_chan, n_core, bits = sizes
    received, sent = exchanged[:bits], exchanged[bits:]
    chans, stations, samples = own_ref.shape[1:]
    tap_count, fine = taps_ref.shape
    beams = delay_in.shape[0]
    frames = final.shape[-2]
    halves = fine // LANES
    chunks = chans * halves
    lane_groups = LANES // stations
    hop = 3 * fine // 4
    groups = frames // PHASES
    quads = LANES // lane_groups // QUAD
    n_stn = 2**bits
    rows = 2 * beams // n_stn
    per = beams // n_stn
    width = frames * lane_groups
    tiles = QUAD * width // LANES
    halo = volts.shape[3] - samples
    stn, chan, core = (lax.axis_index(name) for name in ("stn", "chan", "beam"))

    def fetch(c):
        return pltpu.make_async_copy(
            own_ref.at[:, c], volts.at[:, c, :, pl.ds(0, samples)], own_sem.at[c]
        )

    small = [
        pltpu.make_async_copy(source, target, small_sem.at[i])
        for i, (source, target) in enumerate(
            (
                (taps_hbm, taps_ref),
                (delays_hbm, delay_in),
                (station_hbm, station_in),
                (beam_hbm, beam_in),
                (table_hbm, table),
            )
        )
    ]
    for copy in small:
        copy.start()
    for c in range(chans):
        fetch(c).start()

    own_bit = [(stn // 2 ** (bits - 1 - dim)) % 2 for dim in range(bits)]
    orders = (tuple(range(bits - 1, -1, -1)), tuple(range(bits)))

    def partner(dim):
        return (stn + (1 - 2 * own_bit[dim]) * 2 ** (bits - 1 - dim), chan, core)

    def far(dz, dc):
        return ((chan + dz) % n_chan, (core + dc) % n_core)

    offsets = [(dz, dc) for dz in range(n_chan) for dc in range(n_core)]
    barrier = pltpu.get_barrier_semaphore()
    peers = [partner(dim) for dim in range(bits)] + [(stn, *far(dz, dc)) for dz, dc in offsets[1:]]
    for peer in peers:
        pl.semaphore_signal(barrier, inc=1, device_id=peer, device_id_type=MESH)
    def halo_copy(c):
        return pltpu.make_async_remote_copy(
            src_ref=own_ref.at[:, c, :, pl.ds(0, halo)],
            dst_ref=volts.at[:, c, :, pl.ds(samples, halo)],
            send_sem=halo_send.at[c],
            recv_sem=halo_recv.at[c],
            device_id=(stn, chan, core - 1),
            device_id_type=MESH,
        )

    for copy in small:
        copy.wait()

    for phase in range(PHASES):
        shift = hop * phase % fine
        rolled = taps_ref[...]
        if shift:
            rolled = pltpu.roll(rolled, shift, 1)
        column = lax.broadcasted_iota(jnp.int32, (1, fine), 1)
        for u in range(tap_count + 1):
            late = rolled[u : u + 1] if u < tap_count else jnp.zeros((1, fine), jnp.float32)
            early = rolled[u - 1 : u] if u > 0 else jnp.zeros((1, fine), jnp.float32)
            row = jnp.where(column >= shift, late, early)
            wide_taps[phase, u] = jnp.broadcast_to(row, (16, fine)).astype(jnp.bfloat16)

    pl.semaphore_wait(barrier, len(peers))

    @pl.when(core > 0)
    def _():
        halo_copy(0).start()

    @pl.when(core == n_core - 1)
    def _():
        volts[:, :, :, samples:] = jnp.zeros((2, chans, stations, halo), volts.dtype)

    def widened(value, count):
        wide_int[...] = jnp.zeros(wide_int.shape, jnp.int32)
        wide_int[0:count, 0:stations] = value
        full = wide_int[...]
        step = stations
        while step < LANES:
            full = full + pltpu.roll(full, step, 1)
            step *= 2
        return full[0:count]

    group_of_lane = lax.broadcasted_iota(jnp.int32, (1, LANES), 1) // stations
    station_row = widened(station_in[...], 1).astype(jnp.float32)
    square = (beams, beams)
    diagonal = lax.broadcasted_iota(jnp.int32, square, 0) == lax.broadcasted_iota(jnp.int32, square, 1)
    beam_row = jnp.broadcast_to(beam_in[...].astype(jnp.float32), square)
    beam_column = jnp.sum(jnp.where(diagonal, beam_row, 0.0), axis=1, keepdims=True)
    member[...] = jnp.where(beam_column == station_row, amplitude, 0.0)
    delay = widened(delay_in[...], beams)
    wide_int[...] = delay
    for i, stride in enumerate((lane_groups, QUAD * lane_groups)):
        c, s = unit_turn((delay * stride) & 65535)
        steps[i, 0] = c
        steps[i, 1] = -s

    def filter_channel(c):
        @pl.loop(0, 2)
        def _(ri):
            for half in range(halves):
                for phase in range(PHASES):
                    shift = hop * phase % fine
                    block0 = hop * phase // fine
                    first = 0 if shift < (half + 1) * LANES else 1
                    last = tap_count - 1 if shift <= half * LANES else tap_count
                    lanes = slice(half * LANES, (half + 1) * LANES)
                    taps = {
                        u: wide_taps[phase, u, :, lanes][None] for u in range(first, last + 1)
                    }
                    sums = [[None, None] for _ in range(groups)]
                    for block in range(block0 + first, block0 + last + 1 + 3 * (groups - 1)):
                        at = block * fine + half * LANES
                        value = volts[ri, c, :, at : at + LANES].reshape(stations // 16, 16, LANES)
                        for g in range(groups):
                            u = block - block0 - 3 * g
                            if first <= u <= last:
                                term = taps[u] * value
                                so_far = sums[g][u % 2]
                                sums[g][u % 2] = term if so_far is None else so_far + term
                    for g in range(groups):
                        f = PHASES * g + phase
                        filtered[
                            f * stations : (f + 1) * stations,
                            pl.ds(pl.multiple_of(ri * fine + half * LANES, LANES), LANES),
                        ] = (sums[g][0] + sums[g][1]).reshape(stations, LANES)

    def transform():
        count = LANES // lane_groups

        def one(fb):
            rhs = filtered[pl.ds(pl.multiple_of(fb * LANES, LANES), WIDE * LANES), :]
            result = lax.dot_general(
                table[...], rhs, (((1,), (1,)), ((), ())), preferred_element_type=jnp.float32
            )
            for half in range(halves):
                for ri in range(2):
                    for sub in range(WIDE):
                        pieces = [
                            result[
                                ((half * 2 + ri) * lane_groups + j) * count : ((half * 2 + ri) * lane_groups + j + 1) * count,
                                sub * LANES : (sub + 1) * LANES,
                            ]
                            for j in range(lane_groups)
                        ]
                        for j, piece in enumerate(swap_index_with_lanes(pieces, stations)):
                            at = pl.multiple_of(((fb + sub) * lane_groups + j) * count, count)
                            spectra[half, ri, pl.ds(at, count), :] = piece

        if UNROLL_FB:
            for fb in range(0, frames // lane_groups, WIDE):
                one(fb)
        else:
            @pl.loop(0, frames // lane_groups // WIDE)
            def _(fb):
                one(fb * WIDE)

    def form_beams(chunk, c, half):
        count = LANES // lane_groups
        frequency = (chan * chans + c) * fine + half * LANES + group_of_lane
        cosine, sine = unit_turn((wide_int[...] * frequency) & 65535)
        state[0] = cosine * member[...]
        state[1] = -sine * member[...]
        lane = lax.broadcasted_iota(jnp.int32, (frames, LANES), 1) // stations
        out_lane = lax.broadcasted_iota(jnp.int32, (2 * beams, LANES), 1)

        def times(a, i):
            e_re, e_im = steps[i, 0], steps[i, 1]
            return (a[0] * e_re - a[1] * e_im, a[0] * e_im + a[1] * e_re)

        def stacked(top, bottom):
            both = [v.reshape(n_stn, per, LANES) for v in (top, bottom)]
            return jnp.stack(both, axis=1).reshape(2 * beams, LANES)

        def one(quad):
            first = weight = (state[0], state[1])
            outs = []
            for q in range(QUAD):
                if q:
                    weight = times(weight, 0)
                w_re, w_im = weight
                lhs = jnp.concatenate([stacked(w_re, w_im), stacked(-w_im, w_re)], axis=1)
                at = quad * QUAD + q
                x = [spectra.at[half, ri][pl.ds(at, frames, stride=count), :] for ri in range(2)]
                blocks = [
                    jnp.concatenate([jnp.where(lane == j, v, 0.0) for v in x], axis=1)
                    for j in range(lane_groups)
                ]
                if width < LANES:
                    blocks.append(jnp.zeros((LANES - width, 2 * LANES), jnp.float32))
                turn = q * width % LANES
                if turn:
                    blocks = [jnp.concatenate(blocks, axis=0)]
                    blocks = [blocks[0][LANES - turn :], blocks[0][: LANES - turn]]
                rhs = jnp.concatenate(blocks, axis=0)
                result = lax.dot_general(
                    lhs.astype(jnp.bfloat16),
                    rhs.astype(jnp.bfloat16),
                    (((1,), (1,)), ((), ())),
                    preferred_element_type=jnp.float32,
                )
                outs.append(result)
            following = times(first, 1)
            state[0] = following[0]
            state[1] = following[1]
            for t in range(tiles):
                value = None
                for q in range(QUAD):
                    start = q * width - t * LANES
                    if -width < start < LANES:
                        value = outs[q] if value is None else jnp.where(out_lane >= start, outs[q], value)
                value = value.astype(jnp.bfloat16)
                for d in range(n_stn):
                    place = [(d >> (bits - 1 - dim)) & 1 for dim in range(bits)]
                    part[(chunk, quad // (quads // 2), *place, quad % (quads // 2), t)] = value[
                        d * rows : (d + 1) * rows
                    ]

        for quad in range(quads):
            one(quad)
            if (quad + 1) % (quads // 2) == 0:
                hop_copy(chunk, quad // (quads // 2), 0).start()

    def region(order, stage, last):
        index = [slice(None)] * bits
        for dim in orders[order][:stage]:
            index[dim] = own_bit[dim]
        if stage < bits:
            index[orders[order][stage]] = last(orders[order][stage])
        return index

    def other(dim):
        return 1 - own_bit[dim]

    def with_received(chunk, order, stage, index):
        value = part[(chunk, order, *index)].astype(jnp.float32)
        for earlier in range(stage):
            kept = [dim for dim in range(bits) if dim not in orders[order][: earlier + 1]]
            piece = received[earlier][(chunk, order, *(index[dim] for dim in kept))]
            value = value + piece.astype(jnp.float32)
        return value

    def hop_copy(chunk, order, stage):
        if stage == 0:
            source = part.at[(chunk, order, *region(order, 0, other))]
        else:
            source = sent[stage - 1].at[chunk, order]
        return pltpu.make_async_remote_copy(
            src_ref=source,
            dst_ref=received[stage].at[chunk, order],
            send_sem=send.at[stage, chunk, order],
            recv_sem=recv.at[stage, chunk, order],
            device_id=partner(orders[order][stage]),
            device_id_type=MESH,
        )

    def place_of(chunk):
        c = chunk // halves
        lanes = pl.ds(pl.multiple_of((chunk % halves) * LANES, LANES), LANES)
        return out_ref.at[:, :, chan * chans + c, core, :, lanes]

    def deliver(chunk, number):
        z, k = far(*offsets[number])
        return pltpu.make_async_remote_copy(
            src_ref=final.at[chunk, z, k],
            dst_ref=place_of(chunk),
            send_sem=far_send.at[chunk, number],
            recv_sem=far_recv.at[chunk, number],
            device_id=(stn, z, k),
            device_id_type=MESH,
        )

    def keep(chunk):
        return pltpu.make_async_copy(final.at[chunk, chan, core], place_of(chunk), keep_sem.at[chunk])

    def finish(chunk):
        for order in range(2):
            value = with_received(chunk, order, bits, own_bit)
            for quad in range(quads // 2):
                at = (order * (quads // 2) + quad) * rows
                for t in range(tiles):
                    total_ref[t, at : at + rows, :] = value[quad, t]
        for t in range(tiles):
            turned[t * LANES : (t + 1) * LANES, :] = total_ref[t].T
        pieces = [turned[i * frames : (i + 1) * frames, :] for i in range(rows)]
        for row, piece in enumerate(swap_index_with_lanes(pieces, 1)):
            ri, b = divmod(row, per)
            device, at = divmod(b, per // (n_chan * n_core))
            z, k = divmod(device, n_core)
            final[chunk, z, k, at, ri] = piece.astype(jnp.bfloat16)

    def step(chunk, stage):
        for order in range(2):
            hop_copy(chunk, order, stage - 1).wait_recv()
            if stage < bits:
                sent[stage - 1][chunk, order] = with_received(
                    chunk, order, stage, region(order, stage, other)
                ).astype(jnp.bfloat16)
                hop_copy(chunk, order, stage).start()
        if stage == bits:
            finish(chunk)
            for number in range(len(offsets) - 1, 0, -1):
                deliver(chunk, number).start()
            keep(chunk).start()

    def drain(chunk):
        for order in range(2):
            for stage in range(bits):
                hop_copy(chunk, order, stage).wait_send()
        for number in range(1, len(offsets)):
            deliver(chunk, number).wait()
        keep(chunk).wait()

    @pl.loop(0, chunks + LEAD + bits + DELAY + DRAIN)
    def _(tick):
        def during(chunk, action):
            @pl.when((chunk >= 0) & (chunk < chunks))
            def _():
                action(chunk)

        during(tick - LEAD, lambda chunk: form_beams(chunk, chunk // halves, chunk % halves))
        c = tick // halves

        @pl.when((tick % halves == 0) & (c < chans))
        def _():
            fetch(c).wait()

            @pl.when(core < n_core - 1)
            def _():
                halo_copy(c).wait_recv()

            @pl.when((core > 0) & (c + 1 < chans))
            def _():
                halo_copy(c + 1).start()

            filter_channel(c)

        @pl.when((tick % halves == halves - 1) & (c < chans))
        def _():
            transform()

        for stage in range(1, bits + 1):
            during(tick - LEAD - DELAY - stage, lambda chunk, stage=stage: step(chunk, stage))
        during(tick - LEAD - DELAY - bits - DRAIN, drain)

    @pl.when(core > 0)
    def _():
        for c in range(chans):
            halo_copy(c).wait_send()


def body(volts, taps, delays, station_sub, beam_sub):
    own = jnp.transpose(volts, (0, 2, 1, 3))
    chans, stations, samples = own.shape[1:]
    tap_count, fine = taps.shape
    beams = delays.shape[0]
    n_stn, n_chan, n_core = (lax.axis_size(name) for name in ("stn", "chan", "beam"))
    bits = n_stn.bit_length() - 1
    hop = 3 * fine // 4
    frames = samples // hop
    per = beams // n_stn
    per_device = per // (n_chan * n_core)
    halves = fine // LANES
    chunks = chans * halves
    lane_groups = LANES // stations
    quads = LANES // lane_groups // QUAD
    tiles = QUAD * frames * lane_groups // LANES
    rows = 2 * per
    peers = n_chan * n_core
    assert n_stn == 2**bits and rows == QUAD * lane_groups and quads * rows == LANES
    assert QUAD * frames * lane_groups == tiles * LANES and frames * lane_groups <= LANES
    blocks = hop * (PHASES - 1) // fine + tap_count + 1 + 3 * (frames // PHASES - 1)
    amplitude = 1.0 / math.sqrt(stations * n_stn // SUBARRAYS)
    block = (quads // 2, tiles, rows, LANES)
    pieces = [
        pltpu.VMEM((chunks, 2) + (2,) * (bits - 1 - t) + block, jnp.bfloat16) for t in range(bits)
    ]
    hbm = pl.BlockSpec(memory_space=pltpu.HBM)
    dma = pltpu.SemaphoreType.DMA
    out = pl.pallas_call(
        functools.partial(kernel, (n_chan, n_core, bits), amplitude),
        out_shape=jax.ShapeDtypeStruct(
            (per_device, 2, n_chan * chans, n_core, frames, fine), jnp.bfloat16
        ),
        in_specs=[hbm] * 6,
        out_specs=pl.BlockSpec(memory_space=pl.ANY),
        scratch_shapes=[
            pltpu.VMEM((2, chans, stations, blocks * fine), jnp.bfloat16),
            pltpu.VMEM((tap_count, fine), jnp.float32),
            pltpu.VMEM((halves * 2 * LANES, 2 * fine), jnp.bfloat16),
            pltpu.VMEM((beams, stations), jnp.int32),
            pltpu.VMEM((1, stations), jnp.int32),
            pltpu.VMEM((1, beams), jnp.int32),
            pltpu.VMEM((PHASES, tap_count + 1, 16, fine), jnp.bfloat16),
            pltpu.VMEM((beams, LANES), jnp.int32),
            pltpu.VMEM((beams, LANES), jnp.float32),
            pltpu.VMEM((2, 2, beams, LANES), jnp.float32),
            pltpu.VMEM((2, beams, LANES), jnp.float32),
            pltpu.VMEM((frames * stations, 2 * fine), jnp.bfloat16),
            pltpu.VMEM((halves, 2, frames * LANES // lane_groups, LANES), jnp.float32),
            pltpu.VMEM((tiles, LANES, LANES), jnp.float32),
            pltpu.VMEM((tiles * LANES, LANES), jnp.float32),
            pltpu.VMEM((chunks, 2) + (2,) * bits + block, jnp.bfloat16),
            pltpu.VMEM((chunks, n_chan, n_core, per_device, 2, frames, LANES), jnp.bfloat16),
            dma((chans,)),
            dma((5,)),
            dma((chans,)),
            dma((chans,)),
            dma((bits, chunks, 2)),
            dma((bits, chunks, 2)),
            dma((chunks, peers)),
            dma((chunks, peers)),
            dma((chunks,)),
            *pieces,
            *pieces[1:],
        ],
        compiler_params=pltpu.CompilerParams(
            collective_id=0, has_side_effects=True, vmem_limit_bytes=VMEM_LIMIT
        ),
        name="channelize_and_beamform",
    )(
        *(
            pltpu.with_memory_space_constraint(x, pltpu.HBM)
            for x in (
                own,
                taps,
                dft_table(fine, lane_groups),
                delays,
                station_sub[None],
                beam_sub[None],
            )
        )
    )
    return out.reshape(per_device, 2, n_chan * chans, n_core * frames, fine).astype(jnp.float32)


def solution(mesh):
    placed = (P(None, "stn", "chan", "beam"), P(), P(None, "stn"), P("stn"), P())
    return jax.shard_map(
        body,
        mesh=mesh,
        in_specs=placed,
        out_specs=P(("stn", "chan", "beam"), None, None, None, None),
        check_vma=False,
    )
```

```python
import functools
import math

import jax
import jax.numpy as jnp
import numpy as np
from jax import lax
from jax.experimental import pallas as pl
from jax.experimental.pallas import tpu as pltpu
from jax.sharding import PartitionSpec as P

SUBARRAYS = 4
LANES = 128
QUAD = 4
WIDE = 2
UNROLL_FB = True
LEAD = 2
LATE = 1
DRAIN = 3
PHASES = 4
VMEM_LIMIT = 32 * 2**20
MESH = pl.DeviceIdType.MESH


def dft_table(fine, lane_groups):
    index = np.arange(fine)
    angle = 2.0 * np.pi * (index[:, None] * index[None, :] % fine) / fine
    scale = 1.0 / math.sqrt(fine)
    cosine = np.cos(angle) * scale
    sine = np.sin(angle) * scale
    whole = np.stack([np.concatenate([cosine, sine]), np.concatenate([-sine, cosine])])
    halves = []
    for half in range(fine // LANES):
        k = half * LANES + (np.arange(LANES).reshape(-1, lane_groups).T).reshape(-1)
        halves.append(np.concatenate([whole[0][:, k].T, whole[1][:, k].T]))
    return jnp.asarray(np.stack(halves), jnp.bfloat16)


def unit_turn(turn):
    quarter = (turn + 8192) >> 14
    t = (turn - (quarter << 14)).astype(jnp.float32) * (2.0 * math.pi / 65536.0)
    u = t * t
    sine = t * (1.0 + u * (-1.0 / 6 + u * (1.0 / 120 + u * (-1.0 / 5040))))
    cosine = 1.0 + u * (-0.5 + u * (1.0 / 24 + u * (-1.0 / 720 + u * (1.0 / 40320))))
    odd = (quarter & 1) == 1
    c = jnp.where(odd, sine, cosine)
    s = jnp.where(odd, cosine, sine)
    c = jnp.where(((quarter + 1) & 2) == 2, -c, c)
    s = jnp.where((quarter & 2) == 2, -s, s)
    return c, s


def swap_index_with_lanes(tiles, block):
    lane = lax.broadcasted_iota(jnp.int32, tiles[0].shape, 1)
    bit = 1
    while bit < len(tiles):
        upper = (lane & (bit * block)) != 0
        swapped = list(tiles)
        for i in range(len(tiles)):
            if not i & bit:
                low, high = tiles[i], tiles[i | bit]
                swapped[i] = jnp.where(upper, pltpu.roll(high, bit * block, 1), low)
                swapped[i | bit] = jnp.where(upper, high, pltpu.roll(low, LANES - bit * block, 1))
        tiles = swapped
        bit *= 2
    return tiles


def kernel(
    sizes,
    amplitude,
    own_ref,
    taps_hbm,
    table_hbm,
    delays_hbm,
    station_hbm,
    beam_hbm,
    out_ref,
    volts,
    taps_ref,
    table,
    delay_in,
    station_in,
    beam_in,
    wide_taps,
    wide_int,
    member,
    steps,
    state,
    filtered,
    spectra,
    total_ref,
    turned,
    part,
    final,
    own_sem,
    small_sem,
    halo_send,
    halo_recv,
    send,
    recv,
    far_send,
    far_recv,
    keep_sem,
    *exchanged,
):
    n_chan, n_core, bits = sizes
    received, sent = exchanged[:bits], exchanged[bits:]
    chans, stations, samples = own_ref.shape[1:]
    tap_count, fine = taps_ref.shape
    beams = delay_in.shape[0]
    frames = final.shape[-2]
    halves = fine // LANES
    chunks = chans * halves
    lane_groups = LANES // stations
    hop = 3 * fine // 4
    groups = frames // PHASES
    quads = LANES // lane_groups // QUAD
    n_stn = 2**bits
    rows = 2 * beams // n_stn
    per = beams // n_stn
    width = frames * lane_groups
    tiles = QUAD * width // LANES
    halo = volts.shape[3] - samples
    stn, chan, core = (lax.axis_index(name) for name in ("stn", "chan", "beam"))

    def fetch(c):
        return pltpu.make_async_copy(
            own_ref.at[:, c], volts.at[:, c, :, pl.ds(0, samples)], own_sem.at[c]
        )

    small = [
        pltpu.make_async_copy(source, target, small_sem.at[i])
        for i, (source, target) in enumerate(
            (
                (taps_hbm, taps_ref),
                (delays_hbm, delay_in),
                (station_hbm, station_in),
                (beam_hbm, beam_in),
                (table_hbm, table),
            )
        )
    ]
    for copy in small:
        copy.start()
    for c in range(chans):
        fetch(c).start()

    own_bit = [(stn // 2 ** (bits - 1 - dim)) % 2 for dim in range(bits)]
    orders = (tuple(range(bits - 1, -1, -1)), tuple(range(bits)))

    def partner(dim):
        return (stn + (1 - 2 * own_bit[dim]) * 2 ** (bits - 1 - dim), chan, core)

    def far(dz, dc):
        return ((chan + dz) % n_chan, (core + dc) % n_core)

    offsets = [(dz, dc) for dz in range(n_chan) for dc in range(n_core)]
    barrier = pltpu.get_barrier_semaphore()
    peers = [partner(dim) for dim in range(bits)] + [(stn, *far(dz, dc)) for dz, dc in offsets[1:]]
    for peer in peers:
        pl.semaphore_signal(barrier, inc=1, device_id=peer, device_id_type=MESH)
    def halo_copy(c, ri):
        return pltpu.make_async_remote_copy(
            src_ref=own_ref.at[ri, c, :, pl.ds(0, halo)],
            dst_ref=volts.at[ri, c, :, pl.ds(samples, halo)],
            send_sem=halo_send.at[c, ri],
            recv_sem=halo_recv.at[c, ri],
            device_id=(stn, chan, core - 1),
            device_id_type=MESH,
        )

    def send_halo(c):
        for ri in range(2):
            halo_copy(c, ri).start()

    for copy in small:
        copy.wait()

    for phase in range(PHASES):
        shift = hop * phase % fine
        rolled = taps_ref[...]
        if shift:
            rolled = pltpu.roll(rolled, shift, 1)
        column = lax.broadcasted_iota(jnp.int32, (1, fine), 1)
        for u in range(tap_count + 1):
            late = rolled[u : u + 1] if u < tap_count else jnp.zeros((1, fine), jnp.float32)
            early = rolled[u - 1 : u] if u > 0 else jnp.zeros((1, fine), jnp.float32)
            row = jnp.where(column >= shift, late, early)
            wide_taps[phase, u] = jnp.broadcast_to(row, (16, fine)).astype(jnp.bfloat16)

    pl.semaphore_wait(barrier, len(peers))

    @pl.when(core > 0)
    def _():
        send_halo(0)

    @pl.when(core == n_core - 1)
    def _():
        volts[:, :, :, samples:] = jnp.zeros((2, chans, stations, halo), volts.dtype)

    def widened(value, count):
        wide_int[...] = jnp.zeros(wide_int.shape, jnp.int32)
        wide_int[0:count, 0:stations] = value
        full = wide_int[...]
        step = stations
        while step < LANES:
            full = full + pltpu.roll(full, step, 1)
            step *= 2
        return full[0:count]

    group_of_lane = lax.broadcasted_iota(jnp.int32, (1, LANES), 1) // stations
    station_row = widened(station_in[...], 1).astype(jnp.float32)
    square = (beams, beams)
    diagonal = lax.broadcasted_iota(jnp.int32, square, 0) == lax.broadcasted_iota(jnp.int32, square, 1)
    beam_row = jnp.broadcast_to(beam_in[...].astype(jnp.float32), square)
    beam_column = jnp.sum(jnp.where(diagonal, beam_row, 0.0), axis=1, keepdims=True)
    member[...] = jnp.where(beam_column == station_row, amplitude, 0.0)
    delay = widened(delay_in[...], beams)
    wide_int[...] = delay
    for i, stride in enumerate((lane_groups, QUAD * lane_groups)):
        c, s = unit_turn((delay * stride) & 65535)
        steps[i, 0] = c
        steps[i, 1] = -s

    def filter_channel(c):
        @pl.loop(0, 2)
        def _(ri):
            @pl.when(core < n_core - 1)
            def _():
                halo_copy(c, ri).wait_recv()

            @pl.when((core > 0) & (c + 1 < chans))
            def _():
                halo_copy(c + 1, ri).start()

            for half in range(halves):
                for phase in range(PHASES):
                    shift = hop * phase % fine
                    block0 = hop * phase // fine
                    first = 0 if shift < (half + 1) * LANES else 1
                    last = tap_count - 1 if shift <= half * LANES else tap_count
                    lanes = slice(half * LANES, (half + 1) * LANES)
                    taps = {
                        u: wide_taps[phase, u, :, lanes][None] for u in range(first, last + 1)
                    }
                    sums = [[None, None] for _ in range(groups)]
                    for block in range(block0 + first, block0 + last + 1 + 3 * (groups - 1)):
                        at = block * fine + half * LANES
                        value = volts[ri, c, :, at : at + LANES].reshape(stations // 16, 16, LANES)
                        for g in range(groups):
                            u = block - block0 - 3 * g
                            if first <= u <= last:
                                term = taps[u] * value
                                so_far = sums[g][u % 2]
                                sums[g][u % 2] = term if so_far is None else so_far + term
                    for g in range(groups):
                        f = PHASES * g + phase
                        filtered[
                            f * stations : (f + 1) * stations,
                            pl.ds(pl.multiple_of(ri * fine + half * LANES, LANES), LANES),
                        ] = (sums[g][0] + sums[g][1]).reshape(stations, LANES)

    def transform(half):
        count = LANES // lane_groups

        def one(fb):
            rhs = filtered[pl.ds(pl.multiple_of(fb * LANES, LANES), WIDE * LANES), :]
            result = lax.dot_general(
                table[half], rhs, (((1,), (1,)), ((), ())), preferred_element_type=jnp.float32
            )
            for ri in range(2):
                for sub in range(WIDE):
                    pieces = [
                        result[
                            (ri * lane_groups + j) * count : (ri * lane_groups + j + 1) * count,
                            sub * LANES : (sub + 1) * LANES,
                        ]
                        for j in range(lane_groups)
                    ]
                    for j, piece in enumerate(swap_index_with_lanes(pieces, stations)):
                        at = pl.multiple_of(((fb + sub) * lane_groups + j) * count, count)
                        spectra[half, ri, pl.ds(at, count), :] = piece

        if UNROLL_FB:
            for fb in range(0, frames // lane_groups, WIDE):
                one(fb)
        else:
            @pl.loop(0, frames // lane_groups // WIDE)
            def _(fb):
                one(fb * WIDE)

    def form_beams(chunk, c, half):
        count = LANES // lane_groups
        frequency = (chan * chans + c) * fine + half * LANES + group_of_lane
        cosine, sine = unit_turn((wide_int[...] * frequency) & 65535)
        state[0] = cosine * member[...]
        state[1] = -sine * member[...]
        lane = lax.broadcasted_iota(jnp.int32, (frames, LANES), 1) // stations
        out_lane = lax.broadcasted_iota(jnp.int32, (2 * beams, LANES), 1)

        def times(a, i):
            e_re, e_im = steps[i, 0], steps[i, 1]
            return (a[0] * e_re - a[1] * e_im, a[0] * e_im + a[1] * e_re)

        def stacked(top, bottom):
            both = [v.reshape(n_stn, per, LANES) for v in (top, bottom)]
            return jnp.stack(both, axis=1).reshape(2 * beams, LANES)

        def one(quad):
            first = weight = (state[0], state[1])
            outs = []
            for q in range(QUAD):
                if q:
                    weight = times(weight, 0)
                w_re, w_im = weight
                lhs = jnp.concatenate([stacked(w_re, w_im), stacked(-w_im, w_re)], axis=1)
                at = quad * QUAD + q
                x = [spectra.at[half, ri][pl.ds(at, frames, stride=count), :] for ri in range(2)]
                blocks = [
                    jnp.concatenate([jnp.where(lane == j, v, 0.0) for v in x], axis=1)
                    for j in range(lane_groups)
                ]
                if width < LANES:
                    blocks.append(jnp.zeros((LANES - width, 2 * LANES), jnp.float32))
                turn = q * width % LANES
                if turn:
                    blocks = [jnp.concatenate(blocks, axis=0)]
                    blocks = [blocks[0][LANES - turn :], blocks[0][: LANES - turn]]
                rhs = jnp.concatenate(blocks, axis=0)
                result = lax.dot_general(
                    lhs.astype(jnp.bfloat16),
                    rhs.astype(jnp.bfloat16),
                    (((1,), (1,)), ((), ())),
                    preferred_element_type=jnp.float32,
                )
                outs.append(result)
            following = times(first, 1)
            state[0] = following[0]
            state[1] = following[1]
            for t in range(tiles):
                value = None
                for q in range(QUAD):
                    start = q * width - t * LANES
                    if -width < start < LANES:
                        value = outs[q] if value is None else jnp.where(out_lane >= start, outs[q], value)
                value = value.astype(jnp.bfloat16)
                for d in range(n_stn):
                    place = [(d >> (bits - 1 - dim)) & 1 for dim in range(bits)]
                    part[(chunk, quad // (quads // 2), *place, quad % (quads // 2), t)] = value[
                        d * rows : (d + 1) * rows
                    ]

        for quad in range(quads):
            one(quad)
            if (quad + 1) % (quads // 2) == 0:
                hop_copy(chunk, quad // (quads // 2), 0).start()

    def region(order, stage, last):
        index = [slice(None)] * bits
        for dim in orders[order][:stage]:
            index[dim] = own_bit[dim]
        if stage < bits:
            index[orders[order][stage]] = last(orders[order][stage])
        return index

    def other(dim):
        return 1 - own_bit[dim]

    def with_received(chunk, order, stage, index):
        value = part[(chunk, order, *index)].astype(jnp.float32)
        for earlier in range(stage):
            kept = [dim for dim in range(bits) if dim not in orders[order][: earlier + 1]]
            piece = received[earlier][(chunk, order, *(index[dim] for dim in kept))]
            value = value + piece.astype(jnp.float32)
        return value

    def hop_copy(chunk, order, stage):
        if stage == 0:
            source = part.at[(chunk, order, *region(order, 0, other))]
        else:
            source = sent[stage - 1].at[chunk, order]
        return pltpu.make_async_remote_copy(
            src_ref=source,
            dst_ref=received[stage].at[chunk, order],
            send_sem=send.at[stage, chunk, order],
            recv_sem=recv.at[stage, chunk, order],
            device_id=partner(orders[order][stage]),
            device_id_type=MESH,
        )

    def place_of(chunk):
        c = chunk // halves
        lanes = pl.ds(pl.multiple_of((chunk % halves) * LANES, LANES), LANES)
        return out_ref.at[:, :, chan * chans + c, core, :, lanes]

    def deliver(chunk, number):
        z, k = far(*offsets[number])
        return pltpu.make_async_remote_copy(
            src_ref=final.at[chunk, z, k],
            dst_ref=place_of(chunk),
            send_sem=far_send.at[chunk, number],
            recv_sem=far_recv.at[chunk, number],
            device_id=(stn, z, k),
            device_id_type=MESH,
        )

    def keep(chunk):
        return pltpu.make_async_copy(final.at[chunk, chan, core], place_of(chunk), keep_sem.at[chunk])

    def finish(chunk):
        for order in range(2):
            value = with_received(chunk, order, bits, own_bit)
            for quad in range(quads // 2):
                at = (order * (quads // 2) + quad) * rows
                for t in range(tiles):
                    total_ref[t, at : at + rows, :] = value[quad, t]
        for t in range(tiles):
            turned[t * LANES : (t + 1) * LANES, :] = total_ref[t].T
        pieces = [turned[i * frames : (i + 1) * frames, :] for i in range(rows)]
        for row, piece in enumerate(swap_index_with_lanes(pieces, 1)):
            ri, b = divmod(row, per)
            device, at = divmod(b, per // (n_chan * n_core))
            z, k = divmod(device, n_core)
            final[chunk, z, k, at, ri] = piece.astype(jnp.bfloat16)

    def step(chunk, stage):
        for order in range(2):
            hop_copy(chunk, order, stage - 1).wait_recv()
            if stage < bits:
                sent[stage - 1][chunk, order] = with_received(
                    chunk, order, stage, region(order, stage, other)
                ).astype(jnp.bfloat16)
                hop_copy(chunk, order, stage).start()
        if stage == bits:
            finish(chunk)
            for number in range(len(offsets) - 1, 0, -1):
                deliver(chunk, number).start()
            keep(chunk).start()

    def drain(chunk):
        for order in range(2):
            for stage in range(bits):
                hop_copy(chunk, order, stage).wait_send()
        for number in range(1, len(offsets)):
            deliver(chunk, number).wait()
        keep(chunk).wait()

    @pl.loop(0, chunks + LEAD + bits + LATE + DRAIN)
    def _(tick):
        def during(chunk, action):
            @pl.when((chunk >= 0) & (chunk < chunks))
            def _():
                action(chunk)

        during(tick - LEAD, lambda chunk: form_beams(chunk, chunk // halves, chunk % halves))
        c = tick // halves

        @pl.when((tick >= 1) & (tick <= chunks))
        def _():
            transform((tick - 1) % halves)

        @pl.when((tick % halves == 0) & (c < chans))
        def _():
            fetch(c).wait()
            filter_channel(c)

        for stage in range(1, bits + 1):
            behind = stage + (LATE if stage == bits else 0)
            during(tick - LEAD - behind, lambda chunk, stage=stage: step(chunk, stage))
        during(tick - LEAD - LATE - bits - DRAIN, drain)

    @pl.when(core > 0)
    def _():
        for c in range(chans):
            for ri in range(2):
                halo_copy(c, ri).wait_send()


def body(volts, taps, delays, station_sub, beam_sub):
    own = jnp.transpose(volts, (0, 2, 1, 3))
    chans, stations, samples = own.shape[1:]
    tap_count, fine = taps.shape
    beams = delays.shape[0]
    n_stn, n_chan, n_core = (lax.axis_size(name) for name in ("stn", "chan", "beam"))
    bits = n_stn.bit_length() - 1
    hop = 3 * fine // 4
    frames = samples // hop
    per = beams // n_stn
    per_device = per // (n_chan * n_core)
    halves = fine // LANES
    chunks = chans * halves
    lane_groups = LANES // stations
    quads = LANES // lane_groups // QUAD
    tiles = QUAD * frames * lane_groups // LANES
    rows = 2 * per
    peers = n_chan * n_core
    assert n_stn == 2**bits and rows == QUAD * lane_groups and quads * rows == LANES
    assert QUAD * frames * lane_groups == tiles * LANES and frames * lane_groups <= LANES
    blocks = hop * (PHASES - 1) // fine + tap_count + 1 + 3 * (frames // PHASES - 1)
    amplitude = 1.0 / math.sqrt(stations * n_stn // SUBARRAYS)
    block = (quads // 2, tiles, rows, LANES)
    pieces = [
        pltpu.VMEM((chunks, 2) + (2,) * (bits - 1 - t) + block, jnp.bfloat16) for t in range(bits)
    ]
    hbm = pl.BlockSpec(memory_space=pltpu.HBM)
    dma = pltpu.SemaphoreType.DMA
    out = pl.pallas_call(
        functools.partial(kernel, (n_chan, n_core, bits), amplitude),
        out_shape=jax.ShapeDtypeStruct(
            (per_device, 2, n_chan * chans, n_core, frames, fine), jnp.bfloat16
        ),
        in_specs=[hbm] * 6,
        out_specs=pl.BlockSpec(memory_space=pl.ANY),
        scratch_shapes=[
            pltpu.VMEM((2, chans, stations, blocks * fine), jnp.bfloat16),
            pltpu.VMEM((tap_count, fine), jnp.float32),
            pltpu.VMEM((halves, 2 * LANES, 2 * fine), jnp.bfloat16),
            pltpu.VMEM((beams, stations), jnp.int32),
            pltpu.VMEM((1, stations), jnp.int32),
            pltpu.VMEM((1, beams), jnp.int32),
            pltpu.VMEM((PHASES, tap_count + 1, 16, fine), jnp.bfloat16),
            pltpu.VMEM((beams, LANES), jnp.int32),
            pltpu.VMEM((beams, LANES), jnp.float32),
            pltpu.VMEM((2, 2, beams, LANES), jnp.float32),
            pltpu.VMEM((2, beams, LANES), jnp.float32),
            pltpu.VMEM((frames * stations, 2 * fine), jnp.bfloat16),
            pltpu.VMEM((halves, 2, frames * LANES // lane_groups, LANES), jnp.float32),
            pltpu.VMEM((tiles, LANES, LANES), jnp.float32),
            pltpu.VMEM((tiles * LANES, LANES), jnp.float32),
            pltpu.VMEM((chunks, 2) + (2,) * bits + block, jnp.bfloat16),
            pltpu.VMEM((chunks, n_chan, n_core, per_device, 2, frames, LANES), jnp.bfloat16),
            dma((chans,)),
            dma((5,)),
            dma((chans, 2)),
            dma((chans, 2)),
            dma((bits, chunks, 2)),
            dma((bits, chunks, 2)),
            dma((chunks, peers)),
            dma((chunks, peers)),
            dma((chunks,)),
            *pieces,
            *pieces[1:],
        ],
        compiler_params=pltpu.CompilerParams(
            collective_id=0, has_side_effects=True, vmem_limit_bytes=VMEM_LIMIT
        ),
        name="channelize_and_beamform",
    )(
        *(
            pltpu.with_memory_space_constraint(x, pltpu.HBM)
            for x in (
                own,
                taps,
                dft_table(fine, lane_groups),
                delays,
                station_sub[None],
                beam_sub[None],
            )
        )
    )
    return out.reshape(per_device, 2, n_chan * chans, n_core * frames, fine).astype(jnp.float32)


def solution(mesh):
    placed = (P(None, "stn", "chan", "beam"), P(), P(None, "stn"), P("stn"), P())
    return jax.shard_map(
        body,
        mesh=mesh,
        in_specs=placed,
        out_specs=P(("stn", "chan", "beam"), None, None, None, None),
        check_vma=False,
    )
```

```python
import functools
import math

import jax
import jax.numpy as jnp
import numpy as np
from jax import lax
from jax.experimental import pallas as pl
from jax.experimental.pallas import tpu as pltpu
from jax.sharding import PartitionSpec as P

SUBARRAYS = 4
LANES = 128
QUAD = 4
WIDE = 2
UNROLL_FB = True
LEAD = 2
LATE = 1
PIECES = 2
PHASES = 4
VMEM_LIMIT = 32 * 2**20
MESH = pl.DeviceIdType.MESH


def dft_table(fine, lane_groups):
    index = np.arange(fine)
    angle = 2.0 * np.pi * (index[:, None] * index[None, :] % fine) / fine
    scale = 1.0 / math.sqrt(fine)
    cosine = np.cos(angle) * scale
    sine = np.sin(angle) * scale
    whole = np.stack([np.concatenate([cosine, sine]), np.concatenate([-sine, cosine])])
    halves = []
    for half in range(fine // LANES):
        k = half * LANES + (np.arange(LANES).reshape(-1, lane_groups).T).reshape(-1)
        halves.append(np.concatenate([whole[0][:, k].T, whole[1][:, k].T]))
    return jnp.asarray(np.stack(halves), jnp.bfloat16)


def unit_turn(turn):
    quarter = (turn + 8192) >> 14
    t = (turn - (quarter << 14)).astype(jnp.float32) * (2.0 * math.pi / 65536.0)
    u = t * t
    sine = t * (1.0 + u * (-1.0 / 6 + u * (1.0 / 120 + u * (-1.0 / 5040))))
    cosine = 1.0 + u * (-0.5 + u * (1.0 / 24 + u * (-1.0 / 720 + u * (1.0 / 40320))))
    odd = (quarter & 1) == 1
    c = jnp.where(odd, sine, cosine)
    s = jnp.where(odd, cosine, sine)
    c = jnp.where(((quarter + 1) & 2) == 2, -c, c)
    s = jnp.where((quarter & 2) == 2, -s, s)
    return c, s


def swap_index_with_lanes(tiles, block):
    lane = lax.broadcasted_iota(jnp.int32, tiles[0].shape, 1)
    bit = 1
    while bit < len(tiles):
        upper = (lane & (bit * block)) != 0
        swapped = list(tiles)
        for i in range(len(tiles)):
            if not i & bit:
                low, high = tiles[i], tiles[i | bit]
                swapped[i] = jnp.where(upper, pltpu.roll(high, bit * block, 1), low)
                swapped[i | bit] = jnp.where(upper, high, pltpu.roll(low, LANES - bit * block, 1))
        tiles = swapped
        bit *= 2
    return tiles


def kernel(
    sizes,
    amplitude,
    own_ref,
    taps_hbm,
    table_hbm,
    delays_hbm,
    station_hbm,
    beam_hbm,
    out_ref,
    volts,
    taps_ref,
    table,
    delay_in,
    station_in,
    beam_in,
    wide_taps,
    wide_int,
    member,
    steps,
    state,
    filtered,
    spectra,
    total_ref,
    turned,
    part,
    final,
    own_sem,
    small_sem,
    halo_send,
    halo_recv,
    send,
    recv,
    far_send,
    far_recv,
    *exchanged,
):
    n_chan, n_core, bits = sizes
    received, sent = exchanged[:bits], exchanged[bits:]
    chans, stations, samples = own_ref.shape[1:]
    tap_count, fine = taps_ref.shape
    beams = delay_in.shape[0]
    frames = final.shape[-2]
    halves = fine // LANES
    chunks = chans * halves
    lane_groups = LANES // stations
    hop = 3 * fine // 4
    groups = frames // PHASES
    quads = LANES // lane_groups // QUAD
    n_stn = 2**bits
    rows = 2 * beams // n_stn
    per = beams // n_stn
    width = frames * lane_groups
    tiles = QUAD * width // LANES
    halo = volts.shape[3] - samples
    stn, chan, core = (lax.axis_index(name) for name in ("stn", "chan", "beam"))

    def fetch(c):
        return pltpu.make_async_copy(
            own_ref.at[:, c], volts.at[:, c, :, pl.ds(0, samples)], own_sem.at[c]
        )

    small = [
        pltpu.make_async_copy(source, target, small_sem.at[i])
        for i, (source, target) in enumerate(
            (
                (taps_hbm, taps_ref),
                (delays_hbm, delay_in),
                (station_hbm, station_in),
                (beam_hbm, beam_in),
                (table_hbm, table),
            )
        )
    ]
    for copy in small:
        copy.start()
    for c in range(chans):
        fetch(c).start()

    own_bit = [(stn // 2 ** (bits - 1 - dim)) % 2 for dim in range(bits)]
    orders = (tuple(range(bits - 1, -1, -1)), tuple(range(bits)))

    def partner(dim):
        return (stn + (1 - 2 * own_bit[dim]) * 2 ** (bits - 1 - dim), chan, core)

    def far(dz, dc):
        return ((chan + dz) % n_chan, (core + dc) % n_core)

    offsets = [(dz, dc) for dz in range(n_chan) for dc in range(n_core)]
    barrier = pltpu.get_barrier_semaphore()
    peers = [partner(dim) for dim in range(bits)] + [(stn, *far(dz, dc)) for dz, dc in offsets[1:]]
    for peer in peers:
        pl.semaphore_signal(barrier, inc=1, device_id=peer, device_id_type=MESH)
    def halo_copy(c, ri):
        return pltpu.make_async_remote_copy(
            src_ref=own_ref.at[ri, c, :, pl.ds(0, halo)],
            dst_ref=volts.at[ri, c, :, pl.ds(samples, halo)],
            send_sem=halo_send.at[c, ri],
            recv_sem=halo_recv.at[c, ri],
            device_id=(stn, chan, core - 1),
            device_id_type=MESH,
        )

    def send_halo(c):
        for ri in range(2):
            halo_copy(c, ri).start()

    for copy in small:
        copy.wait()

    for phase in range(PHASES):
        shift = hop * phase % fine
        rolled = taps_ref[...]
        if shift:
            rolled = pltpu.roll(rolled, shift, 1)
        column = lax.broadcasted_iota(jnp.int32, (1, fine), 1)
        for u in range(tap_count + 1):
            late = rolled[u : u + 1] if u < tap_count else jnp.zeros((1, fine), jnp.float32)
            early = rolled[u - 1 : u] if u > 0 else jnp.zeros((1, fine), jnp.float32)
            row = jnp.where(column >= shift, late, early)
            wide_taps[phase, u] = jnp.broadcast_to(row, (16, fine)).astype(jnp.bfloat16)

    pl.semaphore_wait(barrier, len(peers))

    @pl.when(core > 0)
    def _():
        send_halo(0)

    @pl.when(core == n_core - 1)
    def _():
        volts[:, :, :, samples:] = jnp.zeros((2, chans, stations, halo), volts.dtype)

    def widened(value, count):
        wide_int[...] = jnp.zeros(wide_int.shape, jnp.int32)
        wide_int[0:count, 0:stations] = value
        full = wide_int[...]
        step = stations
        while step < LANES:
            full = full + pltpu.roll(full, step, 1)
            step *= 2
        return full[0:count]

    group_of_lane = lax.broadcasted_iota(jnp.int32, (1, LANES), 1) // stations
    station_row = widened(station_in[...], 1).astype(jnp.float32)
    square = (beams, beams)
    diagonal = lax.broadcasted_iota(jnp.int32, square, 0) == lax.broadcasted_iota(jnp.int32, square, 1)
    beam_row = jnp.broadcast_to(beam_in[...].astype(jnp.float32), square)
    beam_column = jnp.sum(jnp.where(diagonal, beam_row, 0.0), axis=1, keepdims=True)
    member[...] = jnp.where(beam_column == station_row, amplitude, 0.0)
    delay = widened(delay_in[...], beams)
    wide_int[...] = delay
    for i, stride in enumerate((lane_groups, QUAD * lane_groups)):
        c, s = unit_turn((delay * stride) & 65535)
        steps[i, 0] = c
        steps[i, 1] = -s

    def filter_channel(c):
        @pl.loop(0, 2)
        def _(ri):
            @pl.when(core < n_core - 1)
            def _():
                halo_copy(c, ri).wait_recv()

            @pl.when((core > 0) & (c + 1 < chans))
            def _():
                halo_copy(c + 1, ri).start()

            for half in range(halves):
                for phase in range(PHASES):
                    shift = hop * phase % fine
                    block0 = hop * phase // fine
                    first = 0 if shift < (half + 1) * LANES else 1
                    last = tap_count - 1 if shift <= half * LANES else tap_count
                    lanes = slice(half * LANES, (half + 1) * LANES)
                    taps = {
                        u: wide_taps[phase, u, :, lanes][None] for u in range(first, last + 1)
                    }
                    sums = [[None, None] for _ in range(groups)]
                    for block in range(block0 + first, block0 + last + 1 + 3 * (groups - 1)):
                        at = block * fine + half * LANES
                        value = volts[ri, c, :, at : at + LANES].reshape(stations // 16, 16, LANES)
                        for g in range(groups):
                            u = block - block0 - 3 * g
                            if first <= u <= last:
                                term = taps[u] * value
                                so_far = sums[g][u % 2]
                                sums[g][u % 2] = term if so_far is None else so_far + term
                    for g in range(groups):
                        f = PHASES * g + phase
                        filtered[
                            f * stations : (f + 1) * stations,
                            pl.ds(pl.multiple_of(ri * fine + half * LANES, LANES), LANES),
                        ] = (sums[g][0] + sums[g][1]).reshape(stations, LANES)

    def transform(half):
        count = LANES // lane_groups

        def one(fb):
            rhs = filtered[pl.ds(pl.multiple_of(fb * LANES, LANES), WIDE * LANES), :]
            result = lax.dot_general(
                table[half], rhs, (((1,), (1,)), ((), ())), preferred_element_type=jnp.float32
            )
            for ri in range(2):
                for sub in range(WIDE):
                    pieces = [
                        result[
                            (ri * lane_groups + j) * count : (ri * lane_groups + j + 1) * count,
                            sub * LANES : (sub + 1) * LANES,
                        ]
                        for j in range(lane_groups)
                    ]
                    for j, piece in enumerate(swap_index_with_lanes(pieces, stations)):
                        at = pl.multiple_of(((fb + sub) * lane_groups + j) * count, count)
                        spectra[half, ri, pl.ds(at, count), :] = piece

        if UNROLL_FB:
            for fb in range(0, frames // lane_groups, WIDE):
                one(fb)
        else:
            @pl.loop(0, frames // lane_groups // WIDE)
            def _(fb):
                one(fb * WIDE)

    def form_beams(chunk, c, half):
        count = LANES // lane_groups
        frequency = (chan * chans + c) * fine + half * LANES + group_of_lane
        cosine, sine = unit_turn((wide_int[...] * frequency) & 65535)
        state[0] = cosine * member[...]
        state[1] = -sine * member[...]
        lane = lax.broadcasted_iota(jnp.int32, (frames, LANES), 1) // stations
        out_lane = lax.broadcasted_iota(jnp.int32, (2 * beams, LANES), 1)

        def times(a, i):
            e_re, e_im = steps[i, 0], steps[i, 1]
            return (a[0] * e_re - a[1] * e_im, a[0] * e_im + a[1] * e_re)

        def stacked(top, bottom):
            both = [v.reshape(n_stn, per, LANES) for v in (top, bottom)]
            return jnp.stack(both, axis=1).reshape(2 * beams, LANES)

        def one(quad):
            first = weight = (state[0], state[1])
            outs = []
            for q in range(QUAD):
                if q:
                    weight = times(weight, 0)
                w_re, w_im = weight
                lhs = jnp.concatenate([stacked(w_re, w_im), stacked(-w_im, w_re)], axis=1)
                at = quad * QUAD + q
                x = [spectra.at[half, ri][pl.ds(at, frames, stride=count), :] for ri in range(2)]
                blocks = [
                    jnp.concatenate([jnp.where(lane == j, v, 0.0) for v in x], axis=1)
                    for j in range(lane_groups)
                ]
                if width < LANES:
                    blocks.append(jnp.zeros((LANES - width, 2 * LANES), jnp.float32))
                turn = q * width % LANES
                if turn:
                    blocks = [jnp.concatenate(blocks, axis=0)]
                    blocks = [blocks[0][LANES - turn :], blocks[0][: LANES - turn]]
                rhs = jnp.concatenate(blocks, axis=0)
                result = lax.dot_general(
                    lhs.astype(jnp.bfloat16),
                    rhs.astype(jnp.bfloat16),
                    (((1,), (1,)), ((), ())),
                    preferred_element_type=jnp.float32,
                )
                outs.append(result)
            following = times(first, 1)
            state[0] = following[0]
            state[1] = following[1]
            for t in range(tiles):
                value = None
                for q in range(QUAD):
                    start = q * width - t * LANES
                    if -width < start < LANES:
                        value = outs[q] if value is None else jnp.where(out_lane >= start, outs[q], value)
                value = value.astype(jnp.bfloat16)
                for d in range(n_stn):
                    place = [(d >> (bits - 1 - dim)) & 1 for dim in range(bits)]
                    part[(chunk, quad // (quads // PIECES), *place, quad % (quads // PIECES), t)] = value[
                        d * rows : (d + 1) * rows
                    ]

        for quad in range(quads):
            one(quad)
            if (quad + 1) % (quads // PIECES) == 0:
                hop_copy(chunk, quad // (quads // PIECES), 0).start()

    def region(order, stage, last):
        index = [slice(None)] * bits
        for dim in orders[order % 2][:stage]:
            index[dim] = own_bit[dim]
        if stage < bits:
            index[orders[order % 2][stage]] = last(orders[order % 2][stage])
        return index

    def other(dim):
        return 1 - own_bit[dim]

    def with_received(chunk, order, stage, index):
        value = part[(chunk, order, *index)].astype(jnp.float32)
        for earlier in range(stage):
            kept = [dim for dim in range(bits) if dim not in orders[order % 2][: earlier + 1]]
            piece = received[earlier][(chunk, order, *(index[dim] for dim in kept))]
            value = value + piece.astype(jnp.float32)
        return value

    def hop_copy(chunk, order, stage):
        if stage == 0:
            source = part.at[(chunk, order, *region(order, 0, other))]
        else:
            source = sent[stage - 1].at[chunk, order]
        return pltpu.make_async_remote_copy(
            src_ref=source,
            dst_ref=received[stage].at[chunk, order],
            send_sem=send.at[stage],
            recv_sem=recv.at[stage, chunk, order],
            device_id=partner(orders[order % 2][stage]),
            device_id_type=MESH,
        )

    def place_of(chunk):
        c = chunk // halves
        lanes = pl.ds(pl.multiple_of((chunk % halves) * LANES, LANES), LANES)
        return out_ref.at[:, :, chan * chans + c, core, :, lanes]

    def deliver(chunk, number):
        z, k = far(*offsets[number])
        return pltpu.make_async_remote_copy(
            src_ref=final.at[chunk, z, k],
            dst_ref=place_of(chunk),
            send_sem=far_send,
            recv_sem=far_recv,
            device_id=(stn, z, k),
            device_id_type=MESH,
        )

    def keep(chunk):
        return pltpu.make_async_copy(final.at[chunk, chan, core], place_of(chunk), far_recv)

    def finish(chunk):
        for order in range(PIECES):
            value = with_received(chunk, order, bits, own_bit)
            for quad in range(quads // PIECES):
                at = (order * (quads // PIECES) + quad) * rows
                for t in range(tiles):
                    total_ref[t, at : at + rows, :] = value[quad, t]
        for t in range(tiles):
            turned[t * LANES : (t + 1) * LANES, :] = total_ref[t].T
        pieces = [turned[i * frames : (i + 1) * frames, :] for i in range(rows)]
        for row, piece in enumerate(swap_index_with_lanes(pieces, 1)):
            ri, b = divmod(row, per)
            device, at = divmod(b, per // (n_chan * n_core))
            z, k = divmod(device, n_core)
            final[chunk, z, k, at, ri] = piece.astype(jnp.bfloat16)

    def step(chunk, stage):
        for order in range(PIECES):
            hop_copy(chunk, order, stage - 1).wait_recv()
            if stage < bits:
                sent[stage - 1][chunk, order] = with_received(
                    chunk, order, stage, region(order, stage, other)
                ).astype(jnp.bfloat16)
                hop_copy(chunk, order, stage).start()
        if stage == bits:
            finish(chunk)
            for number in range(len(offsets) - 1, 0, -1):
                deliver(chunk, number).start()
            keep(chunk).start()

    @pl.loop(0, chunks + LEAD + bits)
    def _(tick):
        def during(chunk, action):
            @pl.when((chunk >= 0) & (chunk < chunks))
            def _():
                action(chunk)

        during(tick - LEAD, lambda chunk: form_beams(chunk, chunk // halves, chunk % halves))
        c = tick // halves

        @pl.when((tick >= 1) & (tick <= chunks))
        def _():
            transform((tick - 1) % halves)

        @pl.when((tick % halves == 0) & (c < chans))
        def _():
            fetch(c).wait()
            filter_channel(c)

        for stage in range(1, bits):
            during(tick - LEAD - stage, lambda chunk, stage=stage: step(chunk, stage))

        def summed(tick):
            caught_up = jnp.where(tick >= LEAD + chunks - 1, LATE, 0)
            return jnp.clip(tick - LEAD - bits - LATE + 1 + caught_up, 0, chunks)

        @pl.loop(summed(tick - 1), summed(tick))
        def _(chunk):
            step(chunk, bits)


    @pl.when(core > 0)
    def _():
        for c in range(chans):
            for ri in range(2):
                halo_copy(c, ri).wait_send()

    def all_of(ref, send_sem, recv_sem):
        return pltpu.make_async_remote_copy(
            src_ref=ref,
            dst_ref=ref,
            send_sem=send_sem,
            recv_sem=recv_sem,
            device_id=partner(0),
            device_id_type=MESH,
        )

    for stage in range(bits):
        all_of(received[stage], send.at[stage], far_recv).wait_send()
    if n_chan > 1:
        all_of(final.at[:, 0 : n_chan - 1], far_send, far_recv).wait_send()
    if n_core > 1:
        all_of(final.at[:, 0, 0 : n_core - 1], far_send, far_recv).wait_send()
    all_of(out_ref, far_send, far_recv).wait_recv()


def body(volts, taps, delays, station_sub, beam_sub):
    own = jnp.transpose(volts, (0, 2, 1, 3))
    chans, stations, samples = own.shape[1:]
    tap_count, fine = taps.shape
    beams = delays.shape[0]
    n_stn, n_chan, n_core = (lax.axis_size(name) for name in ("stn", "chan", "beam"))
    bits = n_stn.bit_length() - 1
    hop = 3 * fine // 4
    frames = samples // hop
    per = beams // n_stn
    per_device = per // (n_chan * n_core)
    halves = fine // LANES
    chunks = chans * halves
    lane_groups = LANES // stations
    quads = LANES // lane_groups // QUAD
    tiles = QUAD * frames * lane_groups // LANES
    rows = 2 * per
    assert n_stn == 2**bits and rows == QUAD * lane_groups and quads * rows == LANES
    assert QUAD * frames * lane_groups == tiles * LANES and frames * lane_groups <= LANES
    blocks = hop * (PHASES - 1) // fine + tap_count + 1 + 3 * (frames // PHASES - 1)
    amplitude = 1.0 / math.sqrt(stations * n_stn // SUBARRAYS)
    block = (quads // PIECES, tiles, rows, LANES)
    pieces = [
        pltpu.VMEM((chunks, PIECES) + (2,) * (bits - 1 - t) + block, jnp.bfloat16) for t in range(bits)
    ]
    hbm = pl.BlockSpec(memory_space=pltpu.HBM)
    dma = pltpu.SemaphoreType.DMA
    out = pl.pallas_call(
        functools.partial(kernel, (n_chan, n_core, bits), amplitude),
        out_shape=jax.ShapeDtypeStruct(
            (per_device, 2, n_chan * chans, n_core, frames, fine), jnp.bfloat16
        ),
        in_specs=[hbm] * 6,
        out_specs=pl.BlockSpec(memory_space=pl.ANY),
        scratch_shapes=[
            pltpu.VMEM((2, chans, stations, blocks * fine), jnp.bfloat16),
            pltpu.VMEM((tap_count, fine), jnp.float32),
            pltpu.VMEM((halves, 2 * LANES, 2 * fine), jnp.bfloat16),
            pltpu.VMEM((beams, stations), jnp.int32),
            pltpu.VMEM((1, stations), jnp.int32),
            pltpu.VMEM((1, beams), jnp.int32),
            pltpu.VMEM((PHASES, tap_count + 1, 16, fine), jnp.bfloat16),
            pltpu.VMEM((beams, LANES), jnp.int32),
            pltpu.VMEM((beams, LANES), jnp.float32),
            pltpu.VMEM((2, 2, beams, LANES), jnp.float32),
            pltpu.VMEM((2, beams, LANES), jnp.float32),
            pltpu.VMEM((frames * stations, 2 * fine), jnp.bfloat16),
            pltpu.VMEM((halves, 2, frames * LANES // lane_groups, LANES), jnp.float32),
            pltpu.VMEM((tiles, LANES, LANES), jnp.float32),
            pltpu.VMEM((tiles * LANES, LANES), jnp.float32),
            pltpu.VMEM((chunks, PIECES) + (2,) * bits + block, jnp.bfloat16),
            pltpu.VMEM((chunks, n_chan, n_core, per_device, 2, frames, LANES), jnp.bfloat16),
            dma((chans,)),
            dma((5,)),
            dma((chans, 2)),
            dma((chans, 2)),
            dma((bits,)),
            dma((bits, chunks, PIECES)),
            dma,
            dma,
            *pieces,
            *pieces[1:],
        ],
        compiler_params=pltpu.CompilerParams(
            collective_id=0, has_side_effects=True, vmem_limit_bytes=VMEM_LIMIT
        ),
        name="channelize_and_beamform",
    )(
        *(
            pltpu.with_memory_space_constraint(x, pltpu.HBM)
            for x in (
                own,
                taps,
                dft_table(fine, lane_groups),
                delays,
                station_sub[None],
                beam_sub[None],
            )
        )
    )
    return out.reshape(per_device, 2, n_chan * chans, n_core * frames, fine).astype(jnp.float32)


def solution(mesh):
    placed = (P(None, "stn", "chan", "beam"), P(), P(None, "stn"), P("stn"), P())
    return jax.shard_map(
        body,
        mesh=mesh,
        in_specs=placed,
        out_specs=P(("stn", "chan", "beam"), None, None, None, None),
        check_vma=False,
    )
```

```python
import functools
import math

import jax
import jax.numpy as jnp
import numpy as np
from jax import lax
from jax.experimental import pallas as pl
from jax.experimental.pallas import tpu as pltpu
from jax.sharding import PartitionSpec as P

SUBARRAYS = 4
LANES = 128
QUAD = 4
WIDE = 2
UNROLL_FB = True
LEAD = 2
LATE = 1
PIECES = 2
PHASES = 4
VMEM_LIMIT = 32 * 2**20
MESH = pl.DeviceIdType.MESH


def dft_table(fine, lane_groups):
    index = np.arange(fine)
    angle = 2.0 * np.pi * (index[:, None] * index[None, :] % fine) / fine
    scale = 1.0 / math.sqrt(fine)
    cosine = np.cos(angle) * scale
    sine = np.sin(angle) * scale
    whole = np.stack([np.concatenate([cosine, sine]), np.concatenate([-sine, cosine])])
    halves = []
    for half in range(fine // LANES):
        k = half * LANES + (np.arange(LANES).reshape(-1, lane_groups).T).reshape(-1)
        halves.append(np.concatenate([whole[0][:, k].T, whole[1][:, k].T]))
    return jnp.asarray(np.stack(halves), jnp.bfloat16)


def unit_turn(turn):
    quarter = (turn + 8192) >> 14
    t = (turn - (quarter << 14)).astype(jnp.float32) * (2.0 * math.pi / 65536.0)
    u = t * t
    sine = t * (1.0 + u * (-1.0 / 6 + u * (1.0 / 120 + u * (-1.0 / 5040))))
    cosine = 1.0 + u * (-0.5 + u * (1.0 / 24 + u * (-1.0 / 720 + u * (1.0 / 40320))))
    odd = (quarter & 1) == 1
    c = jnp.where(odd, sine, cosine)
    s = jnp.where(odd, cosine, sine)
    c = jnp.where(((quarter + 1) & 2) == 2, -c, c)
    s = jnp.where((quarter & 2) == 2, -s, s)
    return c, s


def swap_index_with_lanes(tiles, block):
    lane = lax.broadcasted_iota(jnp.int32, tiles[0].shape, 1)
    bit = 1
    while bit < len(tiles):
        upper = (lane & (bit * block)) != 0
        swapped = list(tiles)
        for i in range(len(tiles)):
            if not i & bit:
                low, high = tiles[i], tiles[i | bit]
                swapped[i] = jnp.where(upper, pltpu.roll(high, bit * block, 1), low)
                swapped[i | bit] = jnp.where(upper, high, pltpu.roll(low, LANES - bit * block, 1))
        tiles = swapped
        bit *= 2
    return tiles


def kernel(
    sizes,
    amplitude,
    own_ref,
    taps_hbm,
    table_hbm,
    delays_hbm,
    station_hbm,
    beam_hbm,
    out_ref,
    volts,
    taps_ref,
    table,
    delay_in,
    station_in,
    beam_in,
    wide_taps,
    wide_int,
    member,
    steps,
    state,
    filtered,
    spectra,
    total_ref,
    turned,
    part,
    final,
    own_sem,
    small_sem,
    halo_send,
    halo_recv,
    send,
    recv,
    far_send,
    far_recv,
    *exchanged,
):
    n_chan, n_core, bits = sizes
    received, sent = exchanged[:bits], exchanged[bits:]
    chans, stations, samples = own_ref.shape[1:]
    tap_count, fine = taps_ref.shape
    beams = delay_in.shape[0]
    frames = final.shape[-2]
    halves = fine // LANES
    chunks = chans * halves
    lane_groups = LANES // stations
    hop = 3 * fine // 4
    groups = frames // PHASES
    quads = LANES // lane_groups // QUAD
    n_stn = 2**bits
    rows = 2 * beams // n_stn
    per = beams // n_stn
    width = frames * lane_groups
    tiles = QUAD * width // LANES
    halo = volts.shape[3] - samples
    stn, chan, core = (lax.axis_index(name) for name in ("stn", "chan", "beam"))

    def fetch(c):
        return pltpu.make_async_copy(
            own_ref.at[:, c], volts.at[:, c, :, pl.ds(0, samples)], own_sem.at[c]
        )

    small = [
        pltpu.make_async_copy(source, target, small_sem.at[i])
        for i, (source, target) in enumerate(
            (
                (taps_hbm, taps_ref),
                (delays_hbm, delay_in),
                (station_hbm, station_in),
                (beam_hbm, beam_in),
                (table_hbm, table),
            )
        )
    ]
    own_bit = [(stn // 2 ** (bits - 1 - dim)) % 2 for dim in range(bits)]
    orders = (tuple(range(bits - 1, -1, -1)), tuple(range(bits)))

    def partner(dim):
        return (stn + (1 - 2 * own_bit[dim]) * 2 ** (bits - 1 - dim), chan, core)

    def far(dz, dc):
        return ((chan + dz) % n_chan, (core + dc) % n_core)

    offsets = [(dz, dc) for dz in range(n_chan) for dc in range(n_core)]
    barrier = pltpu.get_barrier_semaphore()
    peers = [partner(dim) for dim in range(bits)] + [(stn, *far(dz, dc)) for dz, dc in offsets[1:]]
    for peer in peers:
        pl.semaphore_signal(barrier, inc=1, device_id=peer, device_id_type=MESH)
    small[0].start()
    fetch(0).start()
    for copy in small[1:]:
        copy.start()
    for c in range(1, chans):
        fetch(c).start()

    def halo_copy(c, ri):
        return pltpu.make_async_remote_copy(
            src_ref=own_ref.at[ri, c, :, pl.ds(0, halo)],
            dst_ref=volts.at[ri, c, :, pl.ds(samples, halo)],
            send_sem=halo_send.at[c, ri],
            recv_sem=halo_recv.at[c, ri],
            device_id=(stn, chan, core - 1),
            device_id_type=MESH,
        )

    def send_halo(c):
        for ri in range(2):
            halo_copy(c, ri).start()

    small[0].wait()

    pl.semaphore_wait(barrier, len(peers))

    @pl.when(core > 0)
    def _():
        send_halo(0)

    @pl.when(core == n_core - 1)
    def _():
        volts[:, :, :, samples:] = jnp.zeros((2, chans, stations, halo), volts.dtype)

    for phase in range(PHASES):
        shift = hop * phase % fine
        rolled = taps_ref[...]
        if shift:
            rolled = pltpu.roll(rolled, shift, 1)
        column = lax.broadcasted_iota(jnp.int32, (1, fine), 1)
        for u in range(tap_count + 1):
            late = rolled[u : u + 1] if u < tap_count else jnp.zeros((1, fine), jnp.float32)
            early = rolled[u - 1 : u] if u > 0 else jnp.zeros((1, fine), jnp.float32)
            row = jnp.where(column >= shift, late, early)
            wide_taps[phase, u] = jnp.broadcast_to(row, (16, fine)).astype(jnp.bfloat16)

    for copy in small[1:]:
        copy.wait()

    def widened(value, count):
        wide_int[...] = jnp.zeros(wide_int.shape, jnp.int32)
        wide_int[0:count, 0:stations] = value
        full = wide_int[...]
        step = stations
        while step < LANES:
            full = full + pltpu.roll(full, step, 1)
            step *= 2
        return full[0:count]

    group_of_lane = lax.broadcasted_iota(jnp.int32, (1, LANES), 1) // stations
    station_row = widened(station_in[...], 1).astype(jnp.float32)
    square = (beams, beams)
    diagonal = lax.broadcasted_iota(jnp.int32, square, 0) == lax.broadcasted_iota(jnp.int32, square, 1)
    beam_row = jnp.broadcast_to(beam_in[...].astype(jnp.float32), square)
    beam_column = jnp.sum(jnp.where(diagonal, beam_row, 0.0), axis=1, keepdims=True)
    member[...] = jnp.where(beam_column == station_row, amplitude, 0.0)
    delay = widened(delay_in[...], beams)
    wide_int[...] = delay
    for i, stride in enumerate((lane_groups, QUAD * lane_groups)):
        c, s = unit_turn((delay * stride) & 65535)
        steps[i, 0] = c
        steps[i, 1] = -s

    def filter_channel(c, first_part, last_part):
        @pl.loop(first_part, last_part)
        def _(ri):
            @pl.when(ri == 0)
            def _():
                fetch(c).wait()

            @pl.when(core < n_core - 1)
            def _():
                halo_copy(c, ri).wait_recv()

            @pl.when((core > 0) & (c + 1 < chans))
            def _():
                halo_copy(c + 1, ri).start()

            for half in range(halves):
                for phase in range(PHASES):
                    shift = hop * phase % fine
                    block0 = hop * phase // fine
                    first = 0 if shift < (half + 1) * LANES else 1
                    last = tap_count - 1 if shift <= half * LANES else tap_count
                    lanes = slice(half * LANES, (half + 1) * LANES)
                    taps = {
                        u: wide_taps[phase, u, :, lanes][None] for u in range(first, last + 1)
                    }
                    sums = [[None, None] for _ in range(groups)]
                    for block in range(block0 + first, block0 + last + 1 + 3 * (groups - 1)):
                        at = block * fine + half * LANES
                        value = volts[ri, c, :, at : at + LANES].reshape(stations // 16, 16, LANES)
                        for g in range(groups):
                            u = block - block0 - 3 * g
                            if first <= u <= last:
                                term = taps[u] * value
                                so_far = sums[g][u % 2]
                                sums[g][u % 2] = term if so_far is None else so_far + term
                    for g in range(groups):
                        f = PHASES * g + phase
                        filtered[
                            c % 2,
                            f * stations : (f + 1) * stations,
                            pl.ds(pl.multiple_of(ri * fine + half * LANES, LANES), LANES),
                        ] = (sums[g][0] + sums[g][1]).reshape(stations, LANES)

    def transform(chunk):
        half = chunk % halves
        slot = chunk // halves % 2
        count = LANES // lane_groups

        def one(fb):
            rhs = filtered[slot, pl.ds(pl.multiple_of(fb * LANES, LANES), WIDE * LANES), :]
            result = lax.dot_general(
                table[half], rhs, (((1,), (1,)), ((), ())), preferred_element_type=jnp.float32
            )
            for ri in range(2):
                for sub in range(WIDE):
                    pieces = [
                        result[
                            (ri * lane_groups + j) * count : (ri * lane_groups + j + 1) * count,
                            sub * LANES : (sub + 1) * LANES,
                        ]
                        for j in range(lane_groups)
                    ]
                    for j, piece in enumerate(swap_index_with_lanes(pieces, stations)):
                        at = pl.multiple_of(((fb + sub) * lane_groups + j) * count, count)
                        spectra[half, ri, pl.ds(at, count), :] = piece

        if UNROLL_FB:
            for fb in range(0, frames // lane_groups, WIDE):
                one(fb)
        else:
            @pl.loop(0, frames // lane_groups // WIDE)
            def _(fb):
                one(fb * WIDE)

    def form_beams(chunk, c, half):
        count = LANES // lane_groups
        frequency = (chan * chans + c) * fine + half * LANES + group_of_lane
        cosine, sine = unit_turn((wide_int[...] * frequency) & 65535)
        state[0] = cosine * member[...]
        state[1] = -sine * member[...]
        lane = lax.broadcasted_iota(jnp.int32, (frames, LANES), 1) // stations
        out_lane = lax.broadcasted_iota(jnp.int32, (2 * beams, LANES), 1)

        def times(a, i):
            e_re, e_im = steps[i, 0], steps[i, 1]
            return (a[0] * e_re - a[1] * e_im, a[0] * e_im + a[1] * e_re)

        def stacked(top, bottom):
            both = [v.reshape(n_stn, per, LANES) for v in (top, bottom)]
            return jnp.stack(both, axis=1).reshape(2 * beams, LANES)

        def one(quad):
            first = weight = (state[0], state[1])
            outs = []
            for q in range(QUAD):
                if q:
                    weight = times(weight, 0)
                w_re, w_im = weight
                lhs = jnp.concatenate([stacked(w_re, w_im), stacked(-w_im, w_re)], axis=1)
                at = quad * QUAD + q
                x = [spectra.at[half, ri][pl.ds(at, frames, stride=count), :] for ri in range(2)]
                blocks = [
                    jnp.concatenate([jnp.where(lane == j, v, 0.0) for v in x], axis=1)
                    for j in range(lane_groups)
                ]
                if width < LANES:
                    blocks.append(jnp.zeros((LANES - width, 2 * LANES), jnp.float32))
                turn = q * width % LANES
                if turn:
                    blocks = [jnp.concatenate(blocks, axis=0)]
                    blocks = [blocks[0][LANES - turn :], blocks[0][: LANES - turn]]
                rhs = jnp.concatenate(blocks, axis=0)
                result = lax.dot_general(
                    lhs.astype(jnp.bfloat16),
                    rhs.astype(jnp.bfloat16),
                    (((1,), (1,)), ((), ())),
                    preferred_element_type=jnp.float32,
                )
                outs.append(result)
            following = times(first, 1)
            state[0] = following[0]
            state[1] = following[1]
            for t in range(tiles):
                value = None
                for q in range(QUAD):
                    start = q * width - t * LANES
                    if -width < start < LANES:
                        value = outs[q] if value is None else jnp.where(out_lane >= start, outs[q], value)
                value = value.astype(jnp.bfloat16)
                for d in range(n_stn):
                    place = [(d >> (bits - 1 - dim)) & 1 for dim in range(bits)]
                    part[(chunk, quad // (quads // PIECES), *place, quad % (quads // PIECES), t)] = value[
                        d * rows : (d + 1) * rows
                    ]

        for quad in range(quads):
            one(quad)
            if (quad + 1) % (quads // PIECES) == 0:
                hop_copy(chunk, quad // (quads // PIECES), 0).start()

    def region(order, stage, last):
        index = [slice(None)] * bits
        for dim in orders[order % 2][:stage]:
            index[dim] = own_bit[dim]
        if stage < bits:
            index[orders[order % 2][stage]] = last(orders[order % 2][stage])
        return index

    def other(dim):
        return 1 - own_bit[dim]

    def with_received(chunk, order, stage, index):
        value = part[(chunk, order, *index)].astype(jnp.float32)
        for earlier in range(stage):
            kept = [dim for dim in range(bits) if dim not in orders[order % 2][: earlier + 1]]
            piece = received[earlier][(chunk, order, *(index[dim] for dim in kept))]
            value = value + piece.astype(jnp.float32)
        return value

    def hop_copy(chunk, order, stage):
        if stage == 0:
            source = part.at[(chunk, order, *region(order, 0, other))]
        else:
            source = sent[stage - 1].at[chunk, order]
        return pltpu.make_async_remote_copy(
            src_ref=source,
            dst_ref=received[stage].at[chunk, order],
            send_sem=send.at[stage],
            recv_sem=recv.at[stage, chunk, order],
            device_id=partner(orders[order % 2][stage]),
            device_id_type=MESH,
        )

    def place_of(chunk):
        c = chunk // halves
        lanes = pl.ds(pl.multiple_of((chunk % halves) * LANES, LANES), LANES)
        return out_ref.at[:, :, chan * chans + c, core, :, lanes]

    def deliver(chunk, number):
        z, k = far(*offsets[number])
        return pltpu.make_async_remote_copy(
            src_ref=final.at[chunk, z, k],
            dst_ref=place_of(chunk),
            send_sem=far_send,
            recv_sem=far_recv,
            device_id=(stn, z, k),
            device_id_type=MESH,
        )

    def keep(chunk):
        return pltpu.make_async_copy(final.at[chunk, chan, core], place_of(chunk), far_recv)

    def finish(chunk):
        for order in range(PIECES):
            value = with_received(chunk, order, bits, own_bit)
            for quad in range(quads // PIECES):
                at = (order * (quads // PIECES) + quad) * rows
                for t in range(tiles):
                    total_ref[t, at : at + rows, :] = value[quad, t]
        for t in range(tiles):
            turned[t * LANES : (t + 1) * LANES, :] = total_ref[t].T
        pieces = [turned[i * frames : (i + 1) * frames, :] for i in range(rows)]
        for row, piece in enumerate(swap_index_with_lanes(pieces, 1)):
            ri, b = divmod(row, per)
            device, at = divmod(b, per // (n_chan * n_core))
            z, k = divmod(device, n_core)
            final[chunk, z, k, at, ri] = piece.astype(jnp.bfloat16)

    def step(chunk, stage):
        for order in range(PIECES):
            hop_copy(chunk, order, stage - 1).wait_recv()
            if stage < bits:
                sent[stage - 1][chunk, order] = with_received(
                    chunk, order, stage, region(order, stage, other)
                ).astype(jnp.bfloat16)
                hop_copy(chunk, order, stage).start()
        if stage == bits:
            finish(chunk)
            for number in range(len(offsets) - 1, 0, -1):
                deliver(chunk, number).start()
            keep(chunk).start()

    @pl.loop(0, chunks + LEAD + bits)
    def _(tick):
        def during(chunk, action):
            @pl.when((chunk >= 0) & (chunk < chunks))
            def _():
                action(chunk)

        during(tick - LEAD, lambda chunk: form_beams(chunk, chunk // halves, chunk % halves))
        c = tick // halves

        @pl.when((c < chans) & (tick != 1))
        def _():
            filter_channel(c, tick % 2, jnp.where(tick == 0, 2, tick % 2 + 1))

        @pl.when((tick >= 1) & (tick <= chunks))
        def _():
            transform(tick - 1)

        for stage in range(1, bits):
            during(tick - LEAD - stage, lambda chunk, stage=stage: step(chunk, stage))

        def summed(tick):
            caught_up = jnp.where(tick >= LEAD + chunks - 1, LATE, 0)
            return jnp.clip(tick - LEAD - bits - LATE + 1 + caught_up, 0, chunks)

        @pl.loop(summed(tick - 1), summed(tick))
        def _(chunk):
            step(chunk, bits)


    @pl.when(core > 0)
    def _():
        for c in range(chans):
            for ri in range(2):
                halo_copy(c, ri).wait_send()

    def all_of(ref, send_sem, recv_sem):
        return pltpu.make_async_remote_copy(
            src_ref=ref,
            dst_ref=ref,
            send_sem=send_sem,
            recv_sem=recv_sem,
            device_id=partner(0),
            device_id_type=MESH,
        )

    for stage in range(bits):
        all_of(received[stage], send.at[stage], far_recv).wait_send()
    if n_chan > 1:
        all_of(final.at[:, 0 : n_chan - 1], far_send, far_recv).wait_send()
    if n_core > 1:
        all_of(final.at[:, 0, 0 : n_core - 1], far_send, far_recv).wait_send()
    all_of(out_ref, far_send, far_recv).wait_recv()


def body(volts, taps, delays, station_sub, beam_sub):
    own = jnp.transpose(volts, (0, 2, 1, 3))
    chans, stations, samples = own.shape[1:]
    tap_count, fine = taps.shape
    beams = delays.shape[0]
    n_stn, n_chan, n_core = (lax.axis_size(name) for name in ("stn", "chan", "beam"))
    bits = n_stn.bit_length() - 1
    hop = 3 * fine // 4
    frames = samples // hop
    per = beams // n_stn
    per_device = per // (n_chan * n_core)
    halves = fine // LANES
    chunks = chans * halves
    lane_groups = LANES // stations
    quads = LANES // lane_groups // QUAD
    tiles = QUAD * frames * lane_groups // LANES
    rows = 2 * per
    assert halves == 2 and n_stn == 2**bits and rows == QUAD * lane_groups and quads * rows == LANES
    assert QUAD * frames * lane_groups == tiles * LANES and frames * lane_groups <= LANES
    blocks = hop * (PHASES - 1) // fine + tap_count + 1 + 3 * (frames // PHASES - 1)
    amplitude = 1.0 / math.sqrt(stations * n_stn // SUBARRAYS)
    block = (quads // PIECES, tiles, rows, LANES)
    pieces = [
        pltpu.VMEM((chunks, PIECES) + (2,) * (bits - 1 - t) + block, jnp.bfloat16) for t in range(bits)
    ]
    hbm = pl.BlockSpec(memory_space=pltpu.HBM)
    dma = pltpu.SemaphoreType.DMA
    out = pl.pallas_call(
        functools.partial(kernel, (n_chan, n_core, bits), amplitude),
        out_shape=jax.ShapeDtypeStruct(
            (per_device, 2, n_chan * chans, n_core, frames, fine), jnp.bfloat16
        ),
        in_specs=[hbm] * 6,
        out_specs=pl.BlockSpec(memory_space=pl.ANY),
        scratch_shapes=[
            pltpu.VMEM((2, chans, stations, blocks * fine), jnp.bfloat16),
            pltpu.VMEM((tap_count, fine), jnp.float32),
            pltpu.VMEM((halves, 2 * LANES, 2 * fine), jnp.bfloat16),
            pltpu.VMEM((beams, stations), jnp.int32),
            pltpu.VMEM((1, stations), jnp.int32),
            pltpu.VMEM((1, beams), jnp.int32),
            pltpu.VMEM((PHASES, tap_count + 1, 16, fine), jnp.bfloat16),
            pltpu.VMEM((beams, LANES), jnp.int32),
            pltpu.VMEM((beams, LANES), jnp.float32),
            pltpu.VMEM((2, 2, beams, LANES), jnp.float32),
            pltpu.VMEM((2, beams, LANES), jnp.float32),
            pltpu.VMEM((2, frames * stations, 2 * fine), jnp.bfloat16),
            pltpu.VMEM((halves, 2, frames * LANES // lane_groups, LANES), jnp.float32),
            pltpu.VMEM((tiles, LANES, LANES), jnp.float32),
            pltpu.VMEM((tiles * LANES, LANES), jnp.float32),
            pltpu.VMEM((chunks, PIECES) + (2,) * bits + block, jnp.bfloat16),
            pltpu.VMEM((chunks, n_chan, n_core, per_device, 2, frames, LANES), jnp.bfloat16),
            dma((chans,)),
            dma((5,)),
            dma((chans, 2)),
            dma((chans, 2)),
            dma((bits,)),
            dma((bits, chunks, PIECES)),
            dma,
            dma,
            *pieces,
            *pieces[1:],
        ],
        compiler_params=pltpu.CompilerParams(
            collective_id=0, has_side_effects=True, vmem_limit_bytes=VMEM_LIMIT
        ),
        name="channelize_and_beamform",
    )(
        *(
            pltpu.with_memory_space_constraint(x, pltpu.HBM)
            for x in (
                own,
                taps,
                dft_table(fine, lane_groups),
                delays,
                station_sub[None],
                beam_sub[None],
            )
        )
    )
    return out.reshape(per_device, 2, n_chan * chans, n_core * frames, fine).astype(jnp.float32)


def solution(mesh):
    placed = (P(None, "stn", "chan", "beam"), P(), P(None, "stn"), P("stn"), P())
    return jax.shard_map(
        body,
        mesh=mesh,
        in_specs=placed,
        out_specs=P(("stn", "chan", "beam"), None, None, None, None),
        check_vma=False,
    )
```

```python
import functools
import math

import jax
import jax.numpy as jnp
import numpy as np
from jax import lax
from jax.experimental import pallas as pl
from jax.experimental.pallas import tpu as pltpu
from jax.sharding import PartitionSpec as P

SUBARRAYS = 4
LANES = 128
QUAD = 4
WIDE = 2
UNROLL_FB = True
LEAD = 2
LATE = 1
PIECES = 2
PHASES = 4
VMEM_LIMIT = 32 * 2**20
MESH = pl.DeviceIdType.MESH


def dft_table(fine, lane_groups):
    index = np.arange(fine)
    angle = 2.0 * np.pi * (index[:, None] * index[None, :] % fine) / fine
    scale = 1.0 / math.sqrt(fine)
    cosine = np.cos(angle) * scale
    sine = np.sin(angle) * scale
    whole = np.stack([np.concatenate([cosine, sine]), np.concatenate([-sine, cosine])])
    halves = []
    for half in range(fine // LANES):
        k = half * LANES + (np.arange(LANES).reshape(-1, lane_groups).T).reshape(-1)
        halves.append(np.concatenate([whole[0][:, k].T, whole[1][:, k].T]))
    return jnp.asarray(np.stack(halves), jnp.bfloat16)


def unit_turn(turn):
    quarter = (turn + 8192) >> 14
    t = (turn - (quarter << 14)).astype(jnp.float32) * (2.0 * math.pi / 65536.0)
    u = t * t
    sine = t * (1.0 + u * (-1.0 / 6 + u * (1.0 / 120 + u * (-1.0 / 5040))))
    cosine = 1.0 + u * (-0.5 + u * (1.0 / 24 + u * (-1.0 / 720 + u * (1.0 / 40320))))
    odd = (quarter & 1) == 1
    c = jnp.where(odd, sine, cosine)
    s = jnp.where(odd, cosine, sine)
    c = jnp.where(((quarter + 1) & 2) == 2, -c, c)
    s = jnp.where((quarter & 2) == 2, -s, s)
    return c, s


def swap_index_with_lanes(tiles, block):
    lane = lax.broadcasted_iota(jnp.int32, tiles[0].shape, 1)
    bit = 1
    while bit < len(tiles):
        upper = (lane & (bit * block)) != 0
        swapped = list(tiles)
        for i in range(len(tiles)):
            if not i & bit:
                low, high = tiles[i], tiles[i | bit]
                swapped[i] = jnp.where(upper, pltpu.roll(high, bit * block, 1), low)
                swapped[i | bit] = jnp.where(upper, high, pltpu.roll(low, LANES - bit * block, 1))
        tiles = swapped
        bit *= 2
    return tiles


def kernel(
    sizes,
    amplitude,
    own_ref,
    taps_hbm,
    table_hbm,
    delays_hbm,
    station_hbm,
    beam_hbm,
    out_ref,
    volts,
    taps_ref,
    table,
    delay_in,
    station_in,
    beam_in,
    wide_taps,
    wide_int,
    member,
    steps,
    state,
    filtered,
    spectra,
    total_ref,
    turned,
    part,
    final,
    own_sem,
    small_sem,
    halo_send,
    halo_recv,
    send,
    recv,
    far_send,
    far_recv,
    *exchanged,
):
    n_chan, n_core, bits = sizes
    received, sent = exchanged[:bits], exchanged[bits:]
    chans, stations, samples = own_ref.shape[1:]
    tap_count, fine = taps_ref.shape
    beams = delay_in.shape[0]
    frames = final.shape[-2]
    halves = fine // LANES
    chunks = chans * halves
    lane_groups = LANES // stations
    hop = 3 * fine // 4
    groups = frames // PHASES
    quads = LANES // lane_groups // QUAD
    n_stn = 2**bits
    rows = 2 * beams // n_stn
    per = beams // n_stn
    width = frames * lane_groups
    tiles = QUAD * width // LANES
    halo = volts.shape[3] - samples
    stn, chan, core = (lax.axis_index(name) for name in ("stn", "chan", "beam"))

    def fetch(c):
        return pltpu.make_async_copy(
            own_ref.at[:, c], volts.at[:, c, :, pl.ds(0, samples)], own_sem.at[c]
        )

    small = [
        pltpu.make_async_copy(source, target, small_sem.at[i])
        for i, (source, target) in enumerate(
            (
                (taps_hbm, taps_ref),
                (delays_hbm, delay_in),
                (station_hbm, station_in),
                (beam_hbm, beam_in),
                (table_hbm, table),
            )
        )
    ]
    own_bit = [(stn // 2 ** (bits - 1 - dim)) % 2 for dim in range(bits)]
    orders = (tuple(range(bits - 1, -1, -1)), tuple(range(bits)))

    def partner(dim):
        return (stn + (1 - 2 * own_bit[dim]) * 2 ** (bits - 1 - dim), chan, core)

    def far(dz, dc):
        return ((chan + dz) % n_chan, (core + dc) % n_core)

    offsets = [(dz, dc) for dz in range(n_chan) for dc in range(n_core)]
    barrier = pltpu.get_barrier_semaphore()
    peers = [partner(dim) for dim in range(bits)] + [(stn, *far(dz, dc)) for dz, dc in offsets[1:]]
    for peer in peers:
        pl.semaphore_signal(barrier, inc=1, device_id=peer, device_id_type=MESH)
    small[0].start()
    fetch(0).start()
    for copy in small[1:]:
        copy.start()
    for c in range(1, chans):
        fetch(c).start()

    def halo_copy(c, ri):
        return pltpu.make_async_remote_copy(
            src_ref=own_ref.at[ri, c, :, pl.ds(0, halo)],
            dst_ref=volts.at[ri, c, :, pl.ds(samples, halo)],
            send_sem=halo_send.at[c, ri],
            recv_sem=halo_recv.at[c, ri],
            device_id=(stn, chan, core - 1),
            device_id_type=MESH,
        )

    def send_halo(c):
        for ri in range(2):
            halo_copy(c, ri).start()

    small[0].wait()

    pl.semaphore_wait(barrier, len(peers))

    @pl.when(core > 0)
    def _():
        send_halo(0)

    @pl.when(core == n_core - 1)
    def _():
        volts[:, :, :, samples:] = jnp.zeros((2, chans, stations, halo), volts.dtype)

    for phase in range(PHASES):
        shift = hop * phase % fine
        rolled = taps_ref[...]
        if shift:
            rolled = pltpu.roll(rolled, shift, 1)
        column = lax.broadcasted_iota(jnp.int32, (1, fine), 1)
        for u in range(tap_count + 1):
            late = rolled[u : u + 1] if u < tap_count else jnp.zeros((1, fine), jnp.float32)
            early = rolled[u - 1 : u] if u > 0 else jnp.zeros((1, fine), jnp.float32)
            row = jnp.where(column >= shift, late, early)
            wide_taps[phase, u] = jnp.broadcast_to(row, (16, fine)).astype(jnp.bfloat16)

    for copy in small[1:]:
        copy.wait()

    def widened(value, count):
        wide_int[...] = jnp.zeros(wide_int.shape, jnp.int32)
        wide_int[0:count, 0:stations] = value
        full = wide_int[...]
        step = stations
        while step < LANES:
            full = full + pltpu.roll(full, step, 1)
            step *= 2
        return full[0:count]

    group_of_lane = lax.broadcasted_iota(jnp.int32, (1, LANES), 1) // stations
    station_row = widened(station_in[...], 1).astype(jnp.float32)
    square = (beams, beams)
    diagonal = lax.broadcasted_iota(jnp.int32, square, 0) == lax.broadcasted_iota(jnp.int32, square, 1)
    beam_row = jnp.broadcast_to(beam_in[...].astype(jnp.float32), square)
    beam_column = jnp.sum(jnp.where(diagonal, beam_row, 0.0), axis=1, keepdims=True)
    member[...] = jnp.where(beam_column == station_row, amplitude, 0.0)
    delay = widened(delay_in[...], beams)
    wide_int[...] = delay
    for i, stride in enumerate((lane_groups, QUAD * lane_groups)):
        c, s = unit_turn((delay * stride) & 65535)
        steps[i, 0] = c
        steps[i, 1] = -s

    def filter_part(c, ri, local):
        limit = samples // fine
        for half in range(halves):
            for phase in range(PHASES):
                shift = hop * phase % fine
                block0 = hop * phase // fine
                first = 0 if shift < (half + 1) * LANES else 1
                last = tap_count - 1 if shift <= half * LANES else tap_count
                lanes = slice(half * LANES, (half + 1) * LANES)
                taps = {u: wide_taps[phase, u, :, lanes][None] for u in range(first, last + 1)}
                columns = pl.ds(pl.multiple_of(ri * fine + half * LANES, LANES), LANES)
                blocks = [
                    block
                    for block in range(block0 + first, block0 + last + 1 + 3 * (groups - 1))
                    if (block < limit) == local
                ]
                for_group = [
                    [block for block in blocks if first <= block - block0 - 3 * g <= last]
                    for g in range(groups)
                ]
                sums = [[None, None] for _ in range(groups)]
                for g in range(groups):
                    f = PHASES * g + phase
                    if not local and for_group[g] and block0 + 3 * g + first < limit:
                        begun = filtered[c % 2, f * stations : (f + 1) * stations, columns]
                        sums[g][0] = begun.reshape(stations // 16, 16, LANES)
                for block in blocks:
                    at = block * fine + half * LANES
                    value = volts[ri, c, :, at : at + LANES].reshape(stations // 16, 16, LANES)
                    for g in range(groups):
                        if block in for_group[g]:
                            u = block - block0 - 3 * g
                            term = taps[u] * value
                            so_far = sums[g][u % 2]
                            sums[g][u % 2] = term if so_far is None else so_far + term
                for g in range(groups):
                    if for_group[g]:
                        f = PHASES * g + phase
                        parts = [part_sum for part_sum in sums[g] if part_sum is not None]
                        filtered[c % 2, f * stations : (f + 1) * stations, columns] = sum(
                            parts[1:], parts[0]
                        ).reshape(stations, LANES)

    def filter_channel(c, first_part, last_part):
        @pl.loop(first_part, last_part)
        def _(ri):
            @pl.when(ri == 0)
            def _():
                fetch(c).wait()

            filter_part(c, ri, True)

        @pl.loop(first_part, last_part)
        def _(ri):
            @pl.when(core < n_core - 1)
            def _():
                halo_copy(c, ri).wait_recv()

            @pl.when((core > 0) & (c + 1 < chans))
            def _():
                halo_copy(c + 1, ri).start()

            filter_part(c, ri, False)

    def transform(chunk):
        half = chunk % halves
        slot = chunk // halves % 2
        count = LANES // lane_groups

        def one(fb):
            rhs = filtered[slot, pl.ds(pl.multiple_of(fb * LANES, LANES), WIDE * LANES), :]
            result = lax.dot_general(
                table[half], rhs, (((1,), (1,)), ((), ())), preferred_element_type=jnp.float32
            )
            for ri in range(2):
                for sub in range(WIDE):
                    pieces = [
                        result[
                            (ri * lane_groups + j) * count : (ri * lane_groups + j + 1) * count,
                            sub * LANES : (sub + 1) * LANES,
                        ]
                        for j in range(lane_groups)
                    ]
                    for j, piece in enumerate(swap_index_with_lanes(pieces, stations)):
                        at = pl.multiple_of(((fb + sub) * lane_groups + j) * count, count)
                        spectra[half, ri, pl.ds(at, count), :] = piece

        if UNROLL_FB:
            for fb in range(0, frames // lane_groups, WIDE):
                one(fb)
        else:
            @pl.loop(0, frames // lane_groups // WIDE)
            def _(fb):
                one(fb * WIDE)

    def form_beams(chunk, c, half):
        count = LANES // lane_groups
        frequency = (chan * chans + c) * fine + half * LANES + group_of_lane
        cosine, sine = unit_turn((wide_int[...] * frequency) & 65535)
        state[0] = cosine * member[...]
        state[1] = -sine * member[...]
        lane = lax.broadcasted_iota(jnp.int32, (frames, LANES), 1) // stations
        out_lane = lax.broadcasted_iota(jnp.int32, (2 * beams, LANES), 1)

        def times(a, i):
            e_re, e_im = steps[i, 0], steps[i, 1]
            return (a[0] * e_re - a[1] * e_im, a[0] * e_im + a[1] * e_re)

        def stacked(top, bottom):
            both = [v.reshape(n_stn, per, LANES) for v in (top, bottom)]
            return jnp.stack(both, axis=1).reshape(2 * beams, LANES)

        def one(quad):
            first = weight = (state[0], state[1])
            outs = []
            for q in range(QUAD):
                if q:
                    weight = times(weight, 0)
                w_re, w_im = weight
                lhs = jnp.concatenate([stacked(w_re, w_im), stacked(-w_im, w_re)], axis=1)
                at = quad * QUAD + q
                x = [spectra.at[half, ri][pl.ds(at, frames, stride=count), :] for ri in range(2)]
                blocks = [
                    jnp.concatenate([jnp.where(lane == j, v, 0.0) for v in x], axis=1)
                    for j in range(lane_groups)
                ]
                if width < LANES:
                    blocks.append(jnp.zeros((LANES - width, 2 * LANES), jnp.float32))
                turn = q * width % LANES
                if turn:
                    blocks = [jnp.concatenate(blocks, axis=0)]
                    blocks = [blocks[0][LANES - turn :], blocks[0][: LANES - turn]]
                rhs = jnp.concatenate(blocks, axis=0)
                result = lax.dot_general(
                    lhs.astype(jnp.bfloat16),
                    rhs.astype(jnp.bfloat16),
                    (((1,), (1,)), ((), ())),
                    preferred_element_type=jnp.float32,
                )
                outs.append(result)
            following = times(first, 1)
            state[0] = following[0]
            state[1] = following[1]
            for t in range(tiles):
                value = None
                for q in range(QUAD):
                    start = q * width - t * LANES
                    if -width < start < LANES:
                        value = outs[q] if value is None else jnp.where(out_lane >= start, outs[q], value)
                value = value.astype(jnp.bfloat16)
                for d in range(n_stn):
                    place = [(d >> (bits - 1 - dim)) & 1 for dim in range(bits)]
                    part[(chunk, quad // (quads // PIECES), *place, quad % (quads // PIECES), t)] = value[
                        d * rows : (d + 1) * rows
                    ]

        for quad in range(quads):
            one(quad)
            if (quad + 1) % (quads // PIECES) == 0:
                hop_copy(chunk, quad // (quads // PIECES), 0).start()

    def region(order, stage, last):
        index = [slice(None)] * bits
        for dim in orders[order % 2][:stage]:
            index[dim] = own_bit[dim]
        if stage < bits:
            index[orders[order % 2][stage]] = last(orders[order % 2][stage])
        return index

    def other(dim):
        return 1 - own_bit[dim]

    def with_received(chunk, order, stage, index):
        value = part[(chunk, order, *index)].astype(jnp.float32)
        for earlier in range(stage):
            kept = [dim for dim in range(bits) if dim not in orders[order % 2][: earlier + 1]]
            piece = received[earlier][(chunk, order, *(index[dim] for dim in kept))]
            value = value + piece.astype(jnp.float32)
        return value

    def hop_copy(chunk, order, stage):
        if stage == 0:
            source = part.at[(chunk, order, *region(order, 0, other))]
        else:
            source = sent[stage - 1].at[chunk, order]
        return pltpu.make_async_remote_copy(
            src_ref=source,
            dst_ref=received[stage].at[chunk, order],
            send_sem=send.at[stage],
            recv_sem=recv.at[stage, chunk, order],
            device_id=partner(orders[order % 2][stage]),
            device_id_type=MESH,
        )

    def place_of(chunk):
        c = chunk // halves
        lanes = pl.ds(pl.multiple_of((chunk % halves) * LANES, LANES), LANES)
        return out_ref.at[:, :, chan * chans + c, core, :, lanes]

    def deliver(chunk, number):
        z, k = far(*offsets[number])
        return pltpu.make_async_remote_copy(
            src_ref=final.at[chunk, z, k],
            dst_ref=place_of(chunk),
            send_sem=far_send,
            recv_sem=far_recv,
            device_id=(stn, z, k),
            device_id_type=MESH,
        )

    def keep(chunk):
        return pltpu.make_async_copy(final.at[chunk, chan, core], place_of(chunk), far_recv)

    def finish(chunk):
        for order in range(PIECES):
            value = with_received(chunk, order, bits, own_bit)
            for quad in range(quads // PIECES):
                at = (order * (quads // PIECES) + quad) * rows
                for t in range(tiles):
                    total_ref[t, at : at + rows, :] = value[quad, t]
        for t in range(tiles):
            turned[t * LANES : (t + 1) * LANES, :] = total_ref[t].T
        pieces = [turned[i * frames : (i + 1) * frames, :] for i in range(rows)]
        for row, piece in enumerate(swap_index_with_lanes(pieces, 1)):
            ri, b = divmod(row, per)
            device, at = divmod(b, per // (n_chan * n_core))
            z, k = divmod(device, n_core)
            final[chunk, z, k, at, ri] = piece.astype(jnp.bfloat16)

    def step(chunk, stage):
        for order in range(PIECES):
            hop_copy(chunk, order, stage - 1).wait_recv()
            if stage < bits:
                sent[stage - 1][chunk, order] = with_received(
                    chunk, order, stage, region(order, stage, other)
                ).astype(jnp.bfloat16)
                hop_copy(chunk, order, stage).start()
        if stage == bits:
            finish(chunk)
            for number in range(len(offsets) - 1, 0, -1):
                deliver(chunk, number).start()
            keep(chunk).start()

    @pl.loop(0, chunks + LEAD + bits)
    def _(tick):
        def during(chunk, action):
            @pl.when((chunk >= 0) & (chunk < chunks))
            def _():
                action(chunk)

        during(tick - LEAD, lambda chunk: form_beams(chunk, chunk // halves, chunk % halves))
        c = tick // halves

        @pl.when((c < chans) & (tick != 1))
        def _():
            filter_channel(c, tick % 2, jnp.where(tick == 0, 2, tick % 2 + 1))

        @pl.when((tick >= 1) & (tick <= chunks))
        def _():
            transform(tick - 1)

        for stage in range(1, bits):
            during(tick - LEAD - stage, lambda chunk, stage=stage: step(chunk, stage))

        def summed(tick):
            caught_up = jnp.where(tick >= LEAD + chunks - 1, LATE, 0)
            return jnp.clip(tick - LEAD - bits - LATE + 1 + caught_up, 0, chunks)

        @pl.loop(summed(tick - 1), summed(tick))
        def _(chunk):
            step(chunk, bits)


    @pl.when(core > 0)
    def _():
        for c in range(chans):
            for ri in range(2):
                halo_copy(c, ri).wait_send()

    def all_of(ref, send_sem, recv_sem):
        return pltpu.make_async_remote_copy(
            src_ref=ref,
            dst_ref=ref,
            send_sem=send_sem,
            recv_sem=recv_sem,
            device_id=partner(0),
            device_id_type=MESH,
        )

    for stage in range(bits):
        all_of(received[stage], send.at[stage], far_recv).wait_send()
    if n_chan > 1:
        all_of(final.at[:, 0 : n_chan - 1], far_send, far_recv).wait_send()
    if n_core > 1:
        all_of(final.at[:, 0, 0 : n_core - 1], far_send, far_recv).wait_send()
    all_of(out_ref, far_send, far_recv).wait_recv()


def body(volts, taps, delays, station_sub, beam_sub):
    own = jnp.transpose(volts, (0, 2, 1, 3))
    chans, stations, samples = own.shape[1:]
    tap_count, fine = taps.shape
    beams = delays.shape[0]
    n_stn, n_chan, n_core = (lax.axis_size(name) for name in ("stn", "chan", "beam"))
    bits = n_stn.bit_length() - 1
    hop = 3 * fine // 4
    frames = samples // hop
    per = beams // n_stn
    per_device = per // (n_chan * n_core)
    halves = fine // LANES
    chunks = chans * halves
    lane_groups = LANES // stations
    quads = LANES // lane_groups // QUAD
    tiles = QUAD * frames * lane_groups // LANES
    rows = 2 * per
    assert halves == 2 and n_stn == 2**bits and rows == QUAD * lane_groups and quads * rows == LANES
    assert QUAD * frames * lane_groups == tiles * LANES and frames * lane_groups <= LANES
    blocks = hop * (PHASES - 1) // fine + tap_count + 1 + 3 * (frames // PHASES - 1)
    amplitude = 1.0 / math.sqrt(stations * n_stn // SUBARRAYS)
    block = (quads // PIECES, tiles, rows, LANES)
    pieces = [
        pltpu.VMEM((chunks, PIECES) + (2,) * (bits - 1 - t) + block, jnp.bfloat16) for t in range(bits)
    ]
    hbm = pl.BlockSpec(memory_space=pltpu.HBM)
    dma = pltpu.SemaphoreType.DMA
    out = pl.pallas_call(
        functools.partial(kernel, (n_chan, n_core, bits), amplitude),
        out_shape=jax.ShapeDtypeStruct(
            (per_device, 2, n_chan * chans, n_core, frames, fine), jnp.bfloat16
        ),
        in_specs=[hbm] * 6,
        out_specs=pl.BlockSpec(memory_space=pl.ANY),
        scratch_shapes=[
            pltpu.VMEM((2, chans, stations, blocks * fine), jnp.bfloat16),
            pltpu.VMEM((tap_count, fine), jnp.float32),
            pltpu.VMEM((halves, 2 * LANES, 2 * fine), jnp.bfloat16),
            pltpu.VMEM((beams, stations), jnp.int32),
            pltpu.VMEM((1, stations), jnp.int32),
            pltpu.VMEM((1, beams), jnp.int32),
            pltpu.VMEM((PHASES, tap_count + 1, 16, fine), jnp.bfloat16),
            pltpu.VMEM((beams, LANES), jnp.int32),
            pltpu.VMEM((beams, LANES), jnp.float32),
            pltpu.VMEM((2, 2, beams, LANES), jnp.float32),
            pltpu.VMEM((2, beams, LANES), jnp.float32),
            pltpu.VMEM((2, frames * stations, 2 * fine), jnp.bfloat16),
            pltpu.VMEM((halves, 2, frames * LANES // lane_groups, LANES), jnp.float32),
            pltpu.VMEM((tiles, LANES, LANES), jnp.float32),
            pltpu.VMEM((tiles * LANES, LANES), jnp.float32),
            pltpu.VMEM((chunks, PIECES) + (2,) * bits + block, jnp.bfloat16),
            pltpu.VMEM((chunks, n_chan, n_core, per_device, 2, frames, LANES), jnp.bfloat16),
            dma((chans,)),
            dma((5,)),
            dma((chans, 2)),
            dma((chans, 2)),
            dma((bits,)),
            dma((bits, chunks, PIECES)),
            dma,
            dma,
            *pieces,
            *pieces[1:],
        ],
        compiler_params=pltpu.CompilerParams(
            collective_id=0, has_side_effects=True, vmem_limit_bytes=VMEM_LIMIT
        ),
        name="channelize_and_beamform",
    )(
        *(
            pltpu.with_memory_space_constraint(x, pltpu.HBM)
            for x in (
                own,
                taps,
                dft_table(fine, lane_groups),
                delays,
                station_sub[None],
                beam_sub[None],
            )
        )
    )
    return out.reshape(per_device, 2, n_chan * chans, n_core * frames, fine).astype(jnp.float32)


def solution(mesh):
    placed = (P(None, "stn", "chan", "beam"), P(), P(None, "stn"), P("stn"), P())
    return jax.shard_map(
        body,
        mesh=mesh,
        in_specs=placed,
        out_specs=P(("stn", "chan", "beam"), None, None, None, None),
        check_vma=False,
    )
```

```python
import functools
import math

import jax
import jax.numpy as jnp
import numpy as np
from jax import lax
from jax.experimental import pallas as pl
from jax.experimental.pallas import tpu as pltpu
from jax.sharding import PartitionSpec as P

SUBARRAYS = 4
LANES = 128
QUAD = 4
WIDE = 2
UNROLL_FB = True
LEAD = 2
LATE = 1
PIECES = 2
PHASES = 4
VMEM_LIMIT = 32 * 2**20
MESH = pl.DeviceIdType.MESH


def dft_table(fine, lane_groups):
    index = np.arange(fine)
    angle = 2.0 * np.pi * (index[:, None] * index[None, :] % fine) / fine
    scale = 1.0 / math.sqrt(fine)
    cosine = np.cos(angle) * scale
    sine = np.sin(angle) * scale
    whole = np.stack([np.concatenate([cosine, sine]), np.concatenate([-sine, cosine])])
    halves = []
    for half in range(fine // LANES):
        k = half * LANES + (np.arange(LANES).reshape(-1, lane_groups).T).reshape(-1)
        halves.append(np.concatenate([whole[0][:, k].T, whole[1][:, k].T]))
    return jnp.asarray(np.stack(halves), jnp.bfloat16)


def unit_turn(turn):
    quarter = (turn + 8192) >> 14
    t = (turn - (quarter << 14)).astype(jnp.float32) * (2.0 * math.pi / 65536.0)
    u = t * t
    sine = t * (1.0 + u * (-1.0 / 6 + u * (1.0 / 120 + u * (-1.0 / 5040))))
    cosine = 1.0 + u * (-0.5 + u * (1.0 / 24 + u * (-1.0 / 720 + u * (1.0 / 40320))))
    odd = (quarter & 1) == 1
    c = jnp.where(odd, sine, cosine)
    s = jnp.where(odd, cosine, sine)
    c = jnp.where(((quarter + 1) & 2) == 2, -c, c)
    s = jnp.where((quarter & 2) == 2, -s, s)
    return c, s


def swap_index_with_lanes(tiles, block):
    lane = lax.broadcasted_iota(jnp.int32, tiles[0].shape, 1)
    bit = 1
    while bit < len(tiles):
        upper = (lane & (bit * block)) != 0
        swapped = list(tiles)
        for i in range(len(tiles)):
            if not i & bit:
                low, high = tiles[i], tiles[i | bit]
                swapped[i] = jnp.where(upper, pltpu.roll(high, bit * block, 1), low)
                swapped[i | bit] = jnp.where(upper, high, pltpu.roll(low, LANES - bit * block, 1))
        tiles = swapped
        bit *= 2
    return tiles


def kernel(
    sizes,
    amplitude,
    own_ref,
    taps_hbm,
    table_hbm,
    delays_hbm,
    station_hbm,
    beam_hbm,
    out_ref,
    volts,
    taps_ref,
    table,
    delay_in,
    station_in,
    beam_in,
    wide_taps,
    wide_int,
    member,
    steps,
    state,
    filtered,
    spectra,
    total_ref,
    turned,
    part,
    final,
    own_sem,
    small_sem,
    halo_send,
    halo_recv,
    send,
    recv,
    far_send,
    far_recv,
    *exchanged,
):
    n_chan, n_core, bits = sizes
    received, sent = exchanged[:bits], exchanged[bits:]
    chans, stations, samples = own_ref.shape[1:]
    tap_count, fine = taps_ref.shape
    beams = delay_in.shape[0]
    frames = final.shape[-2]
    halves = fine // LANES
    chunks = chans * halves
    lane_groups = LANES // stations
    hop = 3 * fine // 4
    groups = frames // PHASES
    quads = LANES // lane_groups // QUAD
    n_stn = 2**bits
    rows = 2 * beams // n_stn
    per = beams // n_stn
    width = frames * lane_groups
    tiles = QUAD * width // LANES
    halo = volts.shape[3] - samples
    stn, chan, core = (lax.axis_index(name) for name in ("stn", "chan", "beam"))

    def fetch(c):
        return pltpu.make_async_copy(
            own_ref.at[:, c], volts.at[:, c, :, pl.ds(0, samples)], own_sem.at[c]
        )

    small = [
        pltpu.make_async_copy(source, target, small_sem.at[i])
        for i, (source, target) in enumerate(
            (
                (taps_hbm, taps_ref),
                (delays_hbm, delay_in),
                (station_hbm, station_in),
                (beam_hbm, beam_in),
                (table_hbm, table),
            )
        )
    ]
    own_bit = [(stn // 2 ** (bits - 1 - dim)) % 2 for dim in range(bits)]
    orders = (tuple(range(bits - 1, -1, -1)), tuple(range(bits)))

    def partner(dim):
        return (stn + (1 - 2 * own_bit[dim]) * 2 ** (bits - 1 - dim), chan, core)

    def far(dz, dc):
        return ((chan + dz) % n_chan, (core + dc) % n_core)

    offsets = [(dz, dc) for dz in range(n_chan) for dc in range(n_core)]
    barrier = pltpu.get_barrier_semaphore()
    peers = [partner(dim) for dim in range(bits)] + [(stn, *far(dz, dc)) for dz, dc in offsets[1:]]
    for peer in peers:
        pl.semaphore_signal(barrier, inc=1, device_id=peer, device_id_type=MESH)
    small[0].start()
    fetch(0).start()
    for copy in small[1:]:
        copy.start()
    for c in range(1, chans):
        fetch(c).start()

    def halo_copy(c, ri):
        return pltpu.make_async_remote_copy(
            src_ref=own_ref.at[ri, c, :, pl.ds(0, halo)],
            dst_ref=volts.at[ri, c, :, pl.ds(samples, halo)],
            send_sem=halo_send.at[c, ri],
            recv_sem=halo_recv.at[c, ri],
            device_id=(stn, chan, core - 1),
            device_id_type=MESH,
        )

    def send_halo(c):
        for ri in range(2):
            halo_copy(c, ri).start()

    small[0].wait()

    pl.semaphore_wait(barrier, len(peers))

    @pl.when(core > 0)
    def _():
        send_halo(0)

    @pl.when(core == n_core - 1)
    def _():
        volts[:, :, :, samples:] = jnp.zeros((2, chans, stations, halo), volts.dtype)

    for phase in range(PHASES):
        shift = hop * phase % fine
        rolled = taps_ref[...]
        if shift:
            rolled = pltpu.roll(rolled, shift, 1)
        column = lax.broadcasted_iota(jnp.int32, (1, fine), 1)
        for u in range(tap_count + 1):
            late = rolled[u : u + 1] if u < tap_count else jnp.zeros((1, fine), jnp.float32)
            early = rolled[u - 1 : u] if u > 0 else jnp.zeros((1, fine), jnp.float32)
            row = jnp.where(column >= shift, late, early)
            wide_taps[phase, u] = jnp.broadcast_to(row, (16, fine)).astype(jnp.bfloat16)

    for copy in small[1:]:
        copy.wait()

    def widened(value, count):
        wide_int[...] = jnp.zeros(wide_int.shape, jnp.int32)
        wide_int[0:count, 0:stations] = value
        full = wide_int[...]
        step = stations
        while step < LANES:
            full = full + pltpu.roll(full, step, 1)
            step *= 2
        return full[0:count]

    group_of_lane = lax.broadcasted_iota(jnp.int32, (1, LANES), 1) // stations
    station_row = widened(station_in[...], 1).astype(jnp.float32)
    square = (beams, beams)
    diagonal = lax.broadcasted_iota(jnp.int32, square, 0) == lax.broadcasted_iota(jnp.int32, square, 1)
    beam_row = jnp.broadcast_to(beam_in[...].astype(jnp.float32), square)
    beam_column = jnp.sum(jnp.where(diagonal, beam_row, 0.0), axis=1, keepdims=True)
    member[...] = jnp.where(beam_column == station_row, amplitude, 0.0)
    delay = widened(delay_in[...], beams)
    wide_int[...] = delay
    for i, stride in enumerate((lane_groups, QUAD * lane_groups)):
        c, s = unit_turn((delay * stride) & 65535)
        steps[i, 0] = c
        steps[i, 1] = -s

    def filter_part(c, ri, local):
        limit = samples // fine
        for half in range(halves):
            for phase in range(PHASES):
                shift = hop * phase % fine
                block0 = hop * phase // fine
                first = 0 if shift < (half + 1) * LANES else 1
                last = tap_count - 1 if shift <= half * LANES else tap_count
                lanes = slice(half * LANES, (half + 1) * LANES)
                taps = {u: wide_taps[phase, u, :, lanes][None] for u in range(first, last + 1)}
                columns = pl.ds(pl.multiple_of(ri * fine + half * LANES, LANES), LANES)
                blocks = [
                    block
                    for block in range(block0 + first, block0 + last + 1 + 3 * (groups - 1))
                    if (block < limit) == local
                ]
                for_group = [
                    [block for block in blocks if first <= block - block0 - 3 * g <= last]
                    for g in range(groups)
                ]
                sums = [[None, None] for _ in range(groups)]
                for g in range(groups):
                    f = PHASES * g + phase
                    if not local and for_group[g] and block0 + 3 * g + first < limit:
                        begun = filtered[c % 2, f * stations : (f + 1) * stations, columns]
                        sums[g][0] = begun.reshape(stations // 16, 16, LANES)
                for block in blocks:
                    at = block * fine + half * LANES
                    value = volts[ri, c, :, at : at + LANES].reshape(stations // 16, 16, LANES)
                    for g in range(groups):
                        if block in for_group[g]:
                            u = block - block0 - 3 * g
                            term = taps[u] * value
                            so_far = sums[g][u % 2]
                            sums[g][u % 2] = term if so_far is None else so_far + term
                for g in range(groups):
                    if for_group[g]:
                        f = PHASES * g + phase
                        parts = [part_sum for part_sum in sums[g] if part_sum is not None]
                        filtered[c % 2, f * stations : (f + 1) * stations, columns] = sum(
                            parts[1:], parts[0]
                        ).reshape(stations, LANES)

    def filter_channel(c, first_part, last_part):
        @pl.loop(first_part, last_part)
        def _(ri):
            @pl.when(ri == 0)
            def _():
                fetch(c).wait()

            filter_part(c, ri, True)

        @pl.loop(first_part, last_part)
        def _(ri):
            @pl.when(core < n_core - 1)
            def _():
                halo_copy(c, ri).wait_recv()

            @pl.when((core > 0) & (c + 1 < chans))
            def _():
                halo_copy(c + 1, ri).start()

            filter_part(c, ri, False)

    def transform(chunk):
        half = chunk % halves
        slot = chunk // halves % 2
        count = LANES // lane_groups

        def one(fb):
            rhs = filtered[slot, pl.ds(pl.multiple_of(fb * LANES, LANES), WIDE * LANES), :]
            result = lax.dot_general(
                table[half], rhs, (((1,), (1,)), ((), ())), preferred_element_type=jnp.float32
            )
            for ri in range(2):
                for sub in range(WIDE):
                    pieces = [
                        result[
                            (ri * lane_groups + j) * count : (ri * lane_groups + j + 1) * count,
                            sub * LANES : (sub + 1) * LANES,
                        ]
                        for j in range(lane_groups)
                    ]
                    for j, piece in enumerate(swap_index_with_lanes(pieces, stations)):
                        at = pl.multiple_of(((fb + sub) * lane_groups + j) * count, count)
                        spectra[half, ri, pl.ds(at, count), :] = piece

        if UNROLL_FB:
            for fb in range(0, frames // lane_groups, WIDE):
                one(fb)
        else:
            @pl.loop(0, frames // lane_groups // WIDE)
            def _(fb):
                one(fb * WIDE)

    def form_beams(chunk, c, half):
        count = LANES // lane_groups
        frequency = (chan * chans + c) * fine + half * LANES + group_of_lane
        cosine, sine = unit_turn((wide_int[...] * frequency) & 65535)
        state[0] = cosine * member[...]
        state[1] = -sine * member[...]
        lane = lax.broadcasted_iota(jnp.int32, (frames, LANES), 1) // stations
        out_lane = lax.broadcasted_iota(jnp.int32, (2 * beams, LANES), 1)

        def times(a, i):
            e_re, e_im = steps[i, 0], steps[i, 1]
            return (a[0] * e_re - a[1] * e_im, a[0] * e_im + a[1] * e_re)

        def stacked(top, bottom):
            both = [v.reshape(n_stn, per, LANES) for v in (top, bottom)]
            return jnp.stack(both, axis=1).reshape(2 * beams, LANES)

        def one(quad):
            first = weight = (state[0], state[1])
            outs = []
            for q in range(QUAD):
                if q:
                    weight = times(weight, 0)
                w_re, w_im = weight
                lhs = jnp.concatenate([stacked(w_re, w_im), stacked(-w_im, w_re)], axis=1)
                at = quad * QUAD + q
                x = [spectra.at[half, ri][pl.ds(at, frames, stride=count), :] for ri in range(2)]
                blocks = [
                    jnp.concatenate([jnp.where(lane == j, v, 0.0) for v in x], axis=1)
                    for j in range(lane_groups)
                ]
                if width < LANES:
                    blocks.append(jnp.zeros((LANES - width, 2 * LANES), jnp.float32))
                turn = q * width % LANES
                if turn:
                    blocks = [jnp.concatenate(blocks, axis=0)]
                    blocks = [blocks[0][LANES - turn :], blocks[0][: LANES - turn]]
                rhs = jnp.concatenate(blocks, axis=0)
                result = lax.dot_general(
                    lhs.astype(jnp.bfloat16),
                    rhs.astype(jnp.bfloat16),
                    (((1,), (1,)), ((), ())),
                    preferred_element_type=jnp.float32,
                )
                outs.append(result)
            following = times(first, 1)
            state[0] = following[0]
            state[1] = following[1]
            for t in range(tiles):
                value = None
                for q in range(QUAD):
                    start = q * width - t * LANES
                    if -width < start < LANES:
                        value = outs[q] if value is None else jnp.where(out_lane >= start, outs[q], value)
                value = value.astype(jnp.bfloat16)
                for d in range(n_stn):
                    place = [(d >> (bits - 1 - dim)) & 1 for dim in range(bits)]
                    part[(chunk, quad // (quads // PIECES), *place, quad % (quads // PIECES), t)] = value[
                        d * rows : (d + 1) * rows
                    ]

        for quad in range(quads):
            one(quad)
            if (quad + 1) % (quads // PIECES) == 0:
                hop_copy(chunk, quad // (quads // PIECES), 0).start()

    def region(order, stage, last):
        index = [slice(None)] * bits
        for dim in orders[order % 2][:stage]:
            index[dim] = own_bit[dim]
        if stage < bits:
            index[orders[order % 2][stage]] = last(orders[order % 2][stage])
        return index

    def other(dim):
        return 1 - own_bit[dim]

    def with_received(chunk, order, stage, index):
        value = part[(chunk, order, *index)].astype(jnp.float32)
        for earlier in range(stage):
            kept = [dim for dim in range(bits) if dim not in orders[order % 2][: earlier + 1]]
            piece = received[earlier][(chunk, order, *(index[dim] for dim in kept))]
            value = value + piece.astype(jnp.float32)
        return value

    def hop_copy(chunk, order, stage):
        if stage == 0:
            source = part.at[(chunk, order, *region(order, 0, other))]
        else:
            source = sent[stage - 1].at[chunk, order]
        return pltpu.make_async_remote_copy(
            src_ref=source,
            dst_ref=received[stage].at[chunk, order],
            send_sem=send.at[stage],
            recv_sem=recv.at[stage, chunk, order],
            device_id=partner(orders[order % 2][stage]),
            device_id_type=MESH,
        )

    def place_of(chunk):
        c = chunk // halves
        lanes = pl.ds(pl.multiple_of((chunk % halves) * LANES, LANES), LANES)
        return out_ref.at[:, :, chan * chans + c, core, :, lanes]

    def deliver(chunk, number):
        z, k = far(*offsets[number])
        return pltpu.make_async_remote_copy(
            src_ref=final.at[chunk, z, k],
            dst_ref=place_of(chunk),
            send_sem=far_send,
            recv_sem=far_recv,
            device_id=(stn, z, k),
            device_id_type=MESH,
        )

    def keep(chunk):
        return pltpu.make_async_copy(final.at[chunk, chan, core], place_of(chunk), far_recv)

    def finish(chunk):
        for order in range(PIECES):
            value = with_received(chunk, order, bits, own_bit)
            for quad in range(quads // PIECES):
                at = (order * (quads // PIECES) + quad) * rows
                for t in range(tiles):
                    total_ref[t, at : at + rows, :] = value[quad, t]
        for t in range(tiles):
            turned[t * LANES : (t + 1) * LANES, :] = total_ref[t].T
        pieces = [turned[i * frames : (i + 1) * frames, :] for i in range(rows)]
        for row, piece in enumerate(swap_index_with_lanes(pieces, 1)):
            ri, b = divmod(row, per)
            device, at = divmod(b, per // (n_chan * n_core))
            z, k = divmod(device, n_core)
            final[chunk, z, k, at, ri] = piece.astype(jnp.bfloat16)

    def step(chunk, stage):
        for order in range(PIECES):
            hop_copy(chunk, order, stage - 1).wait_recv()
            if stage < bits:
                sent[stage - 1][chunk, order] = with_received(
                    chunk, order, stage, region(order, stage, other)
                ).astype(jnp.bfloat16)
                hop_copy(chunk, order, stage).start()
        if stage == bits:
            finish(chunk)
            for number in range(1, len(offsets)):
                deliver(chunk, number).start()
            keep(chunk).start()

    @pl.loop(0, chunks + LEAD + bits)
    def _(tick):
        def during(chunk, action):
            @pl.when((chunk >= 0) & (chunk < chunks))
            def _():
                action(chunk)

        during(tick - LEAD, lambda chunk: form_beams(chunk, chunk // halves, chunk % halves))
        c = tick // halves

        @pl.when((c < chans) & (tick != 1))
        def _():
            filter_channel(c, tick % 2, jnp.where(tick == 0, 2, tick % 2 + 1))

        @pl.when((tick >= 1) & (tick <= chunks))
        def _():
            transform(tick - 1)

        for stage in range(1, bits):
            during(tick - LEAD - stage, lambda chunk, stage=stage: step(chunk, stage))

        def summed(tick):
            caught_up = jnp.where(tick >= LEAD + chunks - 1, LATE, 0)
            return jnp.clip(tick - LEAD - bits - LATE + 1 + caught_up, 0, chunks)

        @pl.loop(summed(tick - 1), summed(tick))
        def _(chunk):
            step(chunk, bits)


    @pl.when(core > 0)
    def _():
        for c in range(chans):
            for ri in range(2):
                halo_copy(c, ri).wait_send()

    def all_of(ref, send_sem, recv_sem):
        return pltpu.make_async_remote_copy(
            src_ref=ref,
            dst_ref=ref,
            send_sem=send_sem,
            recv_sem=recv_sem,
            device_id=partner(0),
            device_id_type=MESH,
        )

    for stage in range(bits):
        all_of(received[stage], send.at[stage], far_recv).wait_send()
    if n_chan > 1:
        all_of(final.at[:, 0 : n_chan - 1], far_send, far_recv).wait_send()
    if n_core > 1:
        all_of(final.at[:, 0, 0 : n_core - 1], far_send, far_recv).wait_send()
    all_of(out_ref, far_send, far_recv).wait_recv()


def body(volts, taps, delays, station_sub, beam_sub):
    own = jnp.transpose(volts, (0, 2, 1, 3))
    chans, stations, samples = own.shape[1:]
    tap_count, fine = taps.shape
    beams = delays.shape[0]
    n_stn, n_chan, n_core = (lax.axis_size(name) for name in ("stn", "chan", "beam"))
    bits = n_stn.bit_length() - 1
    hop = 3 * fine // 4
    frames = samples // hop
    per = beams // n_stn
    per_device = per // (n_chan * n_core)
    halves = fine // LANES
    chunks = chans * halves
    lane_groups = LANES // stations
    quads = LANES // lane_groups // QUAD
    tiles = QUAD * frames * lane_groups // LANES
    rows = 2 * per
    assert halves == 2 and n_stn == 2**bits and rows == QUAD * lane_groups and quads * rows == LANES
    assert QUAD * frames * lane_groups == tiles * LANES and frames * lane_groups <= LANES
    blocks = hop * (PHASES - 1) // fine + tap_count + 1 + 3 * (frames // PHASES - 1)
    amplitude = 1.0 / math.sqrt(stations * n_stn // SUBARRAYS)
    block = (quads // PIECES, tiles, rows, LANES)
    pieces = [
        pltpu.VMEM((chunks, PIECES) + (2,) * (bits - 1 - t) + block, jnp.bfloat16) for t in range(bits)
    ]
    hbm = pl.BlockSpec(memory_space=pltpu.HBM)
    dma = pltpu.SemaphoreType.DMA
    out = pl.pallas_call(
        functools.partial(kernel, (n_chan, n_core, bits), amplitude),
        out_shape=jax.ShapeDtypeStruct(
            (per_device, 2, n_chan * chans, n_core, frames, fine), jnp.bfloat16
        ),
        in_specs=[hbm] * 6,
        out_specs=pl.BlockSpec(memory_space=pl.ANY),
        scratch_shapes=[
            pltpu.VMEM((2, chans, stations, blocks * fine), jnp.bfloat16),
            pltpu.VMEM((tap_count, fine), jnp.float32),
            pltpu.VMEM((halves, 2 * LANES, 2 * fine), jnp.bfloat16),
            pltpu.VMEM((beams, stations), jnp.int32),
            pltpu.VMEM((1, stations), jnp.int32),
            pltpu.VMEM((1, beams), jnp.int32),
            pltpu.VMEM((PHASES, tap_count + 1, 16, fine), jnp.bfloat16),
            pltpu.VMEM((beams, LANES), jnp.int32),
            pltpu.VMEM((beams, LANES), jnp.float32),
            pltpu.VMEM((2, 2, beams, LANES), jnp.float32),
            pltpu.VMEM((2, beams, LANES), jnp.float32),
            pltpu.VMEM((2, frames * stations, 2 * fine), jnp.bfloat16),
            pltpu.VMEM((halves, 2, frames * LANES // lane_groups, LANES), jnp.float32),
            pltpu.VMEM((tiles, LANES, LANES), jnp.float32),
            pltpu.VMEM((tiles * LANES, LANES), jnp.float32),
            pltpu.VMEM((chunks, PIECES) + (2,) * bits + block, jnp.bfloat16),
            pltpu.VMEM((chunks, n_chan, n_core, per_device, 2, frames, LANES), jnp.bfloat16),
            dma((chans,)),
            dma((5,)),
            dma((chans, 2)),
            dma((chans, 2)),
            dma((bits,)),
            dma((bits, chunks, PIECES)),
            dma,
            dma,
            *pieces,
            *pieces[1:],
        ],
        compiler_params=pltpu.CompilerParams(
            collective_id=0, has_side_effects=True, vmem_limit_bytes=VMEM_LIMIT
        ),
        name="channelize_and_beamform",
    )(
        *(
            pltpu.with_memory_space_constraint(x, pltpu.HBM)
            for x in (
                own,
                taps,
                dft_table(fine, lane_groups),
                delays,
                station_sub[None],
                beam_sub[None],
            )
        )
    )
    return out.reshape(per_device, 2, n_chan * chans, n_core * frames, fine).astype(jnp.float32)


def solution(mesh):
    placed = (P(None, "stn", "chan", "beam"), P(), P(None, "stn"), P("stn"), P())
    return jax.shard_map(
        body,
        mesh=mesh,
        in_specs=placed,
        out_specs=P(("stn", "chan", "beam"), None, None, None, None),
        check_vma=False,
    )
```

```python
import functools
import math

import jax
import jax.numpy as jnp
import numpy as np
from jax import lax
from jax.experimental import pallas as pl
from jax.experimental.pallas import tpu as pltpu
from jax.sharding import PartitionSpec as P

SUBARRAYS = 4
LANES = 128
QUAD = 4
WIDE = 2
UNROLL_FB = True
LEAD = 2
LATE = 1
PIECES = 2
PHASES = 4
VMEM_LIMIT = 32 * 2**20
MESH = pl.DeviceIdType.MESH


def dft_table(fine, lane_groups):
    index = np.arange(fine)
    angle = 2.0 * np.pi * (index[:, None] * index[None, :] % fine) / fine
    scale = 1.0 / math.sqrt(fine)
    cosine = np.cos(angle) * scale
    sine = np.sin(angle) * scale
    whole = np.stack([np.concatenate([cosine, sine]), np.concatenate([-sine, cosine])])
    halves = []
    for half in range(fine // LANES):
        k = half * LANES + (np.arange(LANES).reshape(-1, lane_groups).T).reshape(-1)
        halves.append(np.concatenate([whole[0][:, k].T, whole[1][:, k].T]))
    return jnp.asarray(np.stack(halves), jnp.bfloat16)


def unit_turn(turn):
    quarter = (turn + 8192) >> 14
    t = (turn - (quarter << 14)).astype(jnp.float32) * (2.0 * math.pi / 65536.0)
    u = t * t
    sine = t * (1.0 + u * (-1.0 / 6 + u * (1.0 / 120 + u * (-1.0 / 5040))))
    cosine = 1.0 + u * (-0.5 + u * (1.0 / 24 + u * (-1.0 / 720 + u * (1.0 / 40320))))
    odd = (quarter & 1) == 1
    c = jnp.where(odd, sine, cosine)
    s = jnp.where(odd, cosine, sine)
    c = jnp.where(((quarter + 1) & 2) == 2, -c, c)
    s = jnp.where((quarter & 2) == 2, -s, s)
    return c, s


def swap_index_with_lanes(tiles, block):
    lane = lax.broadcasted_iota(jnp.int32, tiles[0].shape, 1)
    bit = 1
    while bit < len(tiles):
        upper = (lane & (bit * block)) != 0
        swapped = list(tiles)
        for i in range(len(tiles)):
            if not i & bit:
                low, high = tiles[i], tiles[i | bit]
                swapped[i] = jnp.where(upper, pltpu.roll(high, bit * block, 1), low)
                swapped[i | bit] = jnp.where(upper, high, pltpu.roll(low, LANES - bit * block, 1))
        tiles = swapped
        bit *= 2
    return tiles


def kernel(
    sizes,
    amplitude,
    own_ref,
    taps_hbm,
    table_hbm,
    delays_hbm,
    station_hbm,
    beam_hbm,
    out_ref,
    volts,
    taps_ref,
    table,
    delay_in,
    station_in,
    beam_in,
    wide_taps,
    wide_int,
    member,
    steps,
    state,
    filtered,
    spectra,
    total_ref,
    turned,
    part,
    final,
    own_sem,
    small_sem,
    halo_send,
    halo_recv,
    send,
    recv,
    far_send,
    far_recv,
    *exchanged,
):
    n_chan, n_core, bits = sizes
    received, sent = exchanged[:bits], exchanged[bits:]
    chans, stations, samples = own_ref.shape[1:]
    tap_count, fine = taps_ref.shape
    beams = delay_in.shape[0]
    frames = final.shape[-2]
    halves = fine // LANES
    chunks = chans * halves
    lane_groups = LANES // stations
    hop = 3 * fine // 4
    groups = frames // PHASES
    quads = LANES // lane_groups // QUAD
    n_stn = 2**bits
    rows = 2 * beams // n_stn
    per = beams // n_stn
    width = frames * lane_groups
    tiles = QUAD * width // LANES
    halo = volts.shape[3] - samples
    stn, chan, core = (lax.axis_index(name) for name in ("stn", "chan", "beam"))

    def fetch(c):
        return pltpu.make_async_copy(
            own_ref.at[:, c], volts.at[:, c, :, pl.ds(0, samples)], own_sem.at[c]
        )

    small = [
        pltpu.make_async_copy(source, target, small_sem.at[i])
        for i, (source, target) in enumerate(
            (
                (taps_hbm, taps_ref),
                (delays_hbm, delay_in),
                (station_hbm, station_in),
                (beam_hbm, beam_in),
                (table_hbm, table),
            )
        )
    ]
    own_bit = [(stn // 2 ** (bits - 1 - dim)) % 2 for dim in range(bits)]
    orders = (tuple(range(bits - 1, -1, -1)), tuple(range(bits)))

    def partner(dim):
        return (stn + (1 - 2 * own_bit[dim]) * 2 ** (bits - 1 - dim), chan, core)

    def far(dz, dc):
        return ((chan + dz) % n_chan, (core + dc) % n_core)

    offsets = [(dz, dc) for dc in range(n_core) for dz in range(n_chan)]
    barrier = pltpu.get_barrier_semaphore()
    peers = [partner(dim) for dim in range(bits)] + [(stn, *far(dz, dc)) for dz, dc in offsets[1:]]
    for peer in peers:
        pl.semaphore_signal(barrier, inc=1, device_id=peer, device_id_type=MESH)
    small[0].start()
    fetch(0).start()
    for copy in small[1:]:
        copy.start()
    for c in range(1, chans):
        fetch(c).start()

    def halo_copy(c, ri):
        return pltpu.make_async_remote_copy(
            src_ref=own_ref.at[ri, c, :, pl.ds(0, halo)],
            dst_ref=volts.at[ri, c, :, pl.ds(samples, halo)],
            send_sem=halo_send.at[c, ri],
            recv_sem=halo_recv.at[c, ri],
            device_id=(stn, chan, core - 1),
            device_id_type=MESH,
        )

    def send_halo(c):
        for ri in range(2):
            halo_copy(c, ri).start()

    small[0].wait()

    pl.semaphore_wait(barrier, len(peers))

    @pl.when(core > 0)
    def _():
        send_halo(0)

    @pl.when(core == n_core - 1)
    def _():
        volts[:, :, :, samples:] = jnp.zeros((2, chans, stations, halo), volts.dtype)

    for phase in range(PHASES):
        shift = hop * phase % fine
        rolled = taps_ref[...]
        if shift:
            rolled = pltpu.roll(rolled, shift, 1)
        column = lax.broadcasted_iota(jnp.int32, (1, fine), 1)
        for u in range(tap_count + 1):
            late = rolled[u : u + 1] if u < tap_count else jnp.zeros((1, fine), jnp.float32)
            early = rolled[u - 1 : u] if u > 0 else jnp.zeros((1, fine), jnp.float32)
            row = jnp.where(column >= shift, late, early)
            wide_taps[phase, u] = jnp.broadcast_to(row, (16, fine)).astype(jnp.bfloat16)

    for copy in small[1:]:
        copy.wait()

    def widened(value, count):
        wide_int[...] = jnp.zeros(wide_int.shape, jnp.int32)
        wide_int[0:count, 0:stations] = value
        full = wide_int[...]
        step = stations
        while step < LANES:
            full = full + pltpu.roll(full, step, 1)
            step *= 2
        return full[0:count]

    group_of_lane = lax.broadcasted_iota(jnp.int32, (1, LANES), 1) // stations
    station_row = widened(station_in[...], 1).astype(jnp.float32)
    square = (beams, beams)
    diagonal = lax.broadcasted_iota(jnp.int32, square, 0) == lax.broadcasted_iota(jnp.int32, square, 1)
    beam_row = jnp.broadcast_to(beam_in[...].astype(jnp.float32), square)
    beam_column = jnp.sum(jnp.where(diagonal, beam_row, 0.0), axis=1, keepdims=True)
    member[...] = jnp.where(beam_column == station_row, amplitude, 0.0)
    delay = widened(delay_in[...], beams)
    wide_int[...] = delay
    for i, stride in enumerate((lane_groups, QUAD * lane_groups)):
        c, s = unit_turn((delay * stride) & 65535)
        steps[i, 0] = c
        steps[i, 1] = -s

    def filter_part(c, ri, local):
        limit = samples // fine
        for half in range(halves):
            for phase in range(PHASES):
                shift = hop * phase % fine
                block0 = hop * phase // fine
                first = 0 if shift < (half + 1) * LANES else 1
                last = tap_count - 1 if shift <= half * LANES else tap_count
                lanes = slice(half * LANES, (half + 1) * LANES)
                taps = {u: wide_taps[phase, u, :, lanes][None] for u in range(first, last + 1)}
                columns = pl.ds(pl.multiple_of(ri * fine + half * LANES, LANES), LANES)
                blocks = [
                    block
                    for block in range(block0 + first, block0 + last + 1 + 3 * (groups - 1))
                    if (block < limit) == local
                ]
                for_group = [
                    [block for block in blocks if first <= block - block0 - 3 * g <= last]
                    for g in range(groups)
                ]
                sums = [[None, None] for _ in range(groups)]
                for g in range(groups):
                    f = PHASES * g + phase
                    if not local and for_group[g] and block0 + 3 * g + first < limit:
                        begun = filtered[c % 2, f * stations : (f + 1) * stations, columns]
                        sums[g][0] = begun.reshape(stations // 16, 16, LANES)
                for block in blocks:
                    at = block * fine + half * LANES
                    value = volts[ri, c, :, at : at + LANES].reshape(stations // 16, 16, LANES)
                    for g in range(groups):
                        if block in for_group[g]:
                            u = block - block0 - 3 * g
                            term = taps[u] * value
                            so_far = sums[g][u % 2]
                            sums[g][u % 2] = term if so_far is None else so_far + term
                for g in range(groups):
                    if for_group[g]:
                        f = PHASES * g + phase
                        parts = [part_sum for part_sum in sums[g] if part_sum is not None]
                        filtered[c % 2, f * stations : (f + 1) * stations, columns] = sum(
                            parts[1:], parts[0]
                        ).reshape(stations, LANES)

    def filter_channel(c, first_part, last_part):
        @pl.loop(first_part, last_part)
        def _(ri):
            @pl.when(ri == 0)
            def _():
                fetch(c).wait()

            filter_part(c, ri, True)

        @pl.loop(first_part, last_part)
        def _(ri):
            @pl.when(core < n_core - 1)
            def _():
                halo_copy(c, ri).wait_recv()

            @pl.when((core > 0) & (c + 1 < chans))
            def _():
                halo_copy(c + 1, ri).start()

            filter_part(c, ri, False)

    def transform(chunk):
        half = chunk % halves
        slot = chunk // halves % 2
        count = LANES // lane_groups

        def one(fb):
            rhs = filtered[slot, pl.ds(pl.multiple_of(fb * LANES, LANES), WIDE * LANES), :]
            result = lax.dot_general(
                table[half], rhs, (((1,), (1,)), ((), ())), preferred_element_type=jnp.float32
            )
            for ri in range(2):
                for sub in range(WIDE):
                    pieces = [
                        result[
                            (ri * lane_groups + j) * count : (ri * lane_groups + j + 1) * count,
                            sub * LANES : (sub + 1) * LANES,
                        ]
                        for j in range(lane_groups)
                    ]
                    for j, piece in enumerate(swap_index_with_lanes(pieces, stations)):
                        at = pl.multiple_of(((fb + sub) * lane_groups + j) * count, count)
                        spectra[half, ri, pl.ds(at, count), :] = piece

        if UNROLL_FB:
            for fb in range(0, frames // lane_groups, WIDE):
                one(fb)
        else:
            @pl.loop(0, frames // lane_groups // WIDE)
            def _(fb):
                one(fb * WIDE)

    def form_beams(chunk, c, half):
        count = LANES // lane_groups
        frequency = (chan * chans + c) * fine + half * LANES + group_of_lane
        cosine, sine = unit_turn((wide_int[...] * frequency) & 65535)
        state[0] = cosine * member[...]
        state[1] = -sine * member[...]
        lane = lax.broadcasted_iota(jnp.int32, (frames, LANES), 1) // stations
        out_lane = lax.broadcasted_iota(jnp.int32, (2 * beams, LANES), 1)

        def times(a, i):
            e_re, e_im = steps[i, 0], steps[i, 1]
            return (a[0] * e_re - a[1] * e_im, a[0] * e_im + a[1] * e_re)

        def stacked(top, bottom):
            both = [v.reshape(n_stn, per, LANES) for v in (top, bottom)]
            return jnp.stack(both, axis=1).reshape(2 * beams, LANES)

        def one(quad):
            first = weight = (state[0], state[1])
            outs = []
            for q in range(QUAD):
                if q:
                    weight = times(weight, 0)
                w_re, w_im = weight
                lhs = jnp.concatenate([stacked(w_re, w_im), stacked(-w_im, w_re)], axis=1)
                at = quad * QUAD + q
                x = [spectra.at[half, ri][pl.ds(at, frames, stride=count), :] for ri in range(2)]
                blocks = [
                    jnp.concatenate([jnp.where(lane == j, v, 0.0) for v in x], axis=1)
                    for j in range(lane_groups)
                ]
                if width < LANES:
                    blocks.append(jnp.zeros((LANES - width, 2 * LANES), jnp.float32))
                turn = q * width % LANES
                if turn:
                    blocks = [jnp.concatenate(blocks, axis=0)]
                    blocks = [blocks[0][LANES - turn :], blocks[0][: LANES - turn]]
                rhs = jnp.concatenate(blocks, axis=0)
                result = lax.dot_general(
                    lhs.astype(jnp.bfloat16),
                    rhs.astype(jnp.bfloat16),
                    (((1,), (1,)), ((), ())),
                    preferred_element_type=jnp.float32,
                )
                outs.append(result)
            following = times(first, 1)
            state[0] = following[0]
            state[1] = following[1]
            for t in range(tiles):
                value = None
                for q in range(QUAD):
                    start = q * width - t * LANES
                    if -width < start < LANES:
                        value = outs[q] if value is None else jnp.where(out_lane >= start, outs[q], value)
                value = value.astype(jnp.bfloat16)
                for d in range(n_stn):
                    place = [(d >> (bits - 1 - dim)) & 1 for dim in range(bits)]
                    part[(chunk, quad // (quads // PIECES), *place, quad % (quads // PIECES), t)] = value[
                        d * rows : (d + 1) * rows
                    ]

        for quad in range(quads):
            one(quad)
            if (quad + 1) % (quads // PIECES) == 0:
                hop_copy(chunk, quad // (quads // PIECES), 0).start()

    def region(order, stage, last):
        index = [slice(None)] * bits
        for dim in orders[order % 2][:stage]:
            index[dim] = own_bit[dim]
        if stage < bits:
            index[orders[order % 2][stage]] = last(orders[order % 2][stage])
        return index

    def other(dim):
        return 1 - own_bit[dim]

    def with_received(chunk, order, stage, index):
        value = part[(chunk, order, *index)].astype(jnp.float32)
        for earlier in range(stage):
            kept = [dim for dim in range(bits) if dim not in orders[order % 2][: earlier + 1]]
            piece = received[earlier][(chunk, order, *(index[dim] for dim in kept))]
            value = value + piece.astype(jnp.float32)
        return value

    def hop_copy(chunk, order, stage):
        if stage == 0:
            source = part.at[(chunk, order, *region(order, 0, other))]
        else:
            source = sent[stage - 1].at[chunk, order]
        return pltpu.make_async_remote_copy(
            src_ref=source,
            dst_ref=received[stage].at[chunk, order],
            send_sem=send.at[stage],
            recv_sem=recv.at[stage, chunk, order],
            device_id=partner(orders[order % 2][stage]),
            device_id_type=MESH,
        )

    def place_of(chunk):
        c = chunk // halves
        lanes = pl.ds(pl.multiple_of((chunk % halves) * LANES, LANES), LANES)
        return out_ref.at[:, :, chan * chans + c, core, :, lanes]

    def deliver(chunk, number):
        z, k = far(*offsets[number])
        return pltpu.make_async_remote_copy(
            src_ref=final.at[chunk, z, k],
            dst_ref=place_of(chunk),
            send_sem=far_send,
            recv_sem=far_recv,
            device_id=(stn, z, k),
            device_id_type=MESH,
        )

    def keep(chunk):
        return pltpu.make_async_copy(final.at[chunk, chan, core], place_of(chunk), far_recv)

    def finish(chunk):
        for order in range(PIECES):
            value = with_received(chunk, order, bits, own_bit)
            for quad in range(quads // PIECES):
                at = (order * (quads // PIECES) + quad) * rows
                for t in range(tiles):
                    total_ref[t, at : at + rows, :] = value[quad, t]
        for t in range(tiles):
            turned[t * LANES : (t + 1) * LANES, :] = total_ref[t].T
        pieces = [turned[i * frames : (i + 1) * frames, :] for i in range(rows)]
        for row, piece in enumerate(swap_index_with_lanes(pieces, 1)):
            ri, b = divmod(row, per)
            device, at = divmod(b, per // (n_chan * n_core))
            z, k = divmod(device, n_core)
            final[chunk, z, k, at, ri] = piece.astype(jnp.bfloat16)

    def step(chunk, stage):
        for order in range(PIECES):
            hop_copy(chunk, order, stage - 1).wait_recv()
            if stage < bits:
                sent[stage - 1][chunk, order] = with_received(
                    chunk, order, stage, region(order, stage, other)
                ).astype(jnp.bfloat16)
                hop_copy(chunk, order, stage).start()
        if stage == bits:
            finish(chunk)
            for number in range(1, len(offsets)):
                deliver(chunk, number).start()
            keep(chunk).start()

    @pl.loop(0, chunks + LEAD + bits)
    def _(tick):
        def during(chunk, action):
            @pl.when((chunk >= 0) & (chunk < chunks))
            def _():
                action(chunk)

        during(tick - LEAD, lambda chunk: form_beams(chunk, chunk // halves, chunk % halves))
        c = tick // halves

        @pl.when((c < chans) & (tick != 1))
        def _():
            filter_channel(c, tick % 2, jnp.where(tick == 0, 2, tick % 2 + 1))

        @pl.when((tick >= 1) & (tick <= chunks))
        def _():
            transform(tick - 1)

        for stage in range(1, bits):
            during(tick - LEAD - stage, lambda chunk, stage=stage: step(chunk, stage))

        def summed(tick):
            caught_up = jnp.where(tick >= LEAD + chunks - 1, LATE, 0)
            return jnp.clip(tick - LEAD - bits - LATE + 1 + caught_up, 0, chunks)

        @pl.loop(summed(tick - 1), summed(tick))
        def _(chunk):
            step(chunk, bits)


    @pl.when(core > 0)
    def _():
        for c in range(chans):
            for ri in range(2):
                halo_copy(c, ri).wait_send()

    def all_of(ref, send_sem, recv_sem):
        return pltpu.make_async_remote_copy(
            src_ref=ref,
            dst_ref=ref,
            send_sem=send_sem,
            recv_sem=recv_sem,
            device_id=partner(0),
            device_id_type=MESH,
        )

    for stage in range(bits):
        all_of(received[stage], send.at[stage], far_recv).wait_send()
    if n_chan > 1:
        all_of(final.at[:, 0 : n_chan - 1], far_send, far_recv).wait_send()
    if n_core > 1:
        all_of(final.at[:, 0, 0 : n_core - 1], far_send, far_recv).wait_send()
    all_of(out_ref, far_send, far_recv).wait_recv()


def body(volts, taps, delays, station_sub, beam_sub):
    own = jnp.transpose(volts, (0, 2, 1, 3))
    chans, stations, samples = own.shape[1:]
    tap_count, fine = taps.shape
    beams = delays.shape[0]
    n_stn, n_chan, n_core = (lax.axis_size(name) for name in ("stn", "chan", "beam"))
    bits = n_stn.bit_length() - 1
    hop = 3 * fine // 4
    frames = samples // hop
    per = beams // n_stn
    per_device = per // (n_chan * n_core)
    halves = fine // LANES
    chunks = chans * halves
    lane_groups = LANES // stations
    quads = LANES // lane_groups // QUAD
    tiles = QUAD * frames * lane_groups // LANES
    rows = 2 * per
    assert halves == 2 and n_stn == 2**bits and rows == QUAD * lane_groups and quads * rows == LANES
    assert QUAD * frames * lane_groups == tiles * LANES and frames * lane_groups <= LANES
    blocks = hop * (PHASES - 1) // fine + tap_count + 1 + 3 * (frames // PHASES - 1)
    amplitude = 1.0 / math.sqrt(stations * n_stn // SUBARRAYS)
    block = (quads // PIECES, tiles, rows, LANES)
    pieces = [
        pltpu.VMEM((chunks, PIECES) + (2,) * (bits - 1 - t) + block, jnp.bfloat16) for t in range(bits)
    ]
    hbm = pl.BlockSpec(memory_space=pltpu.HBM)
    dma = pltpu.SemaphoreType.DMA
    out = pl.pallas_call(
        functools.partial(kernel, (n_chan, n_core, bits), amplitude),
        out_shape=jax.ShapeDtypeStruct(
            (per_device, 2, n_chan * chans, n_core, frames, fine), jnp.bfloat16
        ),
        in_specs=[hbm] * 6,
        out_specs=pl.BlockSpec(memory_space=pl.ANY),
        scratch_shapes=[
            pltpu.VMEM((2, chans, stations, blocks * fine), jnp.bfloat16),
            pltpu.VMEM((tap_count, fine), jnp.float32),
            pltpu.VMEM((halves, 2 * LANES, 2 * fine), jnp.bfloat16),
            pltpu.VMEM((beams, stations), jnp.int32),
            pltpu.VMEM((1, stations), jnp.int32),
            pltpu.VMEM((1, beams), jnp.int32),
            pltpu.VMEM((PHASES, tap_count + 1, 16, fine), jnp.bfloat16),
            pltpu.VMEM((beams, LANES), jnp.int32),
            pltpu.VMEM((beams, LANES), jnp.float32),
            pltpu.VMEM((2, 2, beams, LANES), jnp.float32),
            pltpu.VMEM((2, beams, LANES), jnp.float32),
            pltpu.VMEM((2, frames * stations, 2 * fine), jnp.bfloat16),
            pltpu.VMEM((halves, 2, frames * LANES // lane_groups, LANES), jnp.float32),
            pltpu.VMEM((tiles, LANES, LANES), jnp.float32),
            pltpu.VMEM((tiles * LANES, LANES), jnp.float32),
            pltpu.VMEM((chunks, PIECES) + (2,) * bits + block, jnp.bfloat16),
            pltpu.VMEM((chunks, n_chan, n_core, per_device, 2, frames, LANES), jnp.bfloat16),
            dma((chans,)),
            dma((5,)),
            dma((chans, 2)),
            dma((chans, 2)),
            dma((bits,)),
            dma((bits, chunks, PIECES)),
            dma,
            dma,
            *pieces,
            *pieces[1:],
        ],
        compiler_params=pltpu.CompilerParams(
            collective_id=0, has_side_effects=True, vmem_limit_bytes=VMEM_LIMIT
        ),
        name="channelize_and_beamform",
    )(
        *(
            pltpu.with_memory_space_constraint(x, pltpu.HBM)
            for x in (
                own,
                taps,
                dft_table(fine, lane_groups),
                delays,
                station_sub[None],
                beam_sub[None],
            )
        )
    )
    return out.reshape(per_device, 2, n_chan * chans, n_core * frames, fine).astype(jnp.float32)


def solution(mesh):
    placed = (P(None, "stn", "chan", "beam"), P(), P(None, "stn"), P("stn"), P())
    return jax.shard_map(
        body,
        mesh=mesh,
        in_specs=placed,
        out_specs=P(("stn", "chan", "beam"), None, None, None, None),
        check_vma=False,
    )
```
